128 devices in a mesh: req: 32 (over y, z, core), tp: 4 (over x).
Axes of the slice: x: 4, y: 4, z: 4, core: 2. Of those that a mesh axis runs over, the one named last changes fastest.
Arguments:
- states: bfloat16 [64, 512, 1024], P('req', 'tp'), may hold values from -45 to 45
- lengths: int32 [64], P('req'), may hold values from 3 to 512, as said below
- w_qkv: bfloat16 [1024, 3, 1024], P(None, None, 'tp'), may hold values from -0.1875 to 0.1875
- b_qkv: float32 [3, 1024], P(None, 'tp'), may hold values from -3 to 3
- w_out: bfloat16 [1024, 1024], P('tp'), may hold values from -0.1875 to 0.1875
- b_out: float32 [1024], replicated, may hold values from -3 to 3
- ln1_gain: float32 [1024], replicated, may hold values from 0.1 to 1.9
- ln1_shift: float32 [1024], replicated, may hold values from -3 to 3
- w_up: bfloat16 [1024, 4096], P(None, 'tp'), may hold values from -0.1875 to 0.1875
- b_up: float32 [4096], P('tp'), may hold values from -3 to 3
- w_down: bfloat16 [4096, 1024], P('tp'), may hold values from -0.09375 to 0.09375
- b_down: float32 [1024], replicated, may hold values from -3 to 3
- ln2_gain: float32 [1024], replicated, may hold values from 0.1 to 1.9
- ln2_shift: float32 [1024], replicated, may hold values from -3 to 3
- index_rows: bfloat16 [524288, 1024], P(('req', 'tp')), may hold values from -0.1875 to 0.1875
- cand_ids: int32 [64, 64], P('req', 'tp'), may hold values from 0 to 524287
Outputs:
- hidden_out: bfloat16 [64, 512, 1024], P('req', 'tp')
- scores: float32 [64, 64], P('req', 'tp')
The draws below stay inside these ranges and needn't reach their ends.
Inputs may be any that keep to these rules, and one draw needn't show every extreme that they name: Valid positions are the first lengths ones of a text; in every draw some text has 512.
All inputs are finite; a program needn't handle non-finite values.
Results may differ from the reference program's by a relative error of at most 0.015.
Values may be sent and summed in bfloat16 or wider, within the bound.
A program may use at most 128 MiB of HBM per device.

```python
import jax
import jax.numpy as jnp
from jax import lax

D = 1024
HEADS = 16
HEAD_DIM = 64
FF = 4096
WINDOW = 512
SEQ = 512
CANDS = 64
TEXTS_ALL = 64
INDEX = 524288
N_TP = 4


def draw_states(key, part):
    key_base = jax.random.fold_in(key, 0)
    return jnp.clip(jax.random.normal(key_base, (TEXTS_ALL, SEQ, D), jnp.float32), -6.0, 6.0).astype(jnp.bfloat16)


def draw_lengths(key, part):
    key_len, key_pick = jax.random.split(key, 2)
    drawn = jax.random.randint(key_len, (TEXTS_ALL,), 3, SEQ + 1, dtype=jnp.int32)
    chosen = jax.random.randint(key_pick, (), 0, TEXTS_ALL, dtype=jnp.int32)
    return jnp.where(jnp.arange(TEXTS_ALL, dtype=jnp.int32) == chosen, jnp.int32(SEQ), drawn).astype(jnp.int32)


def plant(values, stream_key, low, largest):
    extent = values.shape
    index_at = [jax.random.randint(jax.random.fold_in(stream_key, axis), (), 0, extent[axis]) for axis in range(len(extent))]
    values = values.at[tuple(index_at)].set(low)
    longest = extent.index(max(extent))
    index_at[longest] = (index_at[longest] + 1) % extent[longest]
    return values.at[tuple(index_at)].set(largest)


def shard_levels(key, shape, shards, low, largest):
    def one(position, blocks):
        draws = jax.random.uniform(jax.random.fold_in(jax.random.fold_in(key, 6), position), (blocks,), jnp.float32, low / len(shards), largest / len(shards))
        return jnp.repeat(jnp.exp(draws), shape[position] // blocks).reshape((-1,) + (1,) * (len(shape) - position - 1))

    level = one(*shards[0])
    for cut in shards[1:]:
        level = level * one(*cut)
    return level


def noise(rng, extent, scale, reach, cuts=(), kind=jnp.bfloat16):
    result = scale * jax.random.normal(rng, extent, jnp.float32)
    if cuts:
        result = result * shard_levels(rng, extent, cuts, -0.22, 0.18)
    return jnp.clip(result, -reach, reach).astype(kind)


def setup_inputs(seed: int = 0) -> dict:
    keys = jax.random.split(jax.random.key(seed), 17)
    states = draw_states(jax.random.fold_in(keys[16], 71), 0)
    lengths = draw_lengths(jax.random.fold_in(keys[16], 71), 0)
    w_qkv = noise(keys[2], (D, 3, D), D ** -0.5, 0.1875, ((2, 4),))
    b_qkv = noise(keys[3], (3, D), 0.5, 3.0, ((1, 4),), jnp.float32)
    w_out = noise(keys[4], (D, D), D ** -0.5, 0.1875, ((0, 4),))
    b_out = noise(keys[5], (D,), 0.5, 3.0, (), jnp.float32)
    ln1_gain = jnp.clip(1.0 + 0.18 * jax.random.normal(keys[6], (D,), jnp.float32), 0.1, 1.9)
    ln1_shift = noise(keys[7], (D,), 0.5, 3.0, (), jnp.float32)
    w_up = noise(keys[8], (D, FF), D ** -0.5, 0.1875, ((1, 4),))
    b_up = noise(keys[9], (FF,), 0.5, 3.0, ((0, 4),), jnp.float32)
    w_down = noise(keys[10], (FF, D), FF ** -0.5, 0.09375, ((0, 4),))
    b_down = noise(keys[11], (D,), 0.5, 3.0, (), jnp.float32)
    ln2_gain = jnp.clip(1.0 + 0.18 * jax.random.normal(keys[12], (D,), jnp.float32), 0.1, 1.9)
    ln2_shift = noise(keys[13], (D,), 0.5, 3.0, (), jnp.float32)
    index_rows = noise(keys[14], (INDEX, D), D ** -0.5, 0.1875, ((0, 128),))
    cand_ids = plant(jax.random.randint(keys[15], (TEXTS_ALL, CANDS), 0, INDEX), jax.random.fold_in(keys[15], 1), 0, INDEX - 1).astype(jnp.int32)
    return {"states": states, "lengths": lengths, "w_qkv": w_qkv, "b_qkv": b_qkv, "w_out": w_out, "b_out": b_out, "ln1_gain": ln1_gain, "ln1_shift": ln1_shift, "w_up": w_up, "b_up": b_up, "w_down": w_down, "b_down": b_down, "ln2_gain": ln2_gain, "ln2_shift": ln2_shift, "index_rows": index_rows, "cand_ids": cand_ids}


layer_eps = 1e-05
norm_eps = 1e-06

def layer_norm(values, gain, shift):
    centre = values - lax.optimization_barrier(jnp.mean(values, axis=-1, keepdims=True))
    spread = lax.optimization_barrier(jnp.mean(centre * centre, axis=-1, keepdims=True))
    return centre * lax.rsqrt(spread + layer_eps) * gain + shift

def window_attention(queries_h, keys_h, values_h, length):
    seq_len = queries_h.shape[0]
    half_window = WINDOW // 2
    padding = ((half_window, half_window), (0, 0), (0, 0))
    keys_padded = jnp.pad(keys_h, padding)
    values_padded = jnp.pad(values_h, padding)
    scale_factor = HEAD_DIM ** (-0.5)

    def one_block(block_idx):
        blk_start = block_idx * WINDOW
        query_blk = lax.dynamic_slice_in_dim(queries_h, blk_start, WINDOW, 0)
        key_blk = lax.dynamic_slice_in_dim(keys_padded, blk_start, 2 * WINDOW, 0)
        value_blk = lax.dynamic_slice_in_dim(values_padded, blk_start, 2 * WINDOW, 0)
        query_pos = blk_start + jnp.arange(WINDOW, dtype=jnp.int32)
        key_pos = blk_start - half_window + jnp.arange(2 * WINDOW, dtype=jnp.int32)
        keep_mask = (jnp.abs(query_pos[:, None] - key_pos[None, :]) <= half_window) & (key_pos[None, :] >= 0) & (key_pos[None, :] < length)
        logits = jnp.einsum('qhe,khe->hqk', query_blk.astype(jnp.float32), key_blk.astype(jnp.float32)) * scale_factor
        logits = jnp.where(keep_mask[None], logits, jnp.float32(-1e+30))
        top_val = lax.optimization_barrier(jnp.max(logits, axis=-1, keepdims=True))
        expo = jnp.exp(logits - top_val)
        attn_weights = (expo / lax.optimization_barrier(jnp.sum(expo, axis=-1, keepdims=True))).astype(jnp.bfloat16)
        context = jnp.einsum('hqk,khe->qhe', attn_weights.astype(jnp.float32), value_blk.astype(jnp.float32))
        context = jnp.where((query_pos < length)[:, None, None], context, jnp.float32(0.0))
        return context.astype(jnp.bfloat16)
    blocks = lax.map(one_block, jnp.arange(seq_len // WINDOW, dtype=jnp.int32))
    return blocks.reshape(seq_len, HEADS * HEAD_DIM)

def group_sum(left, right, groups):
    seq_len = left.shape[0]
    inner = left.shape[1] // groups
    partial_value = jnp.einsum('sgk,gkd->gsd', left.reshape(seq_len, groups, inner).astype(jnp.float32), right.reshape(groups, inner, right.shape[1]).astype(jnp.float32))
    rounded = lax.optimization_barrier(partial_value.astype(jnp.bfloat16))
    return lax.optimization_barrier(jnp.sum(rounded.astype(jnp.float32), axis=0))

def reference(states, lengths, w_qkv, b_qkv, w_out, b_out, ln1_gain, ln1_shift, w_up, b_up, w_down, b_down, ln2_gain, ln2_shift, index_rows, cand_ids):

    def text_layer(pair):
        text_states, length = pair
        projected = jnp.einsum('sd,dce->sce', text_states.astype(jnp.float32), w_qkv.astype(jnp.float32)) + b_qkv
        projected = projected.astype(jnp.bfloat16)
        seq_len = text_states.shape[0]
        queries_h = projected[:, 0].reshape(seq_len, HEADS, HEAD_DIM)
        keys_h = projected[:, 1].reshape(seq_len, HEADS, HEAD_DIM)
        values_h = projected[:, 2].reshape(seq_len, HEADS, HEAD_DIM)
        context = window_attention(queries_h, keys_h, values_h, length)
        attn_sum = group_sum(context, w_out, N_TP)
        normed = layer_norm(text_states.astype(jnp.float32) + attn_sum + b_out, ln1_gain, ln1_shift).astype(jnp.bfloat16)
        up_act = jax.nn.gelu(jnp.dot(normed, w_up, preferred_element_type=jnp.float32) + b_up, approximate=False).astype(jnp.bfloat16)
        down_sum = group_sum(up_act, w_down, N_TP)
        return layer_norm(normed.astype(jnp.float32) + down_sum + b_down, ln2_gain, ln2_shift).astype(jnp.bfloat16)
    hidden_out = lax.map(text_layer, (states, lengths))
    is_valid = jnp.arange(SEQ, dtype=jnp.int32)[None, :] < lengths[:, None]
    pooled = lax.optimization_barrier(jnp.sum(jnp.where(is_valid[:, :, None], hidden_out.astype(jnp.float32), jnp.float32(0.0)), axis=1)) / lengths.astype(jnp.float32)[:, None]
    query_vec = (pooled * lax.rsqrt(lax.optimization_barrier(jnp.mean(pooled * pooled, axis=-1, keepdims=True)) + norm_eps)).astype(jnp.bfloat16)
    cand_rows = jnp.take(index_rows, cand_ids, axis=0)
    scores = jnp.einsum('td,tcd->tc', query_vec.astype(jnp.float32), cand_rows.astype(jnp.float32))
    return (hidden_out, scores)
```

```python
import jax
import jax.numpy as jnp
from jax import lax
from jax.sharding import PartitionSpec as P

HEAD_DIM = 64
WINDOW = 512


layer_eps = 1e-05
norm_eps = 1e-06


def layer_norm(values, gain, shift):
    centre = values - jnp.mean(values, axis=-1, keepdims=True)
    spread = jnp.mean(centre * centre, axis=-1, keepdims=True)
    return centre * lax.rsqrt(spread + layer_eps) * gain + shift


def window_attention(queries_h, keys_h, values_h, lengths):
    seq_len = queries_h.shape[1]
    half_window = WINDOW // 2
    scale_factor = HEAD_DIM ** (-0.5)
    pos = jnp.arange(seq_len, dtype=jnp.int32)
    near = jnp.abs(pos[:, None] - pos[None, :]) <= half_window
    keep_mask = near[None] & (pos[None, None, :] < lengths[:, None, None])
    logits = (
        jnp.einsum("tqhe,tkhe->thqk", queries_h, keys_h, preferred_element_type=jnp.float32)
        * scale_factor
    )
    logits = jnp.where(keep_mask[:, None], logits, jnp.float32(-1e30))
    top_val = jnp.max(logits, axis=-1, keepdims=True)
    expo = jnp.exp(logits - top_val)
    attn_weights = (expo / jnp.sum(expo, axis=-1, keepdims=True)).astype(jnp.bfloat16)
    context = jnp.einsum(
        "thqk,tkhe->tqhe", attn_weights, values_h, preferred_element_type=jnp.float32
    )
    context = jnp.where(
        (pos[None, :] < lengths[:, None])[:, :, None, None], context, jnp.float32(0.0)
    )
    return context.astype(jnp.bfloat16).reshape(
        queries_h.shape[0], seq_len, queries_h.shape[2] * HEAD_DIM
    )


def per_device(
    states,
    lengths,
    w_qkv,
    b_qkv,
    w_out,
    b_out,
    ln1_gain,
    ln1_shift,
    w_up,
    b_up,
    w_down,
    b_down,
    ln2_gain,
    ln2_shift,
    index_rows,
    cand_ids,
):
    tp_count = lax.axis_size("tp")
    tp_rank = lax.axis_index("tp")
    req_count = lax.axis_size("req")
    req_rank = lax.axis_index("req")
    text_count, row_share, model_width = states.shape
    quarter = cand_ids.shape[1]
    gathered_ids = lax.all_gather(cand_ids, ("req", "tp"), axis=0, tiled=True)
    full_states = lax.all_gather(states, "tp", axis=1, tiled=True)
    seq_len = full_states.shape[1]
    local_width = w_qkv.shape[2]
    heads_here = local_width // HEAD_DIM
    projected = (
        jnp.einsum("tsd,dce->tsce", full_states, w_qkv, preferred_element_type=jnp.float32) + b_qkv
    ).astype(jnp.bfloat16)
    queries_h = projected[:, :, 0].reshape(text_count, seq_len, heads_here, HEAD_DIM)
    keys_h = projected[:, :, 1].reshape(text_count, seq_len, heads_here, HEAD_DIM)
    values_h = projected[:, :, 2].reshape(text_count, seq_len, heads_here, HEAD_DIM)

    context = window_attention(queries_h, keys_h, values_h, lengths)
    partial_value = jnp.einsum("tsk,kd->tsd", context, w_out, preferred_element_type=jnp.float32)
    attn_sum = lax.psum(partial_value.astype(jnp.bfloat16), "tp").astype(jnp.float32)
    normed_full = layer_norm(
        full_states.astype(jnp.float32) + attn_sum + b_out, ln1_gain, ln1_shift
    ).astype(jnp.bfloat16)
    normed_local = lax.dynamic_slice_in_dim(normed_full, tp_rank * row_share, row_share, 1)
    up_act = jax.nn.gelu(
        jnp.einsum("tsd,df->tsf", normed_full, w_up, preferred_element_type=jnp.float32) + b_up,
        approximate=False,
    ).astype(jnp.bfloat16)
    down_part = jnp.einsum("tsf,fd->tsd", up_act, w_down, preferred_element_type=jnp.float32)
    down_sum = lax.psum_scatter(
        down_part.astype(jnp.bfloat16), "tp", scatter_dimension=1, tiled=True
    ).astype(jnp.float32)
    hidden_out = layer_norm(
        normed_local.astype(jnp.float32) + down_sum + b_down, ln2_gain, ln2_shift
    ).astype(jnp.bfloat16)
    positions = tp_rank * row_share + jnp.arange(row_share, dtype=jnp.int32)
    is_valid = positions[None, :] < lengths[:, None]
    local_pool = jnp.sum(
        jnp.where(is_valid[:, :, None], hidden_out.astype(jnp.float32), jnp.float32(0.0)), axis=1
    )
    pooled = lax.psum(local_pool, "tp") / lengths.astype(jnp.float32)[:, None]
    query_vec = (
        pooled * lax.rsqrt(jnp.mean(pooled * pooled, axis=-1, keepdims=True) + norm_eps)
    ).astype(jnp.bfloat16)
    all_queries = lax.all_gather(query_vec, "req", axis=0, tiled=True)
    all_ids = (
        gathered_ids.reshape(req_count, tp_count, text_count, quarter)
        .transpose(0, 2, 1, 3)
        .reshape(req_count * text_count, tp_count * quarter)
    )
    rows_here = index_rows.shape[0]
    first_row = (req_rank * tp_count + tp_rank) * rows_here
    local_ids = all_ids - first_row
    is_owned = (local_ids >= 0) & (local_ids < rows_here)
    safe_ids = jnp.clip(local_ids, 0, rows_here - 1)
    all_scores = jnp.einsum(
        "td,rd->tr", all_queries, index_rows, preferred_element_type=jnp.float32
    )
    picked = jnp.take_along_axis(all_scores, safe_ids, axis=1)
    owner_terms = jnp.where(is_owned, picked, jnp.float32(0.0))
    owner_terms = (
        owner_terms.reshape(req_count, text_count, tp_count, quarter)
        .transpose(0, 2, 1, 3)
        .reshape(req_count * tp_count * text_count, quarter)
    )
    scores = lax.psum_scatter(owner_terms, ("req", "tp"), scatter_dimension=0, tiled=True)
    return (hidden_out, scores)


def solution(mesh):
    placed = (
        P("req", "tp", None),
        P("req"),
        P(None, None, "tp"),
        P(None, "tp"),
        P("tp", None),
        P(),
        P(),
        P(),
        P(None, "tp"),
        P("tp"),
        P("tp", None),
        P(),
        P(),
        P(),
        P(("req", "tp"), None),
        P("req", "tp"),
    )
    return jax.shard_map(
        per_device,
        mesh=mesh,
        in_specs=placed,
        out_specs=(P("req", "tp", None), P("req", "tp")),
        check_vma=False,
    )
```

```python
import jax
import jax.numpy as jnp
from jax import lax
from jax.sharding import PartitionSpec as P

HEAD_DIM = 64
WINDOW = 512


layer_eps = 1e-05
norm_eps = 1e-06


def layer_norm(values, gain, shift):
    centre = values - jnp.mean(values, axis=-1, keepdims=True)
    spread = jnp.mean(centre * centre, axis=-1, keepdims=True)
    return centre * lax.rsqrt(spread + layer_eps) * gain + shift


def window_attention(queries_h, keys_h, values_h, lengths):
    seq_len = queries_h.shape[1]
    half_window = WINDOW // 2
    scale_factor = HEAD_DIM ** (-0.5)
    pos = jnp.arange(seq_len, dtype=jnp.int32)
    near = jnp.abs(pos[:, None] - pos[None, :]) <= half_window
    keep_mask = near[None] & (pos[None, None, :] < lengths[:, None, None])
    logits = (
        jnp.einsum("tqhe,tkhe->thqk", queries_h, keys_h, preferred_element_type=jnp.float32)
        * scale_factor
    )
    logits = jnp.where(keep_mask[:, None], logits, jnp.float32(-1e30))
    top_val = jnp.max(logits, axis=-1, keepdims=True)
    expo = jnp.exp(logits - top_val)
    attn_weights = (expo / jnp.sum(expo, axis=-1, keepdims=True)).astype(jnp.bfloat16)
    context = jnp.einsum(
        "thqk,tkhe->tqhe", attn_weights, values_h, preferred_element_type=jnp.float32
    )
    context = jnp.where(
        (pos[None, :] < lengths[:, None])[:, :, None, None], context, jnp.float32(0.0)
    )
    return context.astype(jnp.bfloat16).reshape(
        queries_h.shape[0], seq_len, queries_h.shape[2] * HEAD_DIM
    )


def per_device(
    states,
    lengths,
    w_qkv,
    b_qkv,
    w_out,
    b_out,
    ln1_gain,
    ln1_shift,
    w_up,
    b_up,
    w_down,
    b_down,
    ln2_gain,
    ln2_shift,
    index_rows,
    cand_ids,
):
    tp_count = lax.axis_size("tp")
    tp_rank = lax.axis_index("tp")
    req_count = lax.axis_size("req")
    req_rank = lax.axis_index("req")
    text_count, row_share, model_width = states.shape
    quarter = cand_ids.shape[1]
    full_states = lax.all_gather(states, "tp", axis=1, tiled=True)
    device_count = req_count * tp_count
    gathered_ids = lax.all_to_all(
        jnp.broadcast_to(cand_ids[None], (device_count,) + cand_ids.shape),
        ("req", "tp"), 0, 0, tiled=True,
    )
    full_states, gathered_ids = lax.optimization_barrier((full_states, gathered_ids))
    seq_len = full_states.shape[1]
    local_width = w_qkv.shape[2]
    heads_here = local_width // HEAD_DIM
    projected = (
        jnp.einsum("tsd,dce->tsce", full_states, w_qkv, preferred_element_type=jnp.float32) + b_qkv
    ).astype(jnp.bfloat16)
    queries_h = projected[:, :, 0].reshape(text_count, seq_len, heads_here, HEAD_DIM)
    keys_h = projected[:, :, 1].reshape(text_count, seq_len, heads_here, HEAD_DIM)
    values_h = projected[:, :, 2].reshape(text_count, seq_len, heads_here, HEAD_DIM)

    context = window_attention(queries_h, keys_h, values_h, lengths)
    partial_value = jnp.einsum("tsk,kd->tsd", context, w_out, preferred_element_type=jnp.float32)
    attn_sum = lax.psum(partial_value.astype(jnp.bfloat16), "tp").astype(jnp.float32)
    normed_full = layer_norm(
        full_states.astype(jnp.float32) + attn_sum + b_out, ln1_gain, ln1_shift
    ).astype(jnp.bfloat16)
    normed_local = lax.dynamic_slice_in_dim(normed_full, tp_rank * row_share, row_share, 1)
    up_act = jax.nn.gelu(
        jnp.einsum("tsd,df->tsf", normed_full, w_up, preferred_element_type=jnp.float32) + b_up,
        approximate=False,
    ).astype(jnp.bfloat16)
    down_part = jnp.einsum("tsf,fd->tsd", up_act, w_down, preferred_element_type=jnp.float32)
    down_sum = lax.psum_scatter(
        down_part.astype(jnp.bfloat16), "tp", scatter_dimension=1, tiled=True
    ).astype(jnp.float32)
    hidden_out = layer_norm(
        normed_local.astype(jnp.float32) + down_sum + b_down, ln2_gain, ln2_shift
    ).astype(jnp.bfloat16)
    positions = tp_rank * row_share + jnp.arange(row_share, dtype=jnp.int32)
    is_valid = positions[None, :] < lengths[:, None]
    local_pool = jnp.sum(
        jnp.where(is_valid[:, :, None], hidden_out.astype(jnp.float32), jnp.float32(0.0)), axis=1
    )
    pooled = lax.psum(local_pool, "tp") / lengths.astype(jnp.float32)[:, None]
    query_vec = (
        pooled * lax.rsqrt(jnp.mean(pooled * pooled, axis=-1, keepdims=True) + norm_eps)
    ).astype(jnp.bfloat16)
    all_queries = lax.all_to_all(
        jnp.broadcast_to(query_vec[None], (req_count,) + query_vec.shape), "req", 0, 0, tiled=True
    ).reshape(req_count * text_count, model_width)
    all_ids = (
        gathered_ids.reshape(req_count, tp_count, text_count, quarter)
        .transpose(0, 2, 1, 3)
        .reshape(req_count * text_count, tp_count * quarter)
    )
    rows_here = index_rows.shape[0]
    first_row = (req_rank * tp_count + tp_rank) * rows_here
    local_ids = all_ids - first_row
    is_owned = (local_ids >= 0) & (local_ids < rows_here)
    safe_ids = jnp.clip(local_ids, 0, rows_here - 1)
    all_scores = jnp.einsum(
        "td,rd->tr", all_queries, index_rows, preferred_element_type=jnp.float32
    )
    score_rows = jnp.take(all_scores.T, safe_ids.reshape(-1), axis=0).reshape(
        safe_ids.shape[0], safe_ids.shape[1], safe_ids.shape[0]
    )
    picked = jnp.einsum("tct->tc", score_rows)
    owner_terms = jnp.where(is_owned, picked, jnp.float32(0.0))
    owner_terms = (
        owner_terms.reshape(req_count, text_count, tp_count, quarter)
        .transpose(0, 2, 1, 3)
        .reshape(device_count, text_count, quarter)
    )
    scores = jnp.sum(lax.all_to_all(owner_terms, ("req", "tp"), 0, 0, tiled=True), axis=0)
    return (hidden_out, scores)


def solution(mesh):
    placed = (
        P("req", "tp", None),
        P("req"),
        P(None, None, "tp"),
        P(None, "tp"),
        P("tp", None),
        P(),
        P(),
        P(),
        P(None, "tp"),
        P("tp"),
        P("tp", None),
        P(),
        P(),
        P(),
        P(("req", "tp"), None),
        P("req", "tp"),
    )
    return jax.shard_map(
        per_device,
        mesh=mesh,
        in_specs=placed,
        out_specs=(P("req", "tp", None), P("req", "tp")),
        check_vma=False,
    )
```

```python
import functools
import jax
import jax.numpy as jnp
from jax import lax
from jax.experimental import pallas as pl
from jax.experimental.pallas import tpu as pltpu
from jax.sharding import PartitionSpec as P

MESH_ID = pl.DeviceIdType.MESH


def _ring_peers():
    n = lax.axis_size("tp")
    me = lax.axis_index("tp")
    rq = lax.axis_index("req")
    core = rq % 2
    right = (me + 1) % n
    left = (me + n - 1) % n
    opp = (me + 2) % n
    relay_to = (me + 1 + 2 * core) % n
    relay_from = (me + n - 1 - 2 * core) % n
    barrier = pltpu.get_barrier_semaphore()
    for peer in (left, right):
        pl.semaphore_signal(barrier, inc=1, device_id=(rq, peer), device_id_type=MESH_ID)
    pl.semaphore_wait(barrier, 2)
    return me, rq, core, right, left, opp, relay_to, relay_from


def _gather_kernel(x_ref, out_ref, send_sem, recv_sem, local_sem):
    me, rq, core, right, left, opp, relay_to, relay_from = _ring_peers()
    rows = x_ref.shape[1]

    def slot(src):
        return out_ref.at[:, pl.ds(src * rows, rows), :]

    local = pltpu.make_async_copy(x_ref, slot(me), local_sem)
    local.start()
    to_right = pltpu.make_async_remote_copy(
        x_ref, slot(me), send_sem.at[0], recv_sem.at[0], device_id=(rq, right), device_id_type=MESH_ID
    )
    to_left = pltpu.make_async_remote_copy(
        x_ref, slot(me), send_sem.at[1], recv_sem.at[1], device_id=(rq, left), device_id_type=MESH_ID
    )
    to_right.start()
    to_left.start()
    from_relay = pltpu.make_async_remote_copy(
        x_ref, slot(relay_from), send_sem.at[2], recv_sem.at[core], device_id=(rq, relay_to),
        device_id_type=MESH_ID,
    )
    from_relay.wait_recv()
    forward = pltpu.make_async_remote_copy(
        slot(relay_from), slot(relay_from), send_sem.at[2], recv_sem.at[2], device_id=(rq, relay_to),
        device_id_type=MESH_ID,
    )
    forward.start()
    other_side = (me + 1 + 2 * (1 - core)) % lax.axis_size("tp")
    from_other = pltpu.make_async_remote_copy(
        x_ref, slot(other_side), send_sem.at[0], recv_sem.at[1 - core], device_id=(rq, right),
        device_id_type=MESH_ID,
    )
    from_other.wait_recv()
    from_opp = pltpu.make_async_remote_copy(
        x_ref, slot(opp), send_sem.at[0], recv_sem.at[2], device_id=(rq, right), device_id_type=MESH_ID
    )
    from_opp.wait_recv()
    to_right.wait_send()
    to_left.wait_send()
    forward.wait_send()
    local.wait()


def ring_all_gather(x, collective_id):
    texts, rows, width = x.shape
    n = lax.axis_size("tp")
    return pl.pallas_call(
        _gather_kernel,
        out_shape=jax.ShapeDtypeStruct((texts, n * rows, width), x.dtype),
        in_specs=[pl.BlockSpec(memory_space=pl.ANY)],
        out_specs=pl.BlockSpec(memory_space=pl.ANY),
        scratch_shapes=[
            pltpu.SemaphoreType.DMA((3,)),
            pltpu.SemaphoreType.DMA((3,)),
            pltpu.SemaphoreType.DMA,
        ],
        compiler_params=pltpu.CompilerParams(collective_id=collective_id, has_side_effects=True),
    )(x)


def _scatter_kernel(p_ref, recv_ref, relay_ref, send_sem, recv_sem, relay_sem):
    me, rq, core, right, left, opp, relay_to, relay_from = _ring_peers()
    rows = recv_ref.shape[2]

    def block(dst):
        return p_ref.at[:, pl.ds(dst * rows, rows), :]

    to_right = pltpu.make_async_remote_copy(
        block(right), recv_ref.at[0], send_sem.at[0], recv_sem.at[0], device_id=(rq, right),
        device_id_type=MESH_ID,
    )
    to_left = pltpu.make_async_remote_copy(
        block(left), recv_ref.at[1], send_sem.at[1], recv_sem.at[1], device_id=(rq, left),
        device_id_type=MESH_ID,
    )
    to_relay = pltpu.make_async_remote_copy(
        block(opp), relay_ref, send_sem.at[2], relay_sem, device_id=(rq, relay_to),
        device_id_type=MESH_ID,
    )
    to_right.start()
    to_left.start()
    to_relay.start()
    to_relay.wait_recv()
    forward = pltpu.make_async_remote_copy(
        relay_ref, recv_ref.at[2], send_sem.at[3], recv_sem.at[2], device_id=(rq, relay_to),
        device_id_type=MESH_ID,
    )
    forward.start()
    to_right.wait_recv()
    to_left.wait_recv()
    forward.wait_recv()
    to_right.wait_send()
    to_left.wait_send()
    to_relay.wait_send()
    forward.wait_send()


def ring_reduce_scatter(p, collective_id):
    texts, all_rows, width = p.shape
    n = lax.axis_size("tp")
    rows = all_rows // n
    recv, _ = pl.pallas_call(
        _scatter_kernel,
        out_shape=(
            jax.ShapeDtypeStruct((n - 1, texts, rows, width), p.dtype),
            jax.ShapeDtypeStruct((texts, rows, width), p.dtype),
        ),
        in_specs=[pl.BlockSpec(memory_space=pl.ANY)],
        out_specs=(pl.BlockSpec(memory_space=pl.ANY), pl.BlockSpec(memory_space=pl.ANY)),
        scratch_shapes=[
            pltpu.SemaphoreType.DMA((4,)),
            pltpu.SemaphoreType.DMA((3,)),
            pltpu.SemaphoreType.DMA,
        ],
        compiler_params=pltpu.CompilerParams(collective_id=collective_id, has_side_effects=True),
    )(p)
    return recv


HEAD_DIM = 64
WINDOW = 512


layer_eps = 1e-05
norm_eps = 1e-06


def layer_norm(values, gain, shift):
    centre = values - jnp.mean(values, axis=-1, keepdims=True)
    spread = jnp.mean(centre * centre, axis=-1, keepdims=True)
    return centre * lax.rsqrt(spread + layer_eps) * gain + shift


def window_attention(queries_h, keys_h, values_h, lengths):
    seq_len = queries_h.shape[1]
    half_window = WINDOW // 2
    scale_factor = HEAD_DIM ** (-0.5)
    pos = jnp.arange(seq_len, dtype=jnp.int32)
    near = jnp.abs(pos[:, None] - pos[None, :]) <= half_window
    keep_mask = near[None] & (pos[None, None, :] < lengths[:, None, None])
    logits = (
        jnp.einsum("tqhe,tkhe->thqk", queries_h, keys_h, preferred_element_type=jnp.float32)
        * scale_factor
    )
    logits = jnp.where(keep_mask[:, None], logits, jnp.float32(-1e30))
    top_val = jnp.max(logits, axis=-1, keepdims=True)
    expo = jnp.exp(logits - top_val)
    attn_weights = (expo / jnp.sum(expo, axis=-1, keepdims=True)).astype(jnp.bfloat16)
    context = jnp.einsum(
        "thqk,tkhe->tqhe", attn_weights, values_h, preferred_element_type=jnp.float32
    )
    context = jnp.where(
        (pos[None, :] < lengths[:, None])[:, :, None, None], context, jnp.float32(0.0)
    )
    return context.astype(jnp.bfloat16).reshape(
        queries_h.shape[0], seq_len, queries_h.shape[2] * HEAD_DIM
    )


def per_device(
    states,
    lengths,
    w_qkv,
    b_qkv,
    w_out,
    b_out,
    ln1_gain,
    ln1_shift,
    w_up,
    b_up,
    w_down,
    b_down,
    ln2_gain,
    ln2_shift,
    index_rows,
    cand_ids,
):
    tp_count = lax.axis_size("tp")
    tp_rank = lax.axis_index("tp")
    req_count = lax.axis_size("req")
    req_rank = lax.axis_index("req")
    text_count, row_share, model_width = states.shape
    quarter = cand_ids.shape[1]
    full_states = ring_all_gather(states, 0)
    device_count = req_count * tp_count
    gathered_ids = lax.all_to_all(
        jnp.broadcast_to(cand_ids[None], (device_count,) + cand_ids.shape),
        ("req", "tp"), 0, 0, tiled=True,
    )
    full_states, gathered_ids = lax.optimization_barrier((full_states, gathered_ids))
    seq_len = full_states.shape[1]
    local_width = w_qkv.shape[2]
    heads_here = local_width // HEAD_DIM
    projected = (
        jnp.einsum("tsd,dce->tsce", full_states, w_qkv, preferred_element_type=jnp.float32) + b_qkv
    ).astype(jnp.bfloat16)
    queries_h = projected[:, :, 0].reshape(text_count, seq_len, heads_here, HEAD_DIM)
    keys_h = projected[:, :, 1].reshape(text_count, seq_len, heads_here, HEAD_DIM)
    values_h = projected[:, :, 2].reshape(text_count, seq_len, heads_here, HEAD_DIM)

    context = window_attention(queries_h, keys_h, values_h, lengths)
    partial_value = jnp.einsum("tsk,kd->tsd", context, w_out, preferred_element_type=jnp.float32)
    partial_value = partial_value.astype(jnp.bfloat16)
    attn_recv = ring_reduce_scatter(partial_value, 1)
    attn_sum = lax.dynamic_slice_in_dim(partial_value, tp_rank * row_share, row_share, 1).astype(
        jnp.float32
    ) + jnp.sum(attn_recv.astype(jnp.float32), axis=0)
    normed_local = layer_norm(
        states.astype(jnp.float32) + attn_sum + b_out, ln1_gain, ln1_shift
    ).astype(jnp.bfloat16)
    normed_full = ring_all_gather(normed_local, 2)
    up_act = jax.nn.gelu(
        jnp.einsum("tsd,df->tsf", normed_full, w_up, preferred_element_type=jnp.float32) + b_up,
        approximate=False,
    ).astype(jnp.bfloat16)
    down_part = jnp.einsum(
        "tsf,fd->tsd", up_act, w_down, preferred_element_type=jnp.float32
    ).astype(jnp.bfloat16)
    down_recv = ring_reduce_scatter(down_part, 3)
    down_sum = lax.dynamic_slice_in_dim(down_part, tp_rank * row_share, row_share, 1).astype(
        jnp.float32
    ) + jnp.sum(down_recv.astype(jnp.float32), axis=0)
    hidden_out = layer_norm(
        normed_local.astype(jnp.float32) + down_sum + b_down, ln2_gain, ln2_shift
    ).astype(jnp.bfloat16)
    positions = tp_rank * row_share + jnp.arange(row_share, dtype=jnp.int32)
    is_valid = positions[None, :] < lengths[:, None]
    local_pool = jnp.sum(
        jnp.where(is_valid[:, :, None], hidden_out.astype(jnp.float32), jnp.float32(0.0)), axis=1
    )
    pooled = lax.psum(local_pool, "tp") / lengths.astype(jnp.float32)[:, None]
    query_vec = (
        pooled * lax.rsqrt(jnp.mean(pooled * pooled, axis=-1, keepdims=True) + norm_eps)
    ).astype(jnp.bfloat16)
    all_queries = lax.all_to_all(
        jnp.broadcast_to(query_vec[None], (req_count,) + query_vec.shape), "req", 0, 0, tiled=True
    ).reshape(req_count * text_count, model_width)
    all_ids = (
        gathered_ids.reshape(req_count, tp_count, text_count, quarter)
        .transpose(0, 2, 1, 3)
        .reshape(req_count * text_count, tp_count * quarter)
    )
    rows_here = index_rows.shape[0]
    first_row = (req_rank * tp_count + tp_rank) * rows_here
    local_ids = all_ids - first_row
    is_owned = (local_ids >= 0) & (local_ids < rows_here)
    safe_ids = jnp.clip(local_ids, 0, rows_here - 1)
    all_scores = jnp.einsum(
        "td,rd->tr", all_queries, index_rows, preferred_element_type=jnp.float32
    )
    score_rows = jnp.take(all_scores.T, safe_ids.reshape(-1), axis=0).reshape(
        safe_ids.shape[0], safe_ids.shape[1], safe_ids.shape[0]
    )
    picked = jnp.einsum("tct->tc", score_rows)
    owner_terms = jnp.where(is_owned, picked, jnp.float32(0.0))
    owner_terms = (
        owner_terms.reshape(req_count, text_count, tp_count, quarter)
        .transpose(0, 2, 1, 3)
        .reshape(device_count, text_count, quarter)
    )
    scores = jnp.sum(lax.all_to_all(owner_terms, ("req", "tp"), 0, 0, tiled=True), axis=0)
    return (hidden_out, scores)


def solution(mesh):
    placed = (
        P("req", "tp", None),
        P("req"),
        P(None, None, "tp"),
        P(None, "tp"),
        P("tp", None),
        P(),
        P(),
        P(),
        P(None, "tp"),
        P("tp"),
        P("tp", None),
        P(),
        P(),
        P(),
        P(("req", "tp"), None),
        P("req", "tp"),
    )
    return jax.shard_map(
        per_device,
        mesh=mesh,
        in_specs=placed,
        out_specs=(P("req", "tp", None), P("req", "tp")),
        check_vma=False,
    )
```

```python
import functools
import jax
import jax.numpy as jnp
from jax import lax
from jax.experimental import pallas as pl
from jax.experimental.pallas import tpu as pltpu
from jax.sharding import PartitionSpec as P

MESH_ID = pl.DeviceIdType.MESH


def _ring_peers():
    n = lax.axis_size("tp")
    me = lax.axis_index("tp")
    rq = lax.axis_index("req")
    core = rq % 2
    right = (me + 1) % n
    left = (me + n - 1) % n
    opp = (me + 2) % n
    relay_to = (me + 1 + 2 * core) % n
    relay_from = (me + n - 1 - 2 * core) % n
    barrier = pltpu.get_barrier_semaphore()
    for peer in (left, right):
        pl.semaphore_signal(barrier, inc=1, device_id=(rq, peer), device_id_type=MESH_ID)
    pl.semaphore_wait(barrier, 2)
    return me, rq, core, right, left, opp, relay_to, relay_from


def _gather_kernel(x_ref, out_ref, send_sem, recv_sem, local_sem):
    me, rq, core, right, left, opp, relay_to, relay_from = _ring_peers()
    rows = x_ref.shape[1]

    def slot(src):
        return out_ref.at[:, pl.ds(src * rows, rows), :]

    local = pltpu.make_async_copy(x_ref, slot(me), local_sem)
    local.start()
    to_right = pltpu.make_async_remote_copy(
        x_ref, slot(me), send_sem.at[0], recv_sem.at[0], device_id=(rq, right), device_id_type=MESH_ID
    )
    to_left = pltpu.make_async_remote_copy(
        x_ref, slot(me), send_sem.at[1], recv_sem.at[1], device_id=(rq, left), device_id_type=MESH_ID
    )
    to_right.start()
    to_left.start()
    from_relay = pltpu.make_async_remote_copy(
        x_ref, slot(relay_from), send_sem.at[2], recv_sem.at[core], device_id=(rq, relay_to),
        device_id_type=MESH_ID,
    )
    from_relay.wait_recv()
    forward = pltpu.make_async_remote_copy(
        slot(relay_from), slot(relay_from), send_sem.at[2], recv_sem.at[2], device_id=(rq, relay_to),
        device_id_type=MESH_ID,
    )
    forward.start()
    other_side = (me + 1 + 2 * (1 - core)) % lax.axis_size("tp")
    from_other = pltpu.make_async_remote_copy(
        x_ref, slot(other_side), send_sem.at[0], recv_sem.at[1 - core], device_id=(rq, right),
        device_id_type=MESH_ID,
    )
    from_other.wait_recv()
    from_opp = pltpu.make_async_remote_copy(
        x_ref, slot(opp), send_sem.at[0], recv_sem.at[2], device_id=(rq, right), device_id_type=MESH_ID
    )
    from_opp.wait_recv()
    to_right.wait_send()
    to_left.wait_send()
    forward.wait_send()
    local.wait()


def ring_all_gather(x, collective_id):
    texts, rows, width = x.shape
    n = lax.axis_size("tp")
    return pl.pallas_call(
        _gather_kernel,
        out_shape=jax.ShapeDtypeStruct((texts, n * rows, width), x.dtype),
        in_specs=[pl.BlockSpec(memory_space=pl.ANY)],
        out_specs=pl.BlockSpec(memory_space=pl.ANY),
        scratch_shapes=[
            pltpu.SemaphoreType.DMA((3,)),
            pltpu.SemaphoreType.DMA((3,)),
            pltpu.SemaphoreType.DMA,
        ],
        compiler_params=pltpu.CompilerParams(collective_id=collective_id, has_side_effects=True),
    )(x)


def _scatter_kernel(p_ref, recv_ref, relay_ref, send_sem, recv_sem, relay_sem):
    me, rq, core, right, left, opp, relay_to, relay_from = _ring_peers()
    rows = recv_ref.shape[2]

    def block(dst):
        return p_ref.at[:, pl.ds(dst * rows, rows), :]

    to_right = pltpu.make_async_remote_copy(
        block(right), recv_ref.at[0], send_sem.at[0], recv_sem.at[0], device_id=(rq, right),
        device_id_type=MESH_ID,
    )
    to_left = pltpu.make_async_remote_copy(
        block(left), recv_ref.at[1], send_sem.at[1], recv_sem.at[1], device_id=(rq, left),
        device_id_type=MESH_ID,
    )
    to_relay = pltpu.make_async_remote_copy(
        block(opp), relay_ref, send_sem.at[2], relay_sem, device_id=(rq, relay_to),
        device_id_type=MESH_ID,
    )
    to_right.start()
    to_left.start()
    to_relay.start()
    to_relay.wait_recv()
    forward = pltpu.make_async_remote_copy(
        relay_ref, recv_ref.at[2], send_sem.at[3], recv_sem.at[2], device_id=(rq, relay_to),
        device_id_type=MESH_ID,
    )
    forward.start()
    to_right.wait_recv()
    to_left.wait_recv()
    forward.wait_recv()
    to_right.wait_send()
    to_left.wait_send()
    to_relay.wait_send()
    forward.wait_send()


def ring_reduce_scatter(p, collective_id):
    texts, all_rows, width = p.shape
    n = lax.axis_size("tp")
    rows = all_rows // n
    recv, _ = pl.pallas_call(
        _scatter_kernel,
        out_shape=(
            jax.ShapeDtypeStruct((n - 1, texts, rows, width), p.dtype),
            jax.ShapeDtypeStruct((texts, rows, width), p.dtype),
        ),
        in_specs=[pl.BlockSpec(memory_space=pl.ANY)],
        out_specs=(pl.BlockSpec(memory_space=pl.ANY), pl.BlockSpec(memory_space=pl.ANY)),
        scratch_shapes=[
            pltpu.SemaphoreType.DMA((4,)),
            pltpu.SemaphoreType.DMA((3,)),
            pltpu.SemaphoreType.DMA,
        ],
        compiler_params=pltpu.CompilerParams(collective_id=collective_id, has_side_effects=True),
    )(p)
    return recv


HEAD_DIM = 64
WINDOW = 512


layer_eps = 1e-05
norm_eps = 1e-06


def layer_norm(values, gain, shift):
    centre = values - jnp.mean(values, axis=-1, keepdims=True)
    spread = jnp.mean(centre * centre, axis=-1, keepdims=True)
    return centre * lax.rsqrt(spread + layer_eps) * gain + shift


def window_attention(queries_h, keys_h, values_h, lengths):
    seq_len = queries_h.shape[1]
    half_window = WINDOW // 2
    scale_factor = HEAD_DIM ** (-0.5)
    pos = jnp.arange(seq_len, dtype=jnp.int32)
    near = jnp.abs(pos[:, None] - pos[None, :]) <= half_window
    keep_mask = near[None] & (pos[None, None, :] < lengths[:, None, None])
    logits = (
        jnp.einsum("tqhe,tkhe->thqk", queries_h, keys_h, preferred_element_type=jnp.float32)
        * scale_factor
    )
    logits = jnp.where(keep_mask[:, None], logits, jnp.float32(-1e30))
    top_val = jnp.max(logits, axis=-1, keepdims=True)
    expo = jnp.exp(logits - top_val)
    attn_weights = (expo / jnp.sum(expo, axis=-1, keepdims=True)).astype(jnp.bfloat16)
    context = jnp.einsum(
        "thqk,tkhe->tqhe", attn_weights, values_h, preferred_element_type=jnp.float32
    )
    context = jnp.where(
        (pos[None, :] < lengths[:, None])[:, :, None, None], context, jnp.float32(0.0)
    )
    return context.astype(jnp.bfloat16).reshape(
        queries_h.shape[0], seq_len, queries_h.shape[2] * HEAD_DIM
    )


def per_device(
    states,
    lengths,
    w_qkv,
    b_qkv,
    w_out,
    b_out,
    ln1_gain,
    ln1_shift,
    w_up,
    b_up,
    w_down,
    b_down,
    ln2_gain,
    ln2_shift,
    index_rows,
    cand_ids,
):
    tp_count = lax.axis_size("tp")
    tp_rank = lax.axis_index("tp")
    req_count = lax.axis_size("req")
    req_rank = lax.axis_index("req")
    text_count, row_share, model_width = states.shape
    quarter = cand_ids.shape[1]
    full_states = ring_all_gather(states, 0)
    device_count = req_count * tp_count
    text_ids = ring_all_gather(cand_ids[:, None, :], 4)
    seq_len = full_states.shape[1]
    local_width = w_qkv.shape[2]
    heads_here = local_width // HEAD_DIM
    projected = (
        jnp.einsum("tsd,dce->tsce", full_states, w_qkv, preferred_element_type=jnp.float32) + b_qkv
    ).astype(jnp.bfloat16)
    queries_h = projected[:, :, 0].reshape(text_count, seq_len, heads_here, HEAD_DIM)
    keys_h = projected[:, :, 1].reshape(text_count, seq_len, heads_here, HEAD_DIM)
    values_h = projected[:, :, 2].reshape(text_count, seq_len, heads_here, HEAD_DIM)

    context = window_attention(queries_h, keys_h, values_h, lengths)
    partial_value = jnp.einsum("tsk,kd->tsd", context, w_out, preferred_element_type=jnp.float32)
    partial_value = partial_value.astype(jnp.bfloat16)
    attn_recv = ring_reduce_scatter(partial_value, 1)
    attn_sum = lax.dynamic_slice_in_dim(partial_value, tp_rank * row_share, row_share, 1).astype(
        jnp.float32
    ) + jnp.sum(attn_recv.astype(jnp.float32), axis=0)
    normed_local = layer_norm(
        states.astype(jnp.float32) + attn_sum + b_out, ln1_gain, ln1_shift
    ).astype(jnp.bfloat16)
    normed_full = ring_all_gather(normed_local, 2)
    up_act = jax.nn.gelu(
        jnp.einsum("tsd,df->tsf", normed_full, w_up, preferred_element_type=jnp.float32) + b_up,
        approximate=False,
    ).astype(jnp.bfloat16)
    down_part = jnp.einsum(
        "tsf,fd->tsd", up_act, w_down, preferred_element_type=jnp.float32
    ).astype(jnp.bfloat16)
    down_recv = ring_reduce_scatter(down_part, 3)
    down_sum = lax.dynamic_slice_in_dim(down_part, tp_rank * row_share, row_share, 1).astype(
        jnp.float32
    ) + jnp.sum(down_recv.astype(jnp.float32), axis=0)
    hidden_out = layer_norm(
        normed_local.astype(jnp.float32) + down_sum + b_down, ln2_gain, ln2_shift
    ).astype(jnp.bfloat16)
    positions = tp_rank * row_share + jnp.arange(row_share, dtype=jnp.int32)
    is_valid = positions[None, :] < lengths[:, None]
    local_pool = jnp.sum(
        jnp.where(is_valid[:, :, None], hidden_out.astype(jnp.float32), jnp.float32(0.0)), axis=1
    )
    pooled = jnp.sum(ring_all_gather(local_pool[:, None, :], 5), axis=1) / lengths.astype(
        jnp.float32
    )[:, None]
    query_vec = (
        pooled * lax.rsqrt(jnp.mean(pooled * pooled, axis=-1, keepdims=True) + norm_eps)
    ).astype(jnp.bfloat16)
    bundle = jnp.concatenate(
        [query_vec.astype(jnp.float32), text_ids.reshape(text_count, -1).astype(jnp.float32)], axis=1
    )
    bundle = lax.all_to_all(
        jnp.broadcast_to(bundle[None], (req_count,) + bundle.shape), "req", 0, 0, tiled=True
    ).reshape(req_count * text_count, bundle.shape[1])
    all_queries = bundle[:, :model_width].astype(jnp.bfloat16)
    all_ids = bundle[:, model_width:].astype(jnp.int32)
    rows_here = index_rows.shape[0]
    first_row = (req_rank * tp_count + tp_rank) * rows_here
    local_ids = all_ids - first_row
    is_owned = (local_ids >= 0) & (local_ids < rows_here)
    safe_ids = jnp.clip(local_ids, 0, rows_here - 1)
    all_scores = jnp.einsum(
        "td,rd->tr", all_queries, index_rows, preferred_element_type=jnp.float32
    )
    score_rows = jnp.take(all_scores.T, safe_ids.reshape(-1), axis=0).reshape(
        safe_ids.shape[0], safe_ids.shape[1], safe_ids.shape[0]
    )
    picked = jnp.einsum("tct->tc", score_rows)
    owner_terms = jnp.where(is_owned, picked, jnp.float32(0.0))
    owner_terms = (
        owner_terms.reshape(req_count, text_count, tp_count, quarter)
        .transpose(0, 2, 1, 3)
        .reshape(device_count, text_count, quarter)
    )
    scores = jnp.sum(lax.all_to_all(owner_terms, ("req", "tp"), 0, 0, tiled=True), axis=0)
    return (hidden_out, scores)


def solution(mesh):
    placed = (
        P("req", "tp", None),
        P("req"),
        P(None, None, "tp"),
        P(None, "tp"),
        P("tp", None),
        P(),
        P(),
        P(),
        P(None, "tp"),
        P("tp"),
        P("tp", None),
        P(),
        P(),
        P(),
        P(("req", "tp"), None),
        P("req", "tp"),
    )
    return jax.shard_map(
        per_device,
        mesh=mesh,
        in_specs=placed,
        out_specs=(P("req", "tp", None), P("req", "tp")),
        check_vma=False,
    )
```

```python
import functools
import jax
import jax.numpy as jnp
from jax import lax
from jax.experimental import pallas as pl
from jax.experimental.pallas import tpu as pltpu
from jax.sharding import PartitionSpec as P

MESH_ID = pl.DeviceIdType.MESH


def _ring_peers():
    n = lax.axis_size("tp")
    me = lax.axis_index("tp")
    rq = lax.axis_index("req")
    core = rq % 2
    right = (me + 1) % n
    left = (me + n - 1) % n
    opp = (me + 2) % n
    relay_to = (me + 1 + 2 * core) % n
    relay_from = (me + n - 1 - 2 * core) % n
    barrier = pltpu.get_barrier_semaphore()
    for peer in (left, right):
        pl.semaphore_signal(barrier, inc=1, device_id=(rq, peer), device_id_type=MESH_ID)
    pl.semaphore_wait(barrier, 2)
    return me, rq, core, right, left, opp, relay_to, relay_from


def _gather_kernel(chunks, x_ref, out_ref, send_sem, recv_sem, local_sem):
    me, rq, core, right, left, opp, relay_to, relay_from = _ring_peers()
    rows = x_ref.shape[1]
    step = rows // chunks

    def part(ref, k):
        return ref.at[:, pl.ds(k * step, step), :]

    def slot(src, k):
        return out_ref.at[:, pl.ds(src * rows + k * step, step), :]

    def copy(src, dst, send, recv, peer):
        return pltpu.make_async_remote_copy(
            src, dst, send, recv, device_id=(rq, peer), device_id_type=MESH_ID
        )

    local = pltpu.make_async_copy(x_ref, out_ref.at[:, pl.ds(me * rows, rows), :], local_sem)
    local.start()
    sends = []
    for k in range(chunks):
        to_right = copy(part(x_ref, k), slot(me, k), send_sem.at[0, k], recv_sem.at[0, k], right)
        to_left = copy(part(x_ref, k), slot(me, k), send_sem.at[1, k], recv_sem.at[1, k], left)
        to_right.start()
        to_left.start()
        sends += [to_right, to_left]
    for k in range(chunks):
        copy(part(x_ref, k), slot(relay_from, k), send_sem.at[2, k], recv_sem.at[core, k], right).wait_recv()
        forward = copy(
            slot(relay_from, k), slot(relay_from, k), send_sem.at[2, k], recv_sem.at[2, k], relay_to
        )
        forward.start()
        sends.append(forward)
    other_side = (me + 1 + 2 * (1 - core)) % lax.axis_size("tp")
    for k in range(chunks):
        copy(part(x_ref, k), slot(other_side, k), send_sem.at[0, k], recv_sem.at[1 - core, k], right).wait_recv()
    for k in range(chunks):
        copy(part(x_ref, k), slot(opp, k), send_sem.at[0, k], recv_sem.at[2, k], right).wait_recv()
    for c in sends:
        c.wait_send()
    local.wait()


def ring_all_gather(x, collective_id, chunks=1):
    texts, rows, width = x.shape
    n = lax.axis_size("tp")
    return pl.pallas_call(
        functools.partial(_gather_kernel, chunks),
        out_shape=jax.ShapeDtypeStruct((texts, n * rows, width), x.dtype),
        in_specs=[pl.BlockSpec(memory_space=pl.ANY)],
        out_specs=pl.BlockSpec(memory_space=pl.ANY),
        scratch_shapes=[
            pltpu.SemaphoreType.DMA((3, chunks)),
            pltpu.SemaphoreType.DMA((3, chunks)),
            pltpu.SemaphoreType.DMA,
        ],
        compiler_params=pltpu.CompilerParams(collective_id=collective_id, has_side_effects=True),
    )(x)


def _scatter_kernel(chunks, p_ref, recv_ref, relay_ref, send_sem, recv_sem, relay_sem):
    me, rq, core, right, left, opp, relay_to, relay_from = _ring_peers()
    rows = recv_ref.shape[2]
    step = rows // chunks

    def block(dst, k):
        return p_ref.at[:, pl.ds(dst * rows + k * step, step), :]

    def part(ref, k):
        return ref.at[:, pl.ds(k * step, step), :]

    def copy(src, dst, send, recv, peer):
        return pltpu.make_async_remote_copy(
            src, dst, send, recv, device_id=(rq, peer), device_id_type=MESH_ID
        )

    sends = []
    relays = []
    for k in range(chunks):
        to_relay = copy(block(opp, k), part(relay_ref, k), send_sem.at[2, k], relay_sem.at[k], relay_to)
        to_right = copy(block(right, k), part(recv_ref.at[0], k), send_sem.at[0, k], recv_sem.at[0, k], right)
        to_left = copy(block(left, k), part(recv_ref.at[1], k), send_sem.at[1, k], recv_sem.at[1, k], left)
        to_relay.start()
        to_right.start()
        to_left.start()
        sends += [to_relay, to_right, to_left]
        relays.append(to_relay)
    forwards = []
    for k in range(chunks):
        relays[k].wait_recv()
        forward = copy(
            part(relay_ref, k), part(recv_ref.at[2], k), send_sem.at[3, k], recv_sem.at[2, k], relay_to
        )
        forward.start()
        sends.append(forward)
        forwards.append(forward)
    for k in range(chunks):
        sends[3 * k + 1].wait_recv()
        sends[3 * k + 2].wait_recv()
        forwards[k].wait_recv()
    for c in sends:
        c.wait_send()


def ring_reduce_scatter(p, collective_id, chunks=1):
    texts, all_rows, width = p.shape
    n = lax.axis_size("tp")
    rows = all_rows // n
    recv, _ = pl.pallas_call(
        functools.partial(_scatter_kernel, chunks),
        out_shape=(
            jax.ShapeDtypeStruct((n - 1, texts, rows, width), p.dtype),
            jax.ShapeDtypeStruct((texts, rows, width), p.dtype),
        ),
        in_specs=[pl.BlockSpec(memory_space=pl.ANY)],
        out_specs=(pl.BlockSpec(memory_space=pl.ANY), pl.BlockSpec(memory_space=pl.ANY)),
        scratch_shapes=[
            pltpu.SemaphoreType.DMA((4, chunks)),
            pltpu.SemaphoreType.DMA((3, chunks)),
            pltpu.SemaphoreType.DMA((chunks,)),
        ],
        compiler_params=pltpu.CompilerParams(collective_id=collective_id, has_side_effects=True),
    )(p)
    return recv


HEAD_DIM = 64
RING_CHUNKS = 4
WINDOW = 512


layer_eps = 1e-05
norm_eps = 1e-06


def layer_norm(values, gain, shift):
    centre = values - jnp.mean(values, axis=-1, keepdims=True)
    spread = jnp.mean(centre * centre, axis=-1, keepdims=True)
    return centre * lax.rsqrt(spread + layer_eps) * gain + shift


def window_attention(queries_h, keys_h, values_h, lengths):
    seq_len = queries_h.shape[1]
    half_window = WINDOW // 2
    scale_factor = HEAD_DIM ** (-0.5)
    pos = jnp.arange(seq_len, dtype=jnp.int32)
    near = jnp.abs(pos[:, None] - pos[None, :]) <= half_window
    keep_mask = near[None] & (pos[None, None, :] < lengths[:, None, None])
    logits = (
        jnp.einsum("tqhe,tkhe->thqk", queries_h, keys_h, preferred_element_type=jnp.float32)
        * scale_factor
    )
    logits = jnp.where(keep_mask[:, None], logits, jnp.float32(-1e30))
    top_val = jnp.max(logits, axis=-1, keepdims=True)
    expo = jnp.exp(logits - top_val)
    attn_weights = (expo / jnp.sum(expo, axis=-1, keepdims=True)).astype(jnp.bfloat16)
    context = jnp.einsum(
        "thqk,tkhe->tqhe", attn_weights, values_h, preferred_element_type=jnp.float32
    )
    context = jnp.where(
        (pos[None, :] < lengths[:, None])[:, :, None, None], context, jnp.float32(0.0)
    )
    return context.astype(jnp.bfloat16).reshape(
        queries_h.shape[0], seq_len, queries_h.shape[2] * HEAD_DIM
    )


def per_device(
    states,
    lengths,
    w_qkv,
    b_qkv,
    w_out,
    b_out,
    ln1_gain,
    ln1_shift,
    w_up,
    b_up,
    w_down,
    b_down,
    ln2_gain,
    ln2_shift,
    index_rows,
    cand_ids,
):
    tp_count = lax.axis_size("tp")
    tp_rank = lax.axis_index("tp")
    req_count = lax.axis_size("req")
    req_rank = lax.axis_index("req")
    text_count, row_share, model_width = states.shape
    quarter = cand_ids.shape[1]
    full_states = ring_all_gather(states, 0, RING_CHUNKS)
    device_count = req_count * tp_count
    text_ids = ring_all_gather(cand_ids[:, None, :], 4)
    seq_len = full_states.shape[1]
    local_width = w_qkv.shape[2]
    heads_here = local_width // HEAD_DIM
    projected = (
        jnp.einsum("tsd,dce->tsce", full_states, w_qkv, preferred_element_type=jnp.float32) + b_qkv
    ).astype(jnp.bfloat16)
    queries_h = projected[:, :, 0].reshape(text_count, seq_len, heads_here, HEAD_DIM)
    keys_h = projected[:, :, 1].reshape(text_count, seq_len, heads_here, HEAD_DIM)
    values_h = projected[:, :, 2].reshape(text_count, seq_len, heads_here, HEAD_DIM)

    context = window_attention(queries_h, keys_h, values_h, lengths)
    partial_value = jnp.einsum("tsk,kd->tsd", context, w_out, preferred_element_type=jnp.float32)
    partial_value = partial_value.astype(jnp.bfloat16)
    attn_recv = ring_reduce_scatter(partial_value, 1, RING_CHUNKS)
    attn_sum = lax.dynamic_slice_in_dim(partial_value, tp_rank * row_share, row_share, 1).astype(
        jnp.float32
    ) + jnp.sum(attn_recv.astype(jnp.float32), axis=0)
    normed_local = layer_norm(
        states.astype(jnp.float32) + attn_sum + b_out, ln1_gain, ln1_shift
    ).astype(jnp.bfloat16)
    normed_full = ring_all_gather(normed_local, 2, RING_CHUNKS)
    up_act = jax.nn.gelu(
        jnp.einsum("tsd,df->tsf", normed_full, w_up, preferred_element_type=jnp.float32) + b_up,
        approximate=False,
    ).astype(jnp.bfloat16)
    down_part = jnp.einsum(
        "tsf,fd->tsd", up_act, w_down, preferred_element_type=jnp.float32
    ).astype(jnp.bfloat16)
    down_recv = ring_reduce_scatter(down_part, 3, RING_CHUNKS)
    down_sum = lax.dynamic_slice_in_dim(down_part, tp_rank * row_share, row_share, 1).astype(
        jnp.float32
    ) + jnp.sum(down_recv.astype(jnp.float32), axis=0)
    hidden_out = layer_norm(
        normed_local.astype(jnp.float32) + down_sum + b_down, ln2_gain, ln2_shift
    ).astype(jnp.bfloat16)
    positions = tp_rank * row_share + jnp.arange(row_share, dtype=jnp.int32)
    is_valid = positions[None, :] < lengths[:, None]
    local_pool = jnp.sum(
        jnp.where(is_valid[:, :, None], hidden_out.astype(jnp.float32), jnp.float32(0.0)), axis=1
    )
    pooled = jnp.sum(ring_all_gather(local_pool[:, None, :], 5), axis=1) / lengths.astype(
        jnp.float32
    )[:, None]
    query_vec = (
        pooled * lax.rsqrt(jnp.mean(pooled * pooled, axis=-1, keepdims=True) + norm_eps)
    ).astype(jnp.bfloat16)
    bundle = jnp.concatenate(
        [query_vec.astype(jnp.float32), text_ids.reshape(text_count, -1).astype(jnp.float32)], axis=1
    )
    bundle = lax.all_to_all(
        jnp.broadcast_to(bundle[None], (req_count,) + bundle.shape), "req", 0, 0, tiled=True
    ).reshape(req_count * text_count, bundle.shape[1])
    all_queries = bundle[:, :model_width].astype(jnp.bfloat16)
    all_ids = bundle[:, model_width:].astype(jnp.int32)
    rows_here = index_rows.shape[0]
    first_row = (req_rank * tp_count + tp_rank) * rows_here
    local_ids = all_ids - first_row
    is_owned = (local_ids >= 0) & (local_ids < rows_here)
    safe_ids = jnp.clip(local_ids, 0, rows_here - 1)
    all_scores = jnp.einsum(
        "td,rd->tr", all_queries, index_rows, preferred_element_type=jnp.float32
    )
    score_rows = jnp.take(all_scores.T, safe_ids.reshape(-1), axis=0).reshape(
        safe_ids.shape[0], safe_ids.shape[1], safe_ids.shape[0]
    )
    picked = jnp.einsum("tct->tc", score_rows)
    owner_terms = jnp.where(is_owned, picked, jnp.float32(0.0))
    owner_terms = (
        owner_terms.reshape(req_count, text_count, tp_count, quarter)
        .transpose(0, 2, 1, 3)
        .reshape(device_count, text_count, quarter)
    )
    scores = jnp.sum(lax.all_to_all(owner_terms, ("req", "tp"), 0, 0, tiled=True), axis=0)
    return (hidden_out, scores)


def solution(mesh):
    placed = (
        P("req", "tp", None),
        P("req"),
        P(None, None, "tp"),
        P(None, "tp"),
        P("tp", None),
        P(),
        P(),
        P(),
        P(None, "tp"),
        P("tp"),
        P("tp", None),
        P(),
        P(),
        P(),
        P(("req", "tp"), None),
        P("req", "tp"),
    )
    return jax.shard_map(
        per_device,
        mesh=mesh,
        in_specs=placed,
        out_specs=(P("req", "tp", None), P("req", "tp")),
        check_vma=False,
    )
```

```python
import functools
import jax
import jax.numpy as jnp
from jax import lax
from jax.experimental import pallas as pl
from jax.experimental.pallas import tpu as pltpu
from jax.sharding import PartitionSpec as P

MESH_ID = pl.DeviceIdType.MESH


def _ring_peers():
    n = lax.axis_size("tp")
    me = lax.axis_index("tp")
    rq = lax.axis_index("req")
    core = rq % 2
    right = (me + 1) % n
    left = (me + n - 1) % n
    opp = (me + 2) % n
    relay_to = (me + 1 + 2 * core) % n
    relay_from = (me + n - 1 - 2 * core) % n
    barrier = pltpu.get_barrier_semaphore()
    for peer in (left, right):
        pl.semaphore_signal(barrier, inc=1, device_id=(rq, peer), device_id_type=MESH_ID)
    pl.semaphore_wait(barrier, 2)
    return me, rq, core, right, left, opp, relay_to, relay_from


def _gather_kernel(chunks, x_ref, out_ref, send_sem, recv_sem, local_sem):
    me, rq, core, right, left, opp, relay_to, relay_from = _ring_peers()
    rows = x_ref.shape[1]
    step = rows // chunks

    def part(ref, k):
        return ref.at[:, pl.ds(k * step, step), :]

    def slot(src, k):
        return out_ref.at[:, pl.ds(src * rows + k * step, step), :]

    def copy(src, dst, send, recv, peer):
        return pltpu.make_async_remote_copy(
            src, dst, send, recv, device_id=(rq, peer), device_id_type=MESH_ID
        )

    local = pltpu.make_async_copy(x_ref, out_ref.at[:, pl.ds(me * rows, rows), :], local_sem)
    local.start()
    sends = []
    for k in range(chunks):
        to_right = copy(part(x_ref, k), slot(me, k), send_sem.at[0, k], recv_sem.at[0, k], right)
        to_left = copy(part(x_ref, k), slot(me, k), send_sem.at[1, k], recv_sem.at[1, k], left)
        to_right.start()
        to_left.start()
        sends += [to_right, to_left]
    for k in range(chunks):
        copy(part(x_ref, k), slot(relay_from, k), send_sem.at[2, k], recv_sem.at[core, k], right).wait_recv()
        forward = copy(
            slot(relay_from, k), slot(relay_from, k), send_sem.at[2, k], recv_sem.at[2, k], relay_to
        )
        forward.start()
        sends.append(forward)
    other_side = (me + 1 + 2 * (1 - core)) % lax.axis_size("tp")
    for k in range(chunks):
        copy(part(x_ref, k), slot(other_side, k), send_sem.at[0, k], recv_sem.at[1 - core, k], right).wait_recv()
    for k in range(chunks):
        copy(part(x_ref, k), slot(opp, k), send_sem.at[0, k], recv_sem.at[2, k], right).wait_recv()
    for c in sends:
        c.wait_send()
    local.wait()


def ring_all_gather(x, collective_id, chunks=1):
    texts, rows, width = x.shape
    n = lax.axis_size("tp")
    return pl.pallas_call(
        functools.partial(_gather_kernel, chunks),
        out_shape=jax.ShapeDtypeStruct((texts, n * rows, width), x.dtype),
        in_specs=[pl.BlockSpec(memory_space=pl.ANY)],
        out_specs=pl.BlockSpec(memory_space=pl.ANY),
        scratch_shapes=[
            pltpu.SemaphoreType.DMA((3, chunks)),
            pltpu.SemaphoreType.DMA((3, chunks)),
            pltpu.SemaphoreType.DMA,
        ],
        compiler_params=pltpu.CompilerParams(collective_id=collective_id, has_side_effects=True),
    )(x)


def _scatter_kernel(chunks, p_ref, recv_ref, relay_ref, send_sem, recv_sem, relay_sem):
    me, rq, core, right, left, opp, relay_to, relay_from = _ring_peers()
    rows = recv_ref.shape[2]
    step = rows // chunks

    def block(dst, k):
        return p_ref.at[:, pl.ds(dst * rows + k * step, step), :]

    def part(ref, k):
        return ref.at[:, pl.ds(k * step, step), :]

    def copy(src, dst, send, recv, peer):
        return pltpu.make_async_remote_copy(
            src, dst, send, recv, device_id=(rq, peer), device_id_type=MESH_ID
        )

    sends = []
    relays = []
    for k in range(chunks):
        to_relay = copy(block(opp, k), part(relay_ref, k), send_sem.at[2, k], relay_sem.at[k], relay_to)
        to_right = copy(block(right, k), part(recv_ref.at[0], k), send_sem.at[0, k], recv_sem.at[0, k], right)
        to_left = copy(block(left, k), part(recv_ref.at[1], k), send_sem.at[1, k], recv_sem.at[1, k], left)
        to_relay.start()
        to_right.start()
        to_left.start()
        sends += [to_relay, to_right, to_left]
        relays.append(to_relay)
    forwards = []
    for k in range(chunks):
        relays[k].wait_recv()
        forward = copy(
            part(relay_ref, k), part(recv_ref.at[2], k), send_sem.at[3, k], recv_sem.at[2, k], relay_to
        )
        forward.start()
        sends.append(forward)
        forwards.append(forward)
    for k in range(chunks):
        sends[3 * k + 1].wait_recv()
        sends[3 * k + 2].wait_recv()
        forwards[k].wait_recv()
    for c in sends:
        c.wait_send()


def ring_reduce_scatter(p, collective_id, chunks=1):
    texts, all_rows, width = p.shape
    n = lax.axis_size("tp")
    rows = all_rows // n
    recv, _ = pl.pallas_call(
        functools.partial(_scatter_kernel, chunks),
        out_shape=(
            jax.ShapeDtypeStruct((n - 1, texts, rows, width), p.dtype),
            jax.ShapeDtypeStruct((texts, rows, width), p.dtype),
        ),
        in_specs=[pl.BlockSpec(memory_space=pl.ANY)],
        out_specs=(pl.BlockSpec(memory_space=pl.ANY), pl.BlockSpec(memory_space=pl.ANY)),
        scratch_shapes=[
            pltpu.SemaphoreType.DMA((4, chunks)),
            pltpu.SemaphoreType.DMA((3, chunks)),
            pltpu.SemaphoreType.DMA((chunks,)),
        ],
        compiler_params=pltpu.CompilerParams(collective_id=collective_id, has_side_effects=True),
    )(p)
    return recv


def _peer_id(axes, peer):
    if axes == ("tp",):
        return (lax.axis_index("req"), peer)
    if axes == ("req",):
        return (peer, lax.axis_index("tp"))
    n_tp = lax.axis_size("tp")
    return (peer // n_tp, peer % n_tp)


def _direct_kernel(axes, scatter, x_ref, out_ref, send_sem, recv_sem, local_sem):
    n = out_ref.shape[0]
    me = lax.axis_index(axes)
    barrier = pltpu.get_barrier_semaphore()

    def greet(d, carry):
        peer = (me + d) % n
        pl.semaphore_signal(barrier, inc=1, device_id=_peer_id(axes, peer), device_id_type=MESH_ID)
        return carry

    lax.fori_loop(1, n, greet, 0)
    pl.semaphore_wait(barrier, n - 1)

    def source(peer):
        return x_ref.at[peer] if scatter else x_ref

    local = pltpu.make_async_copy(source(me), out_ref.at[me], local_sem)
    local.start()

    def send(d, carry):
        peer = (me + d) % n
        pltpu.make_async_remote_copy(
            source(peer), out_ref.at[me], send_sem.at[d], recv_sem.at[me],
            device_id=_peer_id(axes, peer), device_id_type=MESH_ID,
        ).start()
        return carry

    lax.fori_loop(1, n, send, 0)

    def receive(d, carry):
        src = (me + n - d) % n
        pltpu.make_async_remote_copy(
            source(src), out_ref.at[src], send_sem.at[d], recv_sem.at[src],
            device_id=_peer_id(axes, src), device_id_type=MESH_ID,
        ).wait_recv()
        return carry

    lax.fori_loop(1, n, receive, 0)

    def sent(d, carry):
        peer = (me + d) % n
        pltpu.make_async_remote_copy(
            source(peer), out_ref.at[me], send_sem.at[d], recv_sem.at[me],
            device_id=_peer_id(axes, peer), device_id_type=MESH_ID,
        ).wait_send()
        return carry

    lax.fori_loop(1, n, sent, 0)
    local.wait()


def direct_exchange(x, axes, collective_id, scatter=False):
    n = 1
    for name in axes:
        n *= lax.axis_size(name)
    block = x.shape[1:] if scatter else x.shape
    return pl.pallas_call(
        functools.partial(_direct_kernel, axes, scatter),
        out_shape=jax.ShapeDtypeStruct((n,) + block, x.dtype),
        in_specs=[pl.BlockSpec(memory_space=pl.ANY)],
        out_specs=pl.BlockSpec(memory_space=pl.ANY),
        scratch_shapes=[
            pltpu.SemaphoreType.DMA((n,)),
            pltpu.SemaphoreType.DMA((n,)),
            pltpu.SemaphoreType.DMA,
        ],
        compiler_params=pltpu.CompilerParams(collective_id=collective_id, has_side_effects=True),
    )(x)


HEAD_DIM = 64
RING_CHUNKS = 4
WINDOW = 512


layer_eps = 1e-05
norm_eps = 1e-06


def layer_norm(values, gain, shift):
    centre = values - jnp.mean(values, axis=-1, keepdims=True)
    spread = jnp.mean(centre * centre, axis=-1, keepdims=True)
    return centre * lax.rsqrt(spread + layer_eps) * gain + shift


def window_attention(queries_h, keys_h, values_h, lengths):
    seq_len = queries_h.shape[1]
    half_window = WINDOW // 2
    scale_factor = HEAD_DIM ** (-0.5)
    pos = jnp.arange(seq_len, dtype=jnp.int32)
    near = jnp.abs(pos[:, None] - pos[None, :]) <= half_window
    keep_mask = near[None] & (pos[None, None, :] < lengths[:, None, None])
    logits = (
        jnp.einsum("tqhe,tkhe->thqk", queries_h, keys_h, preferred_element_type=jnp.float32)
        * scale_factor
    )
    logits = jnp.where(keep_mask[:, None], logits, jnp.float32(-1e30))
    top_val = jnp.max(logits, axis=-1, keepdims=True)
    expo = jnp.exp(logits - top_val)
    attn_weights = (expo / jnp.sum(expo, axis=-1, keepdims=True)).astype(jnp.bfloat16)
    context = jnp.einsum(
        "thqk,tkhe->tqhe", attn_weights, values_h, preferred_element_type=jnp.float32
    )
    context = jnp.where(
        (pos[None, :] < lengths[:, None])[:, :, None, None], context, jnp.float32(0.0)
    )
    return context.astype(jnp.bfloat16).reshape(
        queries_h.shape[0], seq_len, queries_h.shape[2] * HEAD_DIM
    )


def per_device(
    states,
    lengths,
    w_qkv,
    b_qkv,
    w_out,
    b_out,
    ln1_gain,
    ln1_shift,
    w_up,
    b_up,
    w_down,
    b_down,
    ln2_gain,
    ln2_shift,
    index_rows,
    cand_ids,
):
    tp_count = lax.axis_size("tp")
    tp_rank = lax.axis_index("tp")
    req_count = lax.axis_size("req")
    req_rank = lax.axis_index("req")
    text_count, row_share, model_width = states.shape
    quarter = cand_ids.shape[1]
    full_states = ring_all_gather(states, 0, RING_CHUNKS)
    device_count = req_count * tp_count
    text_ids = jnp.swapaxes(direct_exchange(cand_ids, ("tp",), 4), 0, 1)
    seq_len = full_states.shape[1]
    local_width = w_qkv.shape[2]
    heads_here = local_width // HEAD_DIM
    projected = (
        jnp.einsum("tsd,dce->tsce", full_states, w_qkv, preferred_element_type=jnp.float32) + b_qkv
    ).astype(jnp.bfloat16)
    queries_h = projected[:, :, 0].reshape(text_count, seq_len, heads_here, HEAD_DIM)
    keys_h = projected[:, :, 1].reshape(text_count, seq_len, heads_here, HEAD_DIM)
    values_h = projected[:, :, 2].reshape(text_count, seq_len, heads_here, HEAD_DIM)

    context = window_attention(queries_h, keys_h, values_h, lengths)
    partial_value = jnp.einsum("tsk,kd->tsd", context, w_out, preferred_element_type=jnp.float32)
    partial_value = partial_value.astype(jnp.bfloat16)
    attn_recv = ring_reduce_scatter(partial_value, 1, RING_CHUNKS)
    attn_sum = lax.dynamic_slice_in_dim(partial_value, tp_rank * row_share, row_share, 1).astype(
        jnp.float32
    ) + jnp.sum(attn_recv.astype(jnp.float32), axis=0)
    normed_local = layer_norm(
        states.astype(jnp.float32) + attn_sum + b_out, ln1_gain, ln1_shift
    ).astype(jnp.bfloat16)
    normed_full = ring_all_gather(normed_local, 2, RING_CHUNKS)
    up_act = jax.nn.gelu(
        jnp.einsum("tsd,df->tsf", normed_full, w_up, preferred_element_type=jnp.float32) + b_up,
        approximate=False,
    ).astype(jnp.bfloat16)
    down_part = jnp.einsum(
        "tsf,fd->tsd", up_act, w_down, preferred_element_type=jnp.float32
    ).astype(jnp.bfloat16)
    down_recv = ring_reduce_scatter(down_part, 3, RING_CHUNKS)
    down_sum = lax.dynamic_slice_in_dim(down_part, tp_rank * row_share, row_share, 1).astype(
        jnp.float32
    ) + jnp.sum(down_recv.astype(jnp.float32), axis=0)
    hidden_out = layer_norm(
        normed_local.astype(jnp.float32) + down_sum + b_down, ln2_gain, ln2_shift
    ).astype(jnp.bfloat16)
    positions = tp_rank * row_share + jnp.arange(row_share, dtype=jnp.int32)
    is_valid = positions[None, :] < lengths[:, None]
    local_pool = jnp.sum(
        jnp.where(is_valid[:, :, None], hidden_out.astype(jnp.float32), jnp.float32(0.0)), axis=1
    )
    pooled = jnp.sum(direct_exchange(local_pool, ("tp",), 5), axis=0) / lengths.astype(
        jnp.float32
    )[:, None]
    query_vec = (
        pooled * lax.rsqrt(jnp.mean(pooled * pooled, axis=-1, keepdims=True) + norm_eps)
    ).astype(jnp.bfloat16)
    bundle = jnp.concatenate(
        [query_vec.astype(jnp.float32), text_ids.reshape(text_count, -1).astype(jnp.float32)], axis=1
    )
    bundle = direct_exchange(bundle, ("req",), 6).reshape(req_count * text_count, bundle.shape[1])
    all_queries = bundle[:, :model_width].astype(jnp.bfloat16)
    all_ids = bundle[:, model_width:].astype(jnp.int32)
    rows_here = index_rows.shape[0]
    first_row = (req_rank * tp_count + tp_rank) * rows_here
    local_ids = all_ids - first_row
    is_owned = (local_ids >= 0) & (local_ids < rows_here)
    safe_ids = jnp.clip(local_ids, 0, rows_here - 1)
    all_scores = jnp.einsum(
        "td,rd->tr", all_queries, index_rows, preferred_element_type=jnp.float32
    )
    score_rows = jnp.take(all_scores.T, safe_ids.reshape(-1), axis=0).reshape(
        safe_ids.shape[0], safe_ids.shape[1], safe_ids.shape[0]
    )
    picked = jnp.einsum("tct->tc", score_rows)
    owner_terms = jnp.where(is_owned, picked, jnp.float32(0.0))
    owner_terms = (
        owner_terms.reshape(req_count, text_count, tp_count, quarter)
        .transpose(0, 2, 1, 3)
        .reshape(device_count, text_count, quarter)
    )
    scores = jnp.sum(direct_exchange(owner_terms, ("req", "tp"), 7, scatter=True), axis=0)
    return (hidden_out, scores)


def solution(mesh):
    placed = (
        P("req", "tp", None),
        P("req"),
        P(None, None, "tp"),
        P(None, "tp"),
        P("tp", None),
        P(),
        P(),
        P(),
        P(None, "tp"),
        P("tp"),
        P("tp", None),
        P(),
        P(),
        P(),
        P(("req", "tp"), None),
        P("req", "tp"),
    )
    return jax.shard_map(
        per_device,
        mesh=mesh,
        in_specs=placed,
        out_specs=(P("req", "tp", None), P("req", "tp")),
        check_vma=False,
    )
```

```python
import functools
import jax
import jax.numpy as jnp
from jax import lax
from jax.experimental import pallas as pl
from jax.experimental.pallas import tpu as pltpu
from jax.sharding import PartitionSpec as P

MESH_ID = pl.DeviceIdType.MESH


def _ring_peers():
    n = lax.axis_size("tp")
    me = lax.axis_index("tp")
    rq = lax.axis_index("req")
    core = rq % 2
    right = (me + 1) % n
    left = (me + n - 1) % n
    opp = (me + 2) % n
    relay_to = (me + 1 + 2 * core) % n
    relay_from = (me + n - 1 - 2 * core) % n
    barrier = pltpu.get_barrier_semaphore()
    for peer in (left, right):
        pl.semaphore_signal(barrier, inc=1, device_id=(rq, peer), device_id_type=MESH_ID)
    pl.semaphore_wait(barrier, 2)
    return me, rq, core, right, left, opp, relay_to, relay_from


def _gather_kernel(chunks, x_ref, out_ref, send_sem, recv_sem, local_sem):
    me, rq, core, right, left, opp, relay_to, relay_from = _ring_peers()
    rows = x_ref.shape[1]
    step = rows // chunks

    def part(ref, k):
        return ref.at[:, pl.ds(k * step, step), :]

    def slot(src, k):
        return out_ref.at[:, pl.ds(src * rows + k * step, step), :]

    def copy(src, dst, send, recv, peer):
        return pltpu.make_async_remote_copy(
            src, dst, send, recv, device_id=(rq, peer), device_id_type=MESH_ID
        )

    local = pltpu.make_async_copy(x_ref, out_ref.at[:, pl.ds(me * rows, rows), :], local_sem)
    local.start()
    sends = []
    for k in range(chunks):
        to_right = copy(part(x_ref, k), slot(me, k), send_sem.at[0, k], recv_sem.at[0, k], right)
        to_left = copy(part(x_ref, k), slot(me, k), send_sem.at[1, k], recv_sem.at[1, k], left)
        to_right.start()
        to_left.start()
        sends += [to_right, to_left]
    for k in range(chunks):
        copy(part(x_ref, k), slot(relay_from, k), send_sem.at[2, k], recv_sem.at[core, k], right).wait_recv()
        forward = copy(
            slot(relay_from, k), slot(relay_from, k), send_sem.at[2, k], recv_sem.at[2, k], relay_to
        )
        forward.start()
        sends.append(forward)
    other_side = (me + 1 + 2 * (1 - core)) % lax.axis_size("tp")
    for k in range(chunks):
        copy(part(x_ref, k), slot(other_side, k), send_sem.at[0, k], recv_sem.at[1 - core, k], right).wait_recv()
    for k in range(chunks):
        copy(part(x_ref, k), slot(opp, k), send_sem.at[0, k], recv_sem.at[2, k], right).wait_recv()
    for c in sends:
        c.wait_send()
    local.wait()


def ring_all_gather(x, collective_id, chunks=1):
    texts, rows, width = x.shape
    n = lax.axis_size("tp")
    return pl.pallas_call(
        functools.partial(_gather_kernel, chunks),
        out_shape=jax.ShapeDtypeStruct((texts, n * rows, width), x.dtype),
        in_specs=[pl.BlockSpec(memory_space=pl.ANY)],
        out_specs=pl.BlockSpec(memory_space=pl.ANY),
        scratch_shapes=[
            pltpu.SemaphoreType.DMA((3, chunks)),
            pltpu.SemaphoreType.DMA((3, chunks)),
            pltpu.SemaphoreType.DMA,
        ],
        compiler_params=pltpu.CompilerParams(collective_id=collective_id, has_side_effects=True),
    )(x)


def _scatter_kernel(chunks, p_ref, recv_ref, relay_ref, send_sem, recv_sem, relay_sem):
    me, rq, core, right, left, opp, relay_to, relay_from = _ring_peers()
    rows = recv_ref.shape[2]
    step = rows // chunks

    def block(dst, k):
        return p_ref.at[:, pl.ds(dst * rows + k * step, step), :]

    def part(ref, k):
        return ref.at[:, pl.ds(k * step, step), :]

    def copy(src, dst, send, recv, peer):
        return pltpu.make_async_remote_copy(
            src, dst, send, recv, device_id=(rq, peer), device_id_type=MESH_ID
        )

    sends = []
    relays = []
    for k in range(chunks):
        to_relay = copy(block(opp, k), part(relay_ref, k), send_sem.at[2, k], relay_sem.at[k], relay_to)
        to_right = copy(block(right, k), part(recv_ref.at[0], k), send_sem.at[0, k], recv_sem.at[0, k], right)
        to_left = copy(block(left, k), part(recv_ref.at[1], k), send_sem.at[1, k], recv_sem.at[1, k], left)
        to_relay.start()
        to_right.start()
        to_left.start()
        sends += [to_relay, to_right, to_left]
        relays.append(to_relay)
    forwards = []
    for k in range(chunks):
        relays[k].wait_recv()
        forward = copy(
            part(relay_ref, k), part(recv_ref.at[2], k), send_sem.at[3, k], recv_sem.at[2, k], relay_to
        )
        forward.start()
        sends.append(forward)
        forwards.append(forward)
    for k in range(chunks):
        sends[3 * k + 1].wait_recv()
        sends[3 * k + 2].wait_recv()
        forwards[k].wait_recv()
    for c in sends:
        c.wait_send()


def ring_reduce_scatter(p, collective_id, chunks=1):
    texts, all_rows, width = p.shape
    n = lax.axis_size("tp")
    rows = all_rows // n
    recv, _ = pl.pallas_call(
        functools.partial(_scatter_kernel, chunks),
        out_shape=(
            jax.ShapeDtypeStruct((n - 1, texts, rows, width), p.dtype),
            jax.ShapeDtypeStruct((texts, rows, width), p.dtype),
        ),
        in_specs=[pl.BlockSpec(memory_space=pl.ANY)],
        out_specs=(pl.BlockSpec(memory_space=pl.ANY), pl.BlockSpec(memory_space=pl.ANY)),
        scratch_shapes=[
            pltpu.SemaphoreType.DMA((4, chunks)),
            pltpu.SemaphoreType.DMA((3, chunks)),
            pltpu.SemaphoreType.DMA((chunks,)),
        ],
        compiler_params=pltpu.CompilerParams(collective_id=collective_id, has_side_effects=True),
    )(p)
    return recv


def _peer_id(axes, peer):
    if axes == ("tp",):
        return (lax.axis_index("req"), peer)
    if axes == ("req",):
        return (peer, lax.axis_index("tp"))
    n_tp = lax.axis_size("tp")
    return (peer // n_tp, peer % n_tp)


def _direct_kernel(axes, scatter, x_ref, out_ref, send_sem, recv_sem, local_sem):
    n = out_ref.shape[0]
    me = lax.axis_index(axes)
    barrier = pltpu.get_barrier_semaphore()

    def greet(d, carry):
        peer = (me + d) % n
        pl.semaphore_signal(barrier, inc=1, device_id=_peer_id(axes, peer), device_id_type=MESH_ID)
        return carry

    lax.fori_loop(1, n, greet, 0)
    pl.semaphore_wait(barrier, n - 1)

    def source(peer):
        return x_ref.at[peer] if scatter else x_ref

    local = pltpu.make_async_copy(source(me), out_ref.at[me], local_sem)
    local.start()

    def send(d, carry):
        peer = (me + d) % n
        pltpu.make_async_remote_copy(
            source(peer), out_ref.at[me], send_sem.at[d], recv_sem.at[me],
            device_id=_peer_id(axes, peer), device_id_type=MESH_ID,
        ).start()
        return carry

    lax.fori_loop(1, n, send, 0)

    def receive(d, carry):
        src = (me + n - d) % n
        pltpu.make_async_remote_copy(
            source(src), out_ref.at[src], send_sem.at[d], recv_sem.at[src],
            device_id=_peer_id(axes, src), device_id_type=MESH_ID,
        ).wait_recv()
        return carry

    lax.fori_loop(1, n, receive, 0)

    def sent(d, carry):
        peer = (me + d) % n
        pltpu.make_async_remote_copy(
            source(peer), out_ref.at[me], send_sem.at[d], recv_sem.at[me],
            device_id=_peer_id(axes, peer), device_id_type=MESH_ID,
        ).wait_send()
        return carry

    lax.fori_loop(1, n, sent, 0)
    local.wait()


def direct_exchange(x, axes, collective_id, scatter=False):
    n = 1
    for name in axes:
        n *= lax.axis_size(name)
    block = x.shape[1:] if scatter else x.shape
    return pl.pallas_call(
        functools.partial(_direct_kernel, axes, scatter),
        out_shape=jax.ShapeDtypeStruct((n,) + block, x.dtype),
        in_specs=[pl.BlockSpec(memory_space=pl.ANY)],
        out_specs=pl.BlockSpec(memory_space=pl.ANY),
        scratch_shapes=[
            pltpu.SemaphoreType.DMA((n,)),
            pltpu.SemaphoreType.DMA((n,)),
            pltpu.SemaphoreType.DMA,
        ],
        compiler_params=pltpu.CompilerParams(collective_id=collective_id, has_side_effects=True),
    )(x)


HEAD_DIM = 64
RING_CHUNKS = 4
SPARSE_PAIRS = 128
WINDOW = 512


layer_eps = 1e-05
norm_eps = 1e-06


def layer_norm(values, gain, shift):
    centre = values - jnp.mean(values, axis=-1, keepdims=True)
    spread = jnp.mean(centre * centre, axis=-1, keepdims=True)
    return centre * lax.rsqrt(spread + layer_eps) * gain + shift


def window_attention(queries_h, keys_h, values_h, lengths):
    seq_len = queries_h.shape[1]
    half_window = WINDOW // 2
    scale_factor = HEAD_DIM ** (-0.5)
    pos = jnp.arange(seq_len, dtype=jnp.int32)
    near = jnp.abs(pos[:, None] - pos[None, :]) <= half_window
    keep_mask = near[None] & (pos[None, None, :] < lengths[:, None, None])
    logits = (
        jnp.einsum("tqhe,tkhe->thqk", queries_h, keys_h, preferred_element_type=jnp.float32)
        * scale_factor
    )
    logits = jnp.where(keep_mask[:, None], logits, jnp.float32(-1e30))
    top_val = jnp.max(logits, axis=-1, keepdims=True)
    expo = jnp.exp(logits - top_val)
    attn_weights = (expo / jnp.sum(expo, axis=-1, keepdims=True)).astype(jnp.bfloat16)
    context = jnp.einsum(
        "thqk,tkhe->tqhe", attn_weights, values_h, preferred_element_type=jnp.float32
    )
    context = jnp.where(
        (pos[None, :] < lengths[:, None])[:, :, None, None], context, jnp.float32(0.0)
    )
    return context.astype(jnp.bfloat16).reshape(
        queries_h.shape[0], seq_len, queries_h.shape[2] * HEAD_DIM
    )


def per_device(
    states,
    lengths,
    w_qkv,
    b_qkv,
    w_out,
    b_out,
    ln1_gain,
    ln1_shift,
    w_up,
    b_up,
    w_down,
    b_down,
    ln2_gain,
    ln2_shift,
    index_rows,
    cand_ids,
):
    tp_count = lax.axis_size("tp")
    tp_rank = lax.axis_index("tp")
    req_count = lax.axis_size("req")
    req_rank = lax.axis_index("req")
    text_count, row_share, model_width = states.shape
    quarter = cand_ids.shape[1]
    full_states = ring_all_gather(states, 0, RING_CHUNKS)
    device_count = req_count * tp_count
    text_ids = jnp.swapaxes(direct_exchange(cand_ids, ("tp",), 4), 0, 1)
    seq_len = full_states.shape[1]
    local_width = w_qkv.shape[2]
    heads_here = local_width // HEAD_DIM
    projected = (
        jnp.einsum("tsd,dce->tsce", full_states, w_qkv, preferred_element_type=jnp.float32) + b_qkv
    ).astype(jnp.bfloat16)
    queries_h = projected[:, :, 0].reshape(text_count, seq_len, heads_here, HEAD_DIM)
    keys_h = projected[:, :, 1].reshape(text_count, seq_len, heads_here, HEAD_DIM)
    values_h = projected[:, :, 2].reshape(text_count, seq_len, heads_here, HEAD_DIM)

    context = window_attention(queries_h, keys_h, values_h, lengths)
    partial_value = jnp.einsum("tsk,kd->tsd", context, w_out, preferred_element_type=jnp.float32)
    partial_value = partial_value.astype(jnp.bfloat16)
    attn_recv = ring_reduce_scatter(partial_value, 1, RING_CHUNKS)
    attn_sum = lax.dynamic_slice_in_dim(partial_value, tp_rank * row_share, row_share, 1).astype(
        jnp.float32
    ) + jnp.sum(attn_recv.astype(jnp.float32), axis=0)
    normed_local = layer_norm(
        states.astype(jnp.float32) + attn_sum + b_out, ln1_gain, ln1_shift
    ).astype(jnp.bfloat16)
    normed_full = ring_all_gather(normed_local, 2, RING_CHUNKS)
    up_act = jax.nn.gelu(
        jnp.einsum("tsd,df->tsf", normed_full, w_up, preferred_element_type=jnp.float32) + b_up,
        approximate=False,
    ).astype(jnp.bfloat16)
    down_part = jnp.einsum(
        "tsf,fd->tsd", up_act, w_down, preferred_element_type=jnp.float32
    ).astype(jnp.bfloat16)
    down_recv = ring_reduce_scatter(down_part, 3, RING_CHUNKS)
    down_sum = lax.dynamic_slice_in_dim(down_part, tp_rank * row_share, row_share, 1).astype(
        jnp.float32
    ) + jnp.sum(down_recv.astype(jnp.float32), axis=0)
    hidden_out = layer_norm(
        normed_local.astype(jnp.float32) + down_sum + b_down, ln2_gain, ln2_shift
    ).astype(jnp.bfloat16)
    positions = tp_rank * row_share + jnp.arange(row_share, dtype=jnp.int32)
    is_valid = positions[None, :] < lengths[:, None]
    local_pool = jnp.sum(
        jnp.where(is_valid[:, :, None], hidden_out.astype(jnp.float32), jnp.float32(0.0)), axis=1
    )
    pooled = jnp.sum(direct_exchange(local_pool, ("tp",), 5), axis=0) / lengths.astype(
        jnp.float32
    )[:, None]
    query_vec = (
        pooled * lax.rsqrt(jnp.mean(pooled * pooled, axis=-1, keepdims=True) + norm_eps)
    ).astype(jnp.bfloat16)
    bundle = jnp.concatenate(
        [query_vec.astype(jnp.float32), text_ids.reshape(text_count, -1).astype(jnp.float32)], axis=1
    )
    bundle = direct_exchange(bundle, ("req",), 6).reshape(req_count * text_count, bundle.shape[1])
    all_queries = bundle[:, :model_width].astype(jnp.bfloat16)
    all_ids = bundle[:, model_width:].astype(jnp.int32)
    rows_here = index_rows.shape[0]
    first_row = (req_rank * tp_count + tp_rank) * rows_here
    local_ids = all_ids - first_row
    is_owned = (local_ids >= 0) & (local_ids < rows_here)
    safe_ids = jnp.clip(local_ids, 0, rows_here - 1)
    owned_count = jnp.sum(is_owned.astype(jnp.int32))

    def few_owned(_):
        flat_owned = is_owned.reshape(-1)
        (pair_at,) = jnp.nonzero(flat_owned, size=SPARSE_PAIRS, fill_value=0)
        valid = jnp.arange(SPARSE_PAIRS) < owned_count
        rows = jnp.take(index_rows, safe_ids.reshape(-1)[pair_at], axis=0)
        queries = jnp.take(all_queries, pair_at // all_ids.shape[1], axis=0)
        values = jnp.sum(rows.astype(jnp.float32) * queries.astype(jnp.float32), axis=-1)
        values = jnp.where(valid, values, jnp.float32(0.0))
        return (
            jnp.zeros(flat_owned.shape, jnp.float32).at[pair_at].add(values).reshape(all_ids.shape)
        )

    def many_owned(_):
        all_scores = jnp.einsum(
            "td,rd->tr", all_queries, index_rows, preferred_element_type=jnp.float32
        )
        score_rows = jnp.take(all_scores.T, safe_ids.reshape(-1), axis=0).reshape(
            safe_ids.shape[0], safe_ids.shape[1], safe_ids.shape[0]
        )
        picked = jnp.einsum("tct->tc", score_rows)
        return jnp.where(is_owned, picked, jnp.float32(0.0))

    owner_terms = lax.cond(owned_count <= SPARSE_PAIRS, few_owned, many_owned, None)
    owner_terms = (
        owner_terms.reshape(req_count, text_count, tp_count, quarter)
        .transpose(0, 2, 1, 3)
        .reshape(device_count, text_count, quarter)
    )
    scores = jnp.sum(lax.all_to_all(owner_terms, ("req", "tp"), 0, 0, tiled=True), axis=0)
    return (hidden_out, scores)


def solution(mesh):
    placed = (
        P("req", "tp", None),
        P("req"),
        P(None, None, "tp"),
        P(None, "tp"),
        P("tp", None),
        P(),
        P(),
        P(),
        P(None, "tp"),
        P("tp"),
        P("tp", None),
        P(),
        P(),
        P(),
        P(("req", "tp"), None),
        P("req", "tp"),
    )
    return jax.shard_map(
        per_device,
        mesh=mesh,
        in_specs=placed,
        out_specs=(P("req", "tp", None), P("req", "tp")),
        check_vma=False,
    )
```

```python
import functools
import jax
import jax.numpy as jnp
from jax import lax
from jax.experimental import pallas as pl
from jax.experimental.pallas import tpu as pltpu
from jax.sharding import PartitionSpec as P

MESH_ID = pl.DeviceIdType.MESH


def _ring_peers():
    n = lax.axis_size("tp")
    me = lax.axis_index("tp")
    rq = lax.axis_index("req")
    core = rq % 2
    right = (me + 1) % n
    left = (me + n - 1) % n
    opp = (me + 2) % n
    relay_to = (me + 1 + 2 * core) % n
    relay_from = (me + n - 1 - 2 * core) % n
    barrier = pltpu.get_barrier_semaphore()
    for peer in (left, right):
        pl.semaphore_signal(barrier, inc=1, device_id=(rq, peer), device_id_type=MESH_ID)
    pl.semaphore_wait(barrier, 2)
    return me, rq, core, right, left, opp, relay_to, relay_from


def _gather_kernel(chunks, x_ref, out_ref, send_sem, recv_sem, local_sem):
    me, rq, core, right, left, opp, relay_to, relay_from = _ring_peers()
    rows = x_ref.shape[1]
    step = rows // chunks

    def part(ref, k):
        return ref.at[:, pl.ds(k * step, step), :]

    def slot(src, k):
        return out_ref.at[:, pl.ds(src * rows + k * step, step), :]

    def copy(src, dst, send, recv, peer):
        return pltpu.make_async_remote_copy(
            src, dst, send, recv, device_id=(rq, peer), device_id_type=MESH_ID
        )

    local = pltpu.make_async_copy(x_ref, out_ref.at[:, pl.ds(me * rows, rows), :], local_sem)
    local.start()
    sends = []
    for k in range(chunks):
        to_right = copy(part(x_ref, k), slot(me, k), send_sem.at[0, k], recv_sem.at[0, k], right)
        to_left = copy(part(x_ref, k), slot(me, k), send_sem.at[1, k], recv_sem.at[1, k], left)
        to_right.start()
        to_left.start()
        sends += [to_right, to_left]
    for k in range(chunks):
        copy(part(x_ref, k), slot(relay_from, k), send_sem.at[2, k], recv_sem.at[core, k], right).wait_recv()
        forward = copy(
            slot(relay_from, k), slot(relay_from, k), send_sem.at[2, k], recv_sem.at[2, k], relay_to
        )
        forward.start()
        sends.append(forward)
    other_side = (me + 1 + 2 * (1 - core)) % lax.axis_size("tp")
    for k in range(chunks):
        copy(part(x_ref, k), slot(other_side, k), send_sem.at[0, k], recv_sem.at[1 - core, k], right).wait_recv()
    for k in range(chunks):
        copy(part(x_ref, k), slot(opp, k), send_sem.at[0, k], recv_sem.at[2, k], right).wait_recv()
    for c in sends:
        c.wait_send()
    local.wait()


def ring_all_gather(x, collective_id, chunks=1):
    texts, rows, width = x.shape
    n = lax.axis_size("tp")
    return pl.pallas_call(
        functools.partial(_gather_kernel, chunks),
        out_shape=jax.ShapeDtypeStruct((texts, n * rows, width), x.dtype),
        in_specs=[pl.BlockSpec(memory_space=pl.ANY)],
        out_specs=pl.BlockSpec(memory_space=pl.ANY),
        scratch_shapes=[
            pltpu.SemaphoreType.DMA((3, chunks)),
            pltpu.SemaphoreType.DMA((3, chunks)),
            pltpu.SemaphoreType.DMA,
        ],
        compiler_params=pltpu.CompilerParams(collective_id=collective_id, has_side_effects=True),
    )(x)


def _scatter_kernel(chunks, p_ref, recv_ref, relay_ref, send_sem, recv_sem, relay_sem):
    me, rq, core, right, left, opp, relay_to, relay_from = _ring_peers()
    rows = recv_ref.shape[2]
    step = rows // chunks

    def block(dst, k):
        return p_ref.at[:, pl.ds(dst * rows + k * step, step), :]

    def part(ref, k):
        return ref.at[:, pl.ds(k * step, step), :]

    def copy(src, dst, send, recv, peer):
        return pltpu.make_async_remote_copy(
            src, dst, send, recv, device_id=(rq, peer), device_id_type=MESH_ID
        )

    sends = []
    relays = []
    for k in range(chunks):
        to_relay = copy(block(opp, k), part(relay_ref, k), send_sem.at[2, k], relay_sem.at[k], relay_to)
        to_right = copy(block(right, k), part(recv_ref.at[0], k), send_sem.at[0, k], recv_sem.at[0, k], right)
        to_left = copy(block(left, k), part(recv_ref.at[1], k), send_sem.at[1, k], recv_sem.at[1, k], left)
        to_relay.start()
        to_right.start()
        to_left.start()
        sends += [to_relay, to_right, to_left]
        relays.append(to_relay)
    forwards = []
    for k in range(chunks):
        relays[k].wait_recv()
        forward = copy(
            part(relay_ref, k), part(recv_ref.at[2], k), send_sem.at[3, k], recv_sem.at[2, k], relay_to
        )
        forward.start()
        sends.append(forward)
        forwards.append(forward)
    for k in range(chunks):
        sends[3 * k + 1].wait_recv()
        sends[3 * k + 2].wait_recv()
        forwards[k].wait_recv()
    for c in sends:
        c.wait_send()


def ring_reduce_scatter(p, collective_id, chunks=1):
    texts, all_rows, width = p.shape
    n = lax.axis_size("tp")
    rows = all_rows // n
    recv, _ = pl.pallas_call(
        functools.partial(_scatter_kernel, chunks),
        out_shape=(
            jax.ShapeDtypeStruct((n - 1, texts, rows, width), p.dtype),
            jax.ShapeDtypeStruct((texts, rows, width), p.dtype),
        ),
        in_specs=[pl.BlockSpec(memory_space=pl.ANY)],
        out_specs=(pl.BlockSpec(memory_space=pl.ANY), pl.BlockSpec(memory_space=pl.ANY)),
        scratch_shapes=[
            pltpu.SemaphoreType.DMA((4, chunks)),
            pltpu.SemaphoreType.DMA((3, chunks)),
            pltpu.SemaphoreType.DMA((chunks,)),
        ],
        compiler_params=pltpu.CompilerParams(collective_id=collective_id, has_side_effects=True),
    )(p)
    return recv


def _peer_id(axes, peer):
    if axes == ("tp",):
        return (lax.axis_index("req"), peer)
    if axes == ("req",):
        return (peer, lax.axis_index("tp"))
    n_tp = lax.axis_size("tp")
    return (peer // n_tp, peer % n_tp)


def _direct_kernel(axes, scatter, x_ref, out_ref, send_sem, recv_sem, local_sem):
    n = out_ref.shape[0]
    me = lax.axis_index(axes)
    barrier = pltpu.get_barrier_semaphore()

    def greet(d, carry):
        peer = (me + d) % n
        pl.semaphore_signal(barrier, inc=1, device_id=_peer_id(axes, peer), device_id_type=MESH_ID)
        return carry

    lax.fori_loop(1, n, greet, 0)
    pl.semaphore_wait(barrier, n - 1)

    def source(peer):
        return x_ref.at[peer] if scatter else x_ref

    local = pltpu.make_async_copy(source(me), out_ref.at[me], local_sem)
    local.start()

    def send(d, carry):
        peer = (me + d) % n
        pltpu.make_async_remote_copy(
            source(peer), out_ref.at[me], send_sem.at[d], recv_sem.at[me],
            device_id=_peer_id(axes, peer), device_id_type=MESH_ID,
        ).start()
        return carry

    lax.fori_loop(1, n, send, 0)

    def receive(d, carry):
        src = (me + n - d) % n
        pltpu.make_async_remote_copy(
            source(src), out_ref.at[src], send_sem.at[d], recv_sem.at[src],
            device_id=_peer_id(axes, src), device_id_type=MESH_ID,
        ).wait_recv()
        return carry

    lax.fori_loop(1, n, receive, 0)

    def sent(d, carry):
        peer = (me + d) % n
        pltpu.make_async_remote_copy(
            source(peer), out_ref.at[me], send_sem.at[d], recv_sem.at[me],
            device_id=_peer_id(axes, peer), device_id_type=MESH_ID,
        ).wait_send()
        return carry

    lax.fori_loop(1, n, sent, 0)
    local.wait()


def direct_exchange(x, axes, collective_id, scatter=False):
    n = 1
    for name in axes:
        n *= lax.axis_size(name)
    block = x.shape[1:] if scatter else x.shape
    return pl.pallas_call(
        functools.partial(_direct_kernel, axes, scatter),
        out_shape=jax.ShapeDtypeStruct((n,) + block, x.dtype),
        in_specs=[pl.BlockSpec(memory_space=pl.ANY)],
        out_specs=pl.BlockSpec(memory_space=pl.ANY),
        scratch_shapes=[
            pltpu.SemaphoreType.DMA((n,)),
            pltpu.SemaphoreType.DMA((n,)),
            pltpu.SemaphoreType.DMA,
        ],
        compiler_params=pltpu.CompilerParams(collective_id=collective_id, has_side_effects=True),
    )(x)


HEAD_DIM = 64
RING_CHUNKS = 4
SPARSE_PAIRS = 128
WINDOW = 512


layer_eps = 1e-05
norm_eps = 1e-06


def layer_norm(values, gain, shift):
    centre = values - jnp.mean(values, axis=-1, keepdims=True)
    spread = jnp.mean(centre * centre, axis=-1, keepdims=True)
    return centre * lax.rsqrt(spread + layer_eps) * gain + shift


def window_attention(queries_h, keys_h, values_h, lengths):
    seq_len = queries_h.shape[1]
    half_window = WINDOW // 2
    scale_factor = HEAD_DIM ** (-0.5)
    pos = jnp.arange(seq_len, dtype=jnp.int32)
    near = jnp.abs(pos[:, None] - pos[None, :]) <= half_window
    keep_mask = near[None] & (pos[None, None, :] < lengths[:, None, None])
    logits = (
        jnp.einsum("tqhe,tkhe->thqk", queries_h, keys_h, preferred_element_type=jnp.float32)
        * scale_factor
    )
    logits = jnp.where(keep_mask[:, None], logits, jnp.float32(-1e30))
    top_val = jnp.max(logits, axis=-1, keepdims=True)
    expo = jnp.exp(logits - top_val)
    attn_weights = (expo / jnp.sum(expo, axis=-1, keepdims=True)).astype(jnp.bfloat16)
    context = jnp.einsum(
        "thqk,tkhe->tqhe", attn_weights, values_h, preferred_element_type=jnp.float32
    )
    context = jnp.where(
        (pos[None, :] < lengths[:, None])[:, :, None, None], context, jnp.float32(0.0)
    )
    return context.astype(jnp.bfloat16).reshape(
        queries_h.shape[0], seq_len, queries_h.shape[2] * HEAD_DIM
    )


def per_device(
    states,
    lengths,
    w_qkv,
    b_qkv,
    w_out,
    b_out,
    ln1_gain,
    ln1_shift,
    w_up,
    b_up,
    w_down,
    b_down,
    ln2_gain,
    ln2_shift,
    index_rows,
    cand_ids,
):
    tp_count = lax.axis_size("tp")
    tp_rank = lax.axis_index("tp")
    req_count = lax.axis_size("req")
    req_rank = lax.axis_index("req")
    text_count, row_share, model_width = states.shape
    quarter = cand_ids.shape[1]
    full_states = ring_all_gather(states, 0, RING_CHUNKS)
    device_count = req_count * tp_count
    text_ids = jnp.swapaxes(direct_exchange(cand_ids, ("tp",), 4), 0, 1)
    seq_len = full_states.shape[1]
    local_width = w_qkv.shape[2]
    heads_here = local_width // HEAD_DIM
    projected = (
        jnp.einsum("tsd,dce->tsce", full_states, w_qkv, preferred_element_type=jnp.float32) + b_qkv
    ).astype(jnp.bfloat16)
    queries_h = projected[:, :, 0].reshape(text_count, seq_len, heads_here, HEAD_DIM)
    keys_h = projected[:, :, 1].reshape(text_count, seq_len, heads_here, HEAD_DIM)
    values_h = projected[:, :, 2].reshape(text_count, seq_len, heads_here, HEAD_DIM)

    context = window_attention(queries_h, keys_h, values_h, lengths)
    partial_value = jnp.einsum("tsk,kd->tsd", context, w_out, preferred_element_type=jnp.float32)
    partial_value = partial_value.astype(jnp.bfloat16)
    attn_recv = ring_reduce_scatter(partial_value, 1, RING_CHUNKS)
    attn_sum = lax.dynamic_slice_in_dim(partial_value, tp_rank * row_share, row_share, 1).astype(
        jnp.float32
    ) + jnp.sum(attn_recv.astype(jnp.float32), axis=0)
    normed_local = layer_norm(
        states.astype(jnp.float32) + attn_sum + b_out, ln1_gain, ln1_shift
    ).astype(jnp.bfloat16)
    normed_full = ring_all_gather(normed_local, 2, RING_CHUNKS)
    up_act = jax.nn.gelu(
        jnp.einsum("tsd,df->tsf", normed_full, w_up, preferred_element_type=jnp.float32) + b_up,
        approximate=False,
    ).astype(jnp.bfloat16)
    down_part = jnp.einsum(
        "tsf,fd->tsd", up_act, w_down, preferred_element_type=jnp.float32
    ).astype(jnp.bfloat16)
    down_recv = ring_reduce_scatter(down_part, 3, RING_CHUNKS)
    down_sum = lax.dynamic_slice_in_dim(down_part, tp_rank * row_share, row_share, 1).astype(
        jnp.float32
    ) + jnp.sum(down_recv.astype(jnp.float32), axis=0)
    hidden_out = layer_norm(
        normed_local.astype(jnp.float32) + down_sum + b_down, ln2_gain, ln2_shift
    ).astype(jnp.bfloat16)
    positions = tp_rank * row_share + jnp.arange(row_share, dtype=jnp.int32)
    is_valid = positions[None, :] < lengths[:, None]
    local_pool = jnp.sum(
        jnp.where(is_valid[:, :, None], hidden_out.astype(jnp.float32), jnp.float32(0.0)), axis=1
    )
    pooled = jnp.sum(direct_exchange(local_pool, ("tp",), 5), axis=0) / lengths.astype(
        jnp.float32
    )[:, None]
    query_vec = (
        pooled * lax.rsqrt(jnp.mean(pooled * pooled, axis=-1, keepdims=True) + norm_eps)
    ).astype(jnp.bfloat16)
    bundle = jnp.concatenate(
        [query_vec.astype(jnp.float32), text_ids.reshape(text_count, -1).astype(jnp.float32)], axis=1
    )
    bundle = direct_exchange(bundle, ("req",), 6).reshape(req_count * text_count, bundle.shape[1])
    all_queries = bundle[:, :model_width].astype(jnp.bfloat16)
    all_ids = bundle[:, model_width:].astype(jnp.int32)
    rows_here = index_rows.shape[0]
    first_row = (req_rank * tp_count + tp_rank) * rows_here
    local_ids = all_ids - first_row
    is_owned = (local_ids >= 0) & (local_ids < rows_here)
    safe_ids = jnp.clip(local_ids, 0, rows_here - 1)
    owned_count = jnp.sum(is_owned.astype(jnp.int32))

    def few_owned(_):
        flat_owned = is_owned.reshape(-1)
        owned_int = is_owned.astype(jnp.int32)
        row_counts = jnp.cumsum(owned_int, axis=1)
        row_totals = row_counts[:, -1]
        running = (row_counts + (jnp.cumsum(row_totals) - row_totals)[:, None]).reshape(-1)
        rank = jnp.arange(SPARSE_PAIRS, dtype=jnp.int32)
        chosen = flat_owned[None, :] & (running[None, :] == rank[:, None] + 1)
        pair_index = jnp.arange(flat_owned.shape[0], dtype=jnp.int32)
        pair_at = jnp.sum(jnp.where(chosen, pair_index[None, :], 0), axis=1)
        rows = jnp.take(index_rows, safe_ids.reshape(-1)[pair_at], axis=0)
        queries = jnp.take(all_queries, pair_at // all_ids.shape[1], axis=0)
        values = jnp.sum(rows.astype(jnp.float32) * queries.astype(jnp.float32), axis=-1)
        return jnp.sum(
            jnp.where(chosen, values[:, None], jnp.float32(0.0)), axis=0
        ).reshape(all_ids.shape)

    def many_owned(_):
        all_scores = jnp.einsum(
            "td,rd->tr", all_queries, index_rows, preferred_element_type=jnp.float32
        )
        score_rows = jnp.take(all_scores.T, safe_ids.reshape(-1), axis=0).reshape(
            safe_ids.shape[0], safe_ids.shape[1], safe_ids.shape[0]
        )
        picked = jnp.einsum("tct->tc", score_rows)
        return jnp.where(is_owned, picked, jnp.float32(0.0))

    owner_terms = lax.cond(owned_count <= SPARSE_PAIRS, few_owned, many_owned, None)
    owner_terms = (
        owner_terms.reshape(req_count, text_count, tp_count, quarter)
        .transpose(0, 2, 1, 3)
        .reshape(device_count, text_count, quarter)
    )
    scores = jnp.sum(lax.all_to_all(owner_terms, ("req", "tp"), 0, 0, tiled=True), axis=0)
    return (hidden_out, scores)


def solution(mesh):
    placed = (
        P("req", "tp", None),
        P("req"),
        P(None, None, "tp"),
        P(None, "tp"),
        P("tp", None),
        P(),
        P(),
        P(),
        P(None, "tp"),
        P("tp"),
        P("tp", None),
        P(),
        P(),
        P(),
        P(("req", "tp"), None),
        P("req", "tp"),
    )
    return jax.shard_map(
        per_device,
        mesh=mesh,
        in_specs=placed,
        out_specs=(P("req", "tp", None), P("req", "tp")),
        check_vma=False,
    )
```

```python
import functools
import jax
import jax.numpy as jnp
from jax import lax
from jax.experimental import pallas as pl
from jax.experimental.pallas import tpu as pltpu
from jax.sharding import PartitionSpec as P

MESH_ID = pl.DeviceIdType.MESH


def _ring_peers():
    n = lax.axis_size("tp")
    me = lax.axis_index("tp")
    rq = lax.axis_index("req")
    core = rq % 2
    right = (me + 1) % n
    left = (me + n - 1) % n
    opp = (me + 2) % n
    relay_to = (me + 1 + 2 * core) % n
    relay_from = (me + n - 1 - 2 * core) % n
    barrier = pltpu.get_barrier_semaphore()
    for peer in (left, right):
        pl.semaphore_signal(barrier, inc=1, device_id=(rq, peer), device_id_type=MESH_ID)
    pl.semaphore_wait(barrier, 2)
    return me, rq, core, right, left, opp, relay_to, relay_from


def _gather_kernel(chunks, x_ref, out_ref, send_sem, recv_sem, local_sem):
    me, rq, core, right, left, opp, relay_to, relay_from = _ring_peers()
    rows = x_ref.shape[1]
    step = rows // chunks

    def part(ref, k):
        return ref.at[:, pl.ds(k * step, step), :]

    def slot(src, k):
        return out_ref.at[:, pl.ds(src * rows + k * step, step), :]

    def copy(src, dst, send, recv, peer):
        return pltpu.make_async_remote_copy(
            src, dst, send, recv, device_id=(rq, peer), device_id_type=MESH_ID
        )

    local = pltpu.make_async_copy(x_ref, out_ref.at[:, pl.ds(me * rows, rows), :], local_sem)
    local.start()
    sends = []
    for k in range(chunks):
        to_right = copy(part(x_ref, k), slot(me, k), send_sem.at[0, k], recv_sem.at[0, k], right)
        to_left = copy(part(x_ref, k), slot(me, k), send_sem.at[1, k], recv_sem.at[1, k], left)
        to_right.start()
        to_left.start()
        sends += [to_right, to_left]
    for k in range(chunks):
        copy(part(x_ref, k), slot(relay_from, k), send_sem.at[2, k], recv_sem.at[core, k], right).wait_recv()
        forward = copy(
            slot(relay_from, k), slot(relay_from, k), send_sem.at[2, k], recv_sem.at[2, k], relay_to
        )
        forward.start()
        sends.append(forward)
    other_side = (me + 1 + 2 * (1 - core)) % lax.axis_size("tp")
    for k in range(chunks):
        copy(part(x_ref, k), slot(other_side, k), send_sem.at[0, k], recv_sem.at[1 - core, k], right).wait_recv()
    for k in range(chunks):
        copy(part(x_ref, k), slot(opp, k), send_sem.at[0, k], recv_sem.at[2, k], right).wait_recv()
    for c in sends:
        c.wait_send()
    local.wait()


def ring_all_gather(x, collective_id, chunks=1):
    texts, rows, width = x.shape
    n = lax.axis_size("tp")
    return pl.pallas_call(
        functools.partial(_gather_kernel, chunks),
        out_shape=jax.ShapeDtypeStruct((texts, n * rows, width), x.dtype),
        in_specs=[pl.BlockSpec(memory_space=pl.ANY)],
        out_specs=pl.BlockSpec(memory_space=pl.ANY),
        scratch_shapes=[
            pltpu.SemaphoreType.DMA((3, chunks)),
            pltpu.SemaphoreType.DMA((3, chunks)),
            pltpu.SemaphoreType.DMA,
        ],
        compiler_params=pltpu.CompilerParams(collective_id=collective_id, has_side_effects=True),
    )(x)


def _scatter_kernel(chunks, p_ref, recv_ref, relay_ref, send_sem, recv_sem, relay_sem):
    me, rq, core, right, left, opp, relay_to, relay_from = _ring_peers()
    rows = recv_ref.shape[2]
    step = rows // chunks

    def block(dst, k):
        return p_ref.at[:, pl.ds(dst * rows + k * step, step), :]

    def part(ref, k):
        return ref.at[:, pl.ds(k * step, step), :]

    def copy(src, dst, send, recv, peer):
        return pltpu.make_async_remote_copy(
            src, dst, send, recv, device_id=(rq, peer), device_id_type=MESH_ID
        )

    sends = []
    relays = []
    for k in range(chunks):
        to_relay = copy(block(opp, k), part(relay_ref, k), send_sem.at[2, k], relay_sem.at[k], relay_to)
        to_right = copy(block(right, k), part(recv_ref.at[0], k), send_sem.at[0, k], recv_sem.at[0, k], right)
        to_left = copy(block(left, k), part(recv_ref.at[1], k), send_sem.at[1, k], recv_sem.at[1, k], left)
        to_relay.start()
        to_right.start()
        to_left.start()
        sends += [to_relay, to_right, to_left]
        relays.append(to_relay)
    forwards = []
    for k in range(chunks):
        relays[k].wait_recv()
        forward = copy(
            part(relay_ref, k), part(recv_ref.at[2], k), send_sem.at[3, k], recv_sem.at[2, k], relay_to
        )
        forward.start()
        sends.append(forward)
        forwards.append(forward)
    for k in range(chunks):
        sends[3 * k + 1].wait_recv()
        sends[3 * k + 2].wait_recv()
        forwards[k].wait_recv()
    for c in sends:
        c.wait_send()


def ring_reduce_scatter(p, collective_id, chunks=1):
    texts, all_rows, width = p.shape
    n = lax.axis_size("tp")
    rows = all_rows // n
    recv, _ = pl.pallas_call(
        functools.partial(_scatter_kernel, chunks),
        out_shape=(
            jax.ShapeDtypeStruct((n - 1, texts, rows, width), p.dtype),
            jax.ShapeDtypeStruct((texts, rows, width), p.dtype),
        ),
        in_specs=[pl.BlockSpec(memory_space=pl.ANY)],
        out_specs=(pl.BlockSpec(memory_space=pl.ANY), pl.BlockSpec(memory_space=pl.ANY)),
        scratch_shapes=[
            pltpu.SemaphoreType.DMA((4, chunks)),
            pltpu.SemaphoreType.DMA((3, chunks)),
            pltpu.SemaphoreType.DMA((chunks,)),
        ],
        compiler_params=pltpu.CompilerParams(collective_id=collective_id, has_side_effects=True),
    )(p)
    return recv


def _peer_id(axes, peer):
    if axes == ("tp",):
        return (lax.axis_index("req"), peer)
    if axes == ("req",):
        return (peer, lax.axis_index("tp"))
    n_tp = lax.axis_size("tp")
    return (peer // n_tp, peer % n_tp)


def _direct_kernel(axes, scatter, x_ref, out_ref, send_sem, recv_sem, local_sem):
    n = out_ref.shape[0]
    me = lax.axis_index(axes)
    barrier = pltpu.get_barrier_semaphore()

    def greet(d, carry):
        peer = (me + d) % n
        pl.semaphore_signal(barrier, inc=1, device_id=_peer_id(axes, peer), device_id_type=MESH_ID)
        return carry

    lax.fori_loop(1, n, greet, 0)
    pl.semaphore_wait(barrier, n - 1)

    def source(peer):
        return x_ref.at[peer] if scatter else x_ref

    local = pltpu.make_async_copy(source(me), out_ref.at[me], local_sem)
    local.start()

    def send(d, carry):
        peer = (me + d) % n
        pltpu.make_async_remote_copy(
            source(peer), out_ref.at[me], send_sem.at[d], recv_sem.at[me],
            device_id=_peer_id(axes, peer), device_id_type=MESH_ID,
        ).start()
        return carry

    lax.fori_loop(1, n, send, 0)

    def receive(d, carry):
        src = (me + n - d) % n
        pltpu.make_async_remote_copy(
            source(src), out_ref.at[src], send_sem.at[d], recv_sem.at[src],
            device_id=_peer_id(axes, src), device_id_type=MESH_ID,
        ).wait_recv()
        return carry

    lax.fori_loop(1, n, receive, 0)

    def sent(d, carry):
        peer = (me + d) % n
        pltpu.make_async_remote_copy(
            source(peer), out_ref.at[me], send_sem.at[d], recv_sem.at[me],
            device_id=_peer_id(axes, peer), device_id_type=MESH_ID,
        ).wait_send()
        return carry

    lax.fori_loop(1, n, sent, 0)
    local.wait()


def direct_exchange(x, axes, collective_id, scatter=False):
    n = 1
    for name in axes:
        n *= lax.axis_size(name)
    block = x.shape[1:] if scatter else x.shape
    return pl.pallas_call(
        functools.partial(_direct_kernel, axes, scatter),
        out_shape=jax.ShapeDtypeStruct((n,) + block, x.dtype),
        in_specs=[pl.BlockSpec(memory_space=pl.ANY)],
        out_specs=pl.BlockSpec(memory_space=pl.ANY),
        scratch_shapes=[
            pltpu.SemaphoreType.DMA((n,)),
            pltpu.SemaphoreType.DMA((n,)),
            pltpu.SemaphoreType.DMA,
        ],
        compiler_params=pltpu.CompilerParams(collective_id=collective_id, has_side_effects=True),
    )(x)


HEAD_DIM = 64
RING_CHUNKS = 4
SPARSE_PAIRS = 128
WINDOW = 512


layer_eps = 1e-05
norm_eps = 1e-06


def layer_norm(values, gain, shift):
    centre = values - jnp.mean(values, axis=-1, keepdims=True)
    spread = jnp.mean(centre * centre, axis=-1, keepdims=True)
    return centre * lax.rsqrt(spread + layer_eps) * gain + shift


def window_attention(queries_h, keys_h, values_h, lengths):
    seq_len = queries_h.shape[1]
    half_window = WINDOW // 2
    scale_factor = HEAD_DIM ** (-0.5)
    pos = jnp.arange(seq_len, dtype=jnp.int32)
    near = jnp.abs(pos[:, None] - pos[None, :]) <= half_window
    keep_mask = near[None] & (pos[None, None, :] < lengths[:, None, None])
    logits = (
        jnp.einsum("tqhe,tkhe->thqk", queries_h, keys_h, preferred_element_type=jnp.float32)
        * scale_factor
    )
    logits = jnp.where(keep_mask[:, None], logits, jnp.float32(-1e30))
    top_val = jnp.max(logits, axis=-1, keepdims=True)
    expo = jnp.exp(logits - top_val)
    attn_weights = (expo / jnp.sum(expo, axis=-1, keepdims=True)).astype(jnp.bfloat16)
    context = jnp.einsum(
        "thqk,tkhe->tqhe", attn_weights, values_h, preferred_element_type=jnp.float32
    )
    context = jnp.where(
        (pos[None, :] < lengths[:, None])[:, :, None, None], context, jnp.float32(0.0)
    )
    return context.astype(jnp.bfloat16).reshape(
        queries_h.shape[0], seq_len, queries_h.shape[2] * HEAD_DIM
    )


def per_device(
    states,
    lengths,
    w_qkv,
    b_qkv,
    w_out,
    b_out,
    ln1_gain,
    ln1_shift,
    w_up,
    b_up,
    w_down,
    b_down,
    ln2_gain,
    ln2_shift,
    index_rows,
    cand_ids,
):
    tp_count = lax.axis_size("tp")
    tp_rank = lax.axis_index("tp")
    req_count = lax.axis_size("req")
    req_rank = lax.axis_index("req")
    text_count, row_share, model_width = states.shape
    quarter = cand_ids.shape[1]
    full_states = ring_all_gather(states, 0, RING_CHUNKS)
    device_count = req_count * tp_count
    seq_len = full_states.shape[1]
    local_width = w_qkv.shape[2]
    heads_here = local_width // HEAD_DIM
    projected = (
        jnp.einsum("tsd,dce->tsce", full_states, w_qkv, preferred_element_type=jnp.float32) + b_qkv
    ).astype(jnp.bfloat16)
    queries_h = projected[:, :, 0].reshape(text_count, seq_len, heads_here, HEAD_DIM)
    keys_h = projected[:, :, 1].reshape(text_count, seq_len, heads_here, HEAD_DIM)
    values_h = projected[:, :, 2].reshape(text_count, seq_len, heads_here, HEAD_DIM)

    context = window_attention(queries_h, keys_h, values_h, lengths)
    partial_value = jnp.einsum("tsk,kd->tsd", context, w_out, preferred_element_type=jnp.float32)
    partial_value = partial_value.astype(jnp.bfloat16)
    attn_recv = ring_reduce_scatter(partial_value, 1, RING_CHUNKS)
    attn_sum = lax.dynamic_slice_in_dim(partial_value, tp_rank * row_share, row_share, 1).astype(
        jnp.float32
    ) + jnp.sum(attn_recv.astype(jnp.float32), axis=0)
    normed_local = layer_norm(
        states.astype(jnp.float32) + attn_sum + b_out, ln1_gain, ln1_shift
    ).astype(jnp.bfloat16)
    normed_full = ring_all_gather(normed_local, 2, RING_CHUNKS)
    up_act = jax.nn.gelu(
        jnp.einsum("tsd,df->tsf", normed_full, w_up, preferred_element_type=jnp.float32) + b_up,
        approximate=False,
    ).astype(jnp.bfloat16)
    down_part = jnp.einsum(
        "tsf,fd->tsd", up_act, w_down, preferred_element_type=jnp.float32
    ).astype(jnp.bfloat16)
    down_recv = ring_reduce_scatter(down_part, 3, RING_CHUNKS)
    down_sum = lax.dynamic_slice_in_dim(down_part, tp_rank * row_share, row_share, 1).astype(
        jnp.float32
    ) + jnp.sum(down_recv.astype(jnp.float32), axis=0)
    hidden_out = layer_norm(
        normed_local.astype(jnp.float32) + down_sum + b_down, ln2_gain, ln2_shift
    ).astype(jnp.bfloat16)
    positions = tp_rank * row_share + jnp.arange(row_share, dtype=jnp.int32)
    is_valid = positions[None, :] < lengths[:, None]
    local_pool = jnp.sum(
        jnp.where(is_valid[:, :, None], hidden_out.astype(jnp.float32), jnp.float32(0.0)), axis=1
    )
    pool_and_ids = direct_exchange(
        jnp.concatenate([local_pool, cand_ids.astype(jnp.float32)], axis=1), ("tp",), 5
    )
    text_ids = jnp.swapaxes(pool_and_ids[:, :, model_width:], 0, 1)
    pooled = jnp.sum(pool_and_ids[:, :, :model_width], axis=0) / lengths.astype(
        jnp.float32
    )[:, None]
    query_vec = (
        pooled * lax.rsqrt(jnp.mean(pooled * pooled, axis=-1, keepdims=True) + norm_eps)
    ).astype(jnp.bfloat16)
    bundle = jnp.concatenate(
        [query_vec.astype(jnp.float32), text_ids.reshape(text_count, -1)], axis=1
    )
    bundle = direct_exchange(bundle, ("req",), 6).reshape(req_count * text_count, bundle.shape[1])
    all_queries = bundle[:, :model_width].astype(jnp.bfloat16)
    all_ids = bundle[:, model_width:].astype(jnp.int32)
    rows_here = index_rows.shape[0]
    first_row = (req_rank * tp_count + tp_rank) * rows_here
    local_ids = all_ids - first_row
    is_owned = (local_ids >= 0) & (local_ids < rows_here)
    safe_ids = jnp.clip(local_ids, 0, rows_here - 1)
    owned_count = jnp.sum(is_owned.astype(jnp.int32))

    def few_owned(_):
        flat_owned = is_owned.reshape(-1)
        owned_int = is_owned.astype(jnp.int32)
        row_counts = jnp.cumsum(owned_int, axis=1)
        row_totals = row_counts[:, -1]
        running = (row_counts + (jnp.cumsum(row_totals) - row_totals)[:, None]).reshape(-1)
        rank = jnp.arange(SPARSE_PAIRS, dtype=jnp.int32)
        chosen = flat_owned[None, :] & (running[None, :] == rank[:, None] + 1)
        pair_index = jnp.arange(flat_owned.shape[0], dtype=jnp.int32)
        pair_at = jnp.sum(jnp.where(chosen, pair_index[None, :], 0), axis=1)
        rows = jnp.take(index_rows, safe_ids.reshape(-1)[pair_at], axis=0)
        queries = jnp.take(all_queries, pair_at // all_ids.shape[1], axis=0)
        values = jnp.sum(rows.astype(jnp.float32) * queries.astype(jnp.float32), axis=-1)
        return jnp.sum(
            jnp.where(chosen, values[:, None], jnp.float32(0.0)), axis=0
        ).reshape(all_ids.shape)

    def many_owned(_):
        all_scores = jnp.einsum(
            "td,rd->tr", all_queries, index_rows, preferred_element_type=jnp.float32
        )
        score_rows = jnp.take(all_scores.T, safe_ids.reshape(-1), axis=0).reshape(
            safe_ids.shape[0], safe_ids.shape[1], safe_ids.shape[0]
        )
        picked = jnp.einsum("tct->tc", score_rows)
        return jnp.where(is_owned, picked, jnp.float32(0.0))

    owner_terms = lax.cond(owned_count <= SPARSE_PAIRS, few_owned, many_owned, None)
    owner_terms = (
        owner_terms.reshape(req_count, text_count, tp_count, quarter)
        .transpose(0, 2, 1, 3)
        .reshape(device_count, text_count, quarter)
    )
    scores = jnp.sum(lax.all_to_all(owner_terms, ("req", "tp"), 0, 0, tiled=True), axis=0)
    return (hidden_out, scores)


def solution(mesh):
    placed = (
        P("req", "tp", None),
        P("req"),
        P(None, None, "tp"),
        P(None, "tp"),
        P("tp", None),
        P(),
        P(),
        P(),
        P(None, "tp"),
        P("tp"),
        P("tp", None),
        P(),
        P(),
        P(),
        P(("req", "tp"), None),
        P("req", "tp"),
    )
    return jax.shard_map(
        per_device,
        mesh=mesh,
        in_specs=placed,
        out_specs=(P("req", "tp", None), P("req", "tp")),
        check_vma=False,
    )
```

```python
import functools
import jax
import jax.numpy as jnp
from jax import lax
from jax.experimental import pallas as pl
from jax.experimental.pallas import tpu as pltpu
from jax.sharding import PartitionSpec as P

MESH_ID = pl.DeviceIdType.MESH


def _ring_peers():
    n = lax.axis_size("tp")
    me = lax.axis_index("tp")
    rq = lax.axis_index("req")
    core = rq % 2
    right = (me + 1) % n
    left = (me + n - 1) % n
    opp = (me + 2) % n
    relay_to = (me + 1 + 2 * core) % n
    relay_from = (me + n - 1 - 2 * core) % n
    barrier = pltpu.get_barrier_semaphore()
    for peer in (left, right):
        pl.semaphore_signal(barrier, inc=1, device_id=(rq, peer), device_id_type=MESH_ID)
    pl.semaphore_wait(barrier, 2)
    return me, rq, core, right, left, opp, relay_to, relay_from


def _gather_kernel(chunks, x_ref, out_ref, send_sem, recv_sem, local_sem):
    me, rq, core, right, left, opp, relay_to, relay_from = _ring_peers()
    rows = x_ref.shape[1]
    step = rows // chunks

    def part(ref, k):
        return ref.at[:, pl.ds(k * step, step), :]

    def slot(src, k):
        return out_ref.at[:, pl.ds(src * rows + k * step, step), :]

    def copy(src, dst, send, recv, peer):
        return pltpu.make_async_remote_copy(
            src, dst, send, recv, device_id=(rq, peer), device_id_type=MESH_ID
        )

    local = pltpu.make_async_copy(x_ref, out_ref.at[:, pl.ds(me * rows, rows), :], local_sem)
    local.start()
    sends = []
    for k in range(chunks):
        to_right = copy(part(x_ref, k), slot(me, k), send_sem.at[0, k], recv_sem.at[0, k], right)
        to_left = copy(part(x_ref, k), slot(me, k), send_sem.at[1, k], recv_sem.at[1, k], left)
        to_right.start()
        to_left.start()
        sends += [to_right, to_left]
    for k in range(chunks):
        copy(part(x_ref, k), slot(relay_from, k), send_sem.at[2, k], recv_sem.at[core, k], right).wait_recv()
        forward = copy(
            slot(relay_from, k), slot(relay_from, k), send_sem.at[2, k], recv_sem.at[2, k], relay_to
        )
        forward.start()
        sends.append(forward)
    other_side = (me + 1 + 2 * (1 - core)) % lax.axis_size("tp")
    for k in range(chunks):
        copy(part(x_ref, k), slot(other_side, k), send_sem.at[0, k], recv_sem.at[1 - core, k], right).wait_recv()
    for k in range(chunks):
        copy(part(x_ref, k), slot(opp, k), send_sem.at[0, k], recv_sem.at[2, k], right).wait_recv()
    for c in sends:
        c.wait_send()
    local.wait()


def ring_all_gather(x, collective_id, chunks=1):
    texts, rows, width = x.shape
    n = lax.axis_size("tp")
    return pl.pallas_call(
        functools.partial(_gather_kernel, chunks),
        out_shape=jax.ShapeDtypeStruct((texts, n * rows, width), x.dtype),
        in_specs=[pl.BlockSpec(memory_space=pl.ANY)],
        out_specs=pl.BlockSpec(memory_space=pl.ANY),
        scratch_shapes=[
            pltpu.SemaphoreType.DMA((3, chunks)),
            pltpu.SemaphoreType.DMA((3, chunks)),
            pltpu.SemaphoreType.DMA,
        ],
        compiler_params=pltpu.CompilerParams(collective_id=collective_id, has_side_effects=True),
    )(x)


def _scatter_add_kernel(chunks, p_ref, recv_ref, send_sem, recv_sem, relay_sem, local_sem,
                        own_buf, relay_buf, sum_buf):
    me, rq, core, right, left, opp, relay_to, relay_from = _ring_peers()
    rows = recv_ref.shape[2]
    step = rows // chunks

    def block(dst, k):
        return p_ref.at[:, pl.ds(dst * rows + k * step, step), :]

    def part(ref, k):
        return ref.at[:, pl.ds(k * step, step), :]

    def copy(src, dst, send, recv, peer):
        return pltpu.make_async_remote_copy(
            src, dst, send, recv, device_id=(rq, peer), device_id_type=MESH_ID
        )

    sends = []
    loads = []
    for k in range(chunks):
        to_relay = copy(block(opp, k), relay_buf.at[k], send_sem.at[0, k], relay_sem.at[k], relay_to)
        to_other = copy(
            block(relay_from, k), part(recv_ref.at[1], k), send_sem.at[1, k], recv_sem.at[1, k], relay_from
        )
        to_relay.start()
        to_other.start()
        load = pltpu.make_async_copy(block(relay_to, k), own_buf.at[k], local_sem.at[k])
        load.start()
        sends += [to_relay, to_other]
        loads.append(load)
    forwards = []
    for k in range(chunks):
        sends[2 * k].wait_recv()
        loads[k].wait()
        sum_buf[k] = (
            own_buf[k].astype(jnp.float32) + relay_buf[k].astype(jnp.float32)
        ).astype(sum_buf.dtype)
        forward = copy(sum_buf.at[k], part(recv_ref.at[0], k), send_sem.at[2, k], recv_sem.at[0, k], relay_to)
        forward.start()
        forwards.append(forward)
    for k in range(chunks):
        sends[2 * k + 1].wait_recv()
        forwards[k].wait_recv()
    for c in sends + forwards:
        c.wait_send()


def ring_reduce_scatter_add(p, collective_id, chunks=1):
    texts, all_rows, width = p.shape
    n = lax.axis_size("tp")
    rows = all_rows // n
    step = rows // chunks
    buf = pltpu.VMEM((chunks, texts, step, width), p.dtype)
    return pl.pallas_call(
        functools.partial(_scatter_add_kernel, chunks),
        out_shape=jax.ShapeDtypeStruct((2, texts, rows, width), p.dtype),
        in_specs=[pl.BlockSpec(memory_space=pl.ANY)],
        out_specs=pl.BlockSpec(memory_space=pl.ANY),
        scratch_shapes=[
            pltpu.SemaphoreType.DMA((3, chunks)),
            pltpu.SemaphoreType.DMA((2, chunks)),
            pltpu.SemaphoreType.DMA((chunks,)),
            pltpu.SemaphoreType.DMA((chunks,)),
            buf,
            buf,
            buf,
        ],
        compiler_params=pltpu.CompilerParams(collective_id=collective_id, has_side_effects=True),
    )(p)


def _peer_id(axes, peer):
    if axes == ("tp",):
        return (lax.axis_index("req"), peer)
    if axes == ("req",):
        return (peer, lax.axis_index("tp"))
    n_tp = lax.axis_size("tp")
    return (peer // n_tp, peer % n_tp)


def _direct_kernel(axes, scatter, x_ref, out_ref, send_sem, recv_sem, local_sem):
    n = out_ref.shape[0]
    me = lax.axis_index(axes)
    barrier = pltpu.get_barrier_semaphore()

    def greet(d, carry):
        peer = (me + d) % n
        pl.semaphore_signal(barrier, inc=1, device_id=_peer_id(axes, peer), device_id_type=MESH_ID)
        return carry

    lax.fori_loop(1, n, greet, 0)
    pl.semaphore_wait(barrier, n - 1)

    def source(peer):
        return x_ref.at[peer] if scatter else x_ref

    local = pltpu.make_async_copy(source(me), out_ref.at[me], local_sem)
    local.start()

    def send(d, carry):
        peer = (me + d) % n
        pltpu.make_async_remote_copy(
            source(peer), out_ref.at[me], send_sem.at[d], recv_sem.at[me],
            device_id=_peer_id(axes, peer), device_id_type=MESH_ID,
        ).start()
        return carry

    lax.fori_loop(1, n, send, 0)

    def receive(d, carry):
        src = (me + n - d) % n
        pltpu.make_async_remote_copy(
            source(src), out_ref.at[src], send_sem.at[d], recv_sem.at[src],
            device_id=_peer_id(axes, src), device_id_type=MESH_ID,
        ).wait_recv()
        return carry

    lax.fori_loop(1, n, receive, 0)

    def sent(d, carry):
        peer = (me + d) % n
        pltpu.make_async_remote_copy(
            source(peer), out_ref.at[me], send_sem.at[d], recv_sem.at[me],
            device_id=_peer_id(axes, peer), device_id_type=MESH_ID,
        ).wait_send()
        return carry

    lax.fori_loop(1, n, sent, 0)
    local.wait()


def direct_exchange(x, axes, collective_id, scatter=False):
    n = 1
    for name in axes:
        n *= lax.axis_size(name)
    block = x.shape[1:] if scatter else x.shape
    return pl.pallas_call(
        functools.partial(_direct_kernel, axes, scatter),
        out_shape=jax.ShapeDtypeStruct((n,) + block, x.dtype),
        in_specs=[pl.BlockSpec(memory_space=pl.ANY)],
        out_specs=pl.BlockSpec(memory_space=pl.ANY),
        scratch_shapes=[
            pltpu.SemaphoreType.DMA((n,)),
            pltpu.SemaphoreType.DMA((n,)),
            pltpu.SemaphoreType.DMA,
        ],
        compiler_params=pltpu.CompilerParams(collective_id=collective_id, has_side_effects=True),
    )(x)


HEAD_DIM = 64
RING_CHUNKS = 4
SPARSE_PAIRS = 128
WINDOW = 512


layer_eps = 1e-05
norm_eps = 1e-06


def layer_norm(values, gain, shift):
    centre = values - jnp.mean(values, axis=-1, keepdims=True)
    spread = jnp.mean(centre * centre, axis=-1, keepdims=True)
    return centre * lax.rsqrt(spread + layer_eps) * gain + shift


def window_attention(queries_h, keys_h, values_h, lengths):
    seq_len = queries_h.shape[1]
    half_window = WINDOW // 2
    scale_factor = HEAD_DIM ** (-0.5)
    pos = jnp.arange(seq_len, dtype=jnp.int32)
    near = jnp.abs(pos[:, None] - pos[None, :]) <= half_window
    keep_mask = near[None] & (pos[None, None, :] < lengths[:, None, None])
    logits = (
        jnp.einsum("tqhe,tkhe->thqk", queries_h, keys_h, preferred_element_type=jnp.float32)
        * scale_factor
    )
    logits = jnp.where(keep_mask[:, None], logits, jnp.float32(-1e30))
    top_val = jnp.max(logits, axis=-1, keepdims=True)
    expo = jnp.exp(logits - top_val)
    attn_weights = (expo / jnp.sum(expo, axis=-1, keepdims=True)).astype(jnp.bfloat16)
    context = jnp.einsum(
        "thqk,tkhe->tqhe", attn_weights, values_h, preferred_element_type=jnp.float32
    )
    context = jnp.where(
        (pos[None, :] < lengths[:, None])[:, :, None, None], context, jnp.float32(0.0)
    )
    return context.astype(jnp.bfloat16).reshape(
        queries_h.shape[0], seq_len, queries_h.shape[2] * HEAD_DIM
    )


def per_device(
    states,
    lengths,
    w_qkv,
    b_qkv,
    w_out,
    b_out,
    ln1_gain,
    ln1_shift,
    w_up,
    b_up,
    w_down,
    b_down,
    ln2_gain,
    ln2_shift,
    index_rows,
    cand_ids,
):
    tp_count = lax.axis_size("tp")
    tp_rank = lax.axis_index("tp")
    req_count = lax.axis_size("req")
    req_rank = lax.axis_index("req")
    text_count, row_share, model_width = states.shape
    quarter = cand_ids.shape[1]
    full_states = ring_all_gather(states, 0, RING_CHUNKS)
    device_count = req_count * tp_count
    seq_len = full_states.shape[1]
    local_width = w_qkv.shape[2]
    heads_here = local_width // HEAD_DIM
    projected = (
        jnp.einsum("tsd,dce->tsce", full_states, w_qkv, preferred_element_type=jnp.float32) + b_qkv
    ).astype(jnp.bfloat16)
    queries_h = projected[:, :, 0].reshape(text_count, seq_len, heads_here, HEAD_DIM)
    keys_h = projected[:, :, 1].reshape(text_count, seq_len, heads_here, HEAD_DIM)
    values_h = projected[:, :, 2].reshape(text_count, seq_len, heads_here, HEAD_DIM)

    context = window_attention(queries_h, keys_h, values_h, lengths)
    partial_value = jnp.einsum("tsk,kd->tsd", context, w_out, preferred_element_type=jnp.float32)
    partial_value = partial_value.astype(jnp.bfloat16)
    attn_recv = ring_reduce_scatter_add(partial_value, 1, RING_CHUNKS)
    attn_sum = lax.dynamic_slice_in_dim(partial_value, tp_rank * row_share, row_share, 1).astype(
        jnp.float32
    ) + jnp.sum(attn_recv.astype(jnp.float32), axis=0)
    normed_local = layer_norm(
        states.astype(jnp.float32) + attn_sum + b_out, ln1_gain, ln1_shift
    ).astype(jnp.bfloat16)
    normed_full = ring_all_gather(normed_local, 2, RING_CHUNKS)
    up_act = jax.nn.gelu(
        jnp.einsum("tsd,df->tsf", normed_full, w_up, preferred_element_type=jnp.float32) + b_up,
        approximate=False,
    ).astype(jnp.bfloat16)
    down_part = jnp.einsum(
        "tsf,fd->tsd", up_act, w_down, preferred_element_type=jnp.float32
    ).astype(jnp.bfloat16)
    down_recv = ring_reduce_scatter_add(down_part, 3, RING_CHUNKS)
    down_sum = lax.dynamic_slice_in_dim(down_part, tp_rank * row_share, row_share, 1).astype(
        jnp.float32
    ) + jnp.sum(down_recv.astype(jnp.float32), axis=0)
    hidden_out = layer_norm(
        normed_local.astype(jnp.float32) + down_sum + b_down, ln2_gain, ln2_shift
    ).astype(jnp.bfloat16)
    positions = tp_rank * row_share + jnp.arange(row_share, dtype=jnp.int32)
    is_valid = positions[None, :] < lengths[:, None]
    local_pool = jnp.sum(
        jnp.where(is_valid[:, :, None], hidden_out.astype(jnp.float32), jnp.float32(0.0)), axis=1
    )
    pool_and_ids = direct_exchange(
        jnp.concatenate([local_pool, cand_ids.astype(jnp.float32)], axis=1), ("tp",), 5
    )
    text_ids = jnp.swapaxes(pool_and_ids[:, :, model_width:], 0, 1)
    pooled = jnp.sum(pool_and_ids[:, :, :model_width], axis=0) / lengths.astype(
        jnp.float32
    )[:, None]
    query_vec = (
        pooled * lax.rsqrt(jnp.mean(pooled * pooled, axis=-1, keepdims=True) + norm_eps)
    ).astype(jnp.bfloat16)
    bundle = jnp.concatenate(
        [query_vec.astype(jnp.float32), text_ids.reshape(text_count, -1)], axis=1
    )
    bundle = direct_exchange(bundle, ("req",), 6).reshape(req_count * text_count, bundle.shape[1])
    all_queries = bundle[:, :model_width].astype(jnp.bfloat16)
    all_ids = bundle[:, model_width:].astype(jnp.int32)
    rows_here = index_rows.shape[0]
    first_row = (req_rank * tp_count + tp_rank) * rows_here
    local_ids = all_ids - first_row
    is_owned = (local_ids >= 0) & (local_ids < rows_here)
    safe_ids = jnp.clip(local_ids, 0, rows_here - 1)
    owned_count = jnp.sum(is_owned.astype(jnp.int32))

    def few_owned(_):
        flat_owned = is_owned.reshape(-1)
        owned_int = is_owned.astype(jnp.int32)
        row_counts = jnp.cumsum(owned_int, axis=1)
        row_totals = row_counts[:, -1]
        running = (row_counts + (jnp.cumsum(row_totals) - row_totals)[:, None]).reshape(-1)
        rank = jnp.arange(SPARSE_PAIRS, dtype=jnp.int32)
        chosen = flat_owned[None, :] & (running[None, :] == rank[:, None] + 1)
        pair_index = jnp.arange(flat_owned.shape[0], dtype=jnp.int32)
        pair_at = jnp.sum(jnp.where(chosen, pair_index[None, :], 0), axis=1)
        rows = jnp.take(index_rows, safe_ids.reshape(-1)[pair_at], axis=0)
        queries = jnp.take(all_queries, pair_at // all_ids.shape[1], axis=0)
        values = jnp.sum(rows.astype(jnp.float32) * queries.astype(jnp.float32), axis=-1)
        return jnp.sum(
            jnp.where(chosen, values[:, None], jnp.float32(0.0)), axis=0
        ).reshape(all_ids.shape)

    def many_owned(_):
        all_scores = jnp.einsum(
            "td,rd->tr", all_queries, index_rows, preferred_element_type=jnp.float32
        )
        score_rows = jnp.take(all_scores.T, safe_ids.reshape(-1), axis=0).reshape(
            safe_ids.shape[0], safe_ids.shape[1], safe_ids.shape[0]
        )
        picked = jnp.einsum("tct->tc", score_rows)
        return jnp.where(is_owned, picked, jnp.float32(0.0))

    owner_terms = lax.cond(owned_count <= SPARSE_PAIRS, few_owned, many_owned, None)
    owner_terms = (
        owner_terms.reshape(req_count, text_count, tp_count, quarter)
        .transpose(0, 2, 1, 3)
        .reshape(device_count, text_count, quarter)
    )
    scores = jnp.sum(lax.all_to_all(owner_terms, ("req", "tp"), 0, 0, tiled=True), axis=0)
    return (hidden_out, scores)


def solution(mesh):
    placed = (
        P("req", "tp", None),
        P("req"),
        P(None, None, "tp"),
        P(None, "tp"),
        P("tp", None),
        P(),
        P(),
        P(),
        P(None, "tp"),
        P("tp"),
        P("tp", None),
        P(),
        P(),
        P(),
        P(("req", "tp"), None),
        P("req", "tp"),
    )
    return jax.shard_map(
        per_device,
        mesh=mesh,
        in_specs=placed,
        out_specs=(P("req", "tp", None), P("req", "tp")),
        check_vma=False,
    )
```

```python
import functools
import jax
import jax.numpy as jnp
from jax import lax
from jax.experimental import pallas as pl
from jax.experimental.pallas import tpu as pltpu
from jax.sharding import PartitionSpec as P

MESH_ID = pl.DeviceIdType.MESH


def _ring_peers():
    n = lax.axis_size("tp")
    me = lax.axis_index("tp")
    rq = lax.axis_index("req")
    core = rq % 2
    right = (me + 1) % n
    left = (me + n - 1) % n
    opp = (me + 2) % n
    relay_to = (me + 1 + 2 * core) % n
    relay_from = (me + n - 1 - 2 * core) % n
    barrier = pltpu.get_barrier_semaphore()
    for peer in (left, right):
        pl.semaphore_signal(barrier, inc=1, device_id=(rq, peer), device_id_type=MESH_ID)
    pl.semaphore_wait(barrier, 2)
    return me, rq, core, right, left, opp, relay_to, relay_from


def _gather_kernel(chunks, x_ref, out_ref, send_sem, recv_sem, local_sem):
    me, rq, core, right, left, opp, relay_to, relay_from = _ring_peers()
    rows = x_ref.shape[1]
    step = rows // chunks

    def part(ref, k):
        return ref.at[:, pl.ds(k * step, step), :]

    def slot(src, k):
        return out_ref.at[:, pl.ds(src * rows + k * step, step), :]

    def copy(src, dst, send, recv, peer):
        return pltpu.make_async_remote_copy(
            src, dst, send, recv, device_id=(rq, peer), device_id_type=MESH_ID
        )

    local = pltpu.make_async_copy(x_ref, out_ref.at[:, pl.ds(me * rows, rows), :], local_sem)
    local.start()
    sends = []
    for k in range(chunks):
        to_right = copy(part(x_ref, k), slot(me, k), send_sem.at[0, k], recv_sem.at[0, k], right)
        to_left = copy(part(x_ref, k), slot(me, k), send_sem.at[1, k], recv_sem.at[1, k], left)
        to_right.start()
        to_left.start()
        sends += [to_right, to_left]
    for k in range(chunks):
        copy(part(x_ref, k), slot(relay_from, k), send_sem.at[2, k], recv_sem.at[core, k], right).wait_recv()
        forward = copy(
            slot(relay_from, k), slot(relay_from, k), send_sem.at[2, k], recv_sem.at[2, k], relay_to
        )
        forward.start()
        sends.append(forward)
    other_side = (me + 1 + 2 * (1 - core)) % lax.axis_size("tp")
    for k in range(chunks):
        copy(part(x_ref, k), slot(other_side, k), send_sem.at[0, k], recv_sem.at[1 - core, k], right).wait_recv()
    for k in range(chunks):
        copy(part(x_ref, k), slot(opp, k), send_sem.at[0, k], recv_sem.at[2, k], right).wait_recv()
    for c in sends:
        c.wait_send()
    local.wait()


def ring_all_gather(x, collective_id, chunks=1):
    texts, rows, width = x.shape
    n = lax.axis_size("tp")
    return pl.pallas_call(
        functools.partial(_gather_kernel, chunks),
        out_shape=jax.ShapeDtypeStruct((texts, n * rows, width), x.dtype),
        in_specs=[pl.BlockSpec(memory_space=pl.ANY)],
        out_specs=pl.BlockSpec(memory_space=pl.ANY),
        scratch_shapes=[
            pltpu.SemaphoreType.DMA((3, chunks)),
            pltpu.SemaphoreType.DMA((3, chunks)),
            pltpu.SemaphoreType.DMA,
        ],
        compiler_params=pltpu.CompilerParams(collective_id=collective_id, has_side_effects=True),
    )(x)


def _scatter_add_kernel(chunks, p_ref, recv_ref, send_sem, recv_sem, relay_sem, local_sem,
                        own_buf, relay_buf, sum_buf):
    me, rq, core, right, left, opp, relay_to, relay_from = _ring_peers()
    rows = recv_ref.shape[2]
    step = rows // chunks

    def block(dst, k):
        return p_ref.at[:, pl.ds(dst * rows + k * step, step), :]

    def part(ref, k):
        return ref.at[:, pl.ds(k * step, step), :]

    def copy(src, dst, send, recv, peer):
        return pltpu.make_async_remote_copy(
            src, dst, send, recv, device_id=(rq, peer), device_id_type=MESH_ID
        )

    sends = []
    loads = []
    for k in range(chunks):
        to_relay = copy(block(opp, k), relay_buf.at[k], send_sem.at[0, k], relay_sem.at[k], relay_to)
        to_other = copy(
            block(relay_from, k), part(recv_ref.at[1], k), send_sem.at[1, k], recv_sem.at[1, k], relay_from
        )
        to_relay.start()
        to_other.start()
        load = pltpu.make_async_copy(block(relay_to, k), own_buf.at[k], local_sem.at[k])
        load.start()
        sends += [to_relay, to_other]
        loads.append(load)
    forwards = []
    for k in range(chunks):
        sends[2 * k].wait_recv()
        loads[k].wait()
        sum_buf[k] = (
            own_buf[k].astype(jnp.float32) + relay_buf[k].astype(jnp.float32)
        ).astype(sum_buf.dtype)
        forward = copy(sum_buf.at[k], part(recv_ref.at[0], k), send_sem.at[2, k], recv_sem.at[0, k], relay_to)
        forward.start()
        forwards.append(forward)
    for k in range(chunks):
        sends[2 * k + 1].wait_recv()
        forwards[k].wait_recv()
    for c in sends + forwards:
        c.wait_send()


def ring_reduce_scatter_add(p, collective_id, chunks=1):
    texts, all_rows, width = p.shape
    n = lax.axis_size("tp")
    rows = all_rows // n
    step = rows // chunks
    buf = pltpu.VMEM((chunks, texts, step, width), p.dtype)
    return pl.pallas_call(
        functools.partial(_scatter_add_kernel, chunks),
        out_shape=jax.ShapeDtypeStruct((2, texts, rows, width), p.dtype),
        in_specs=[pl.BlockSpec(memory_space=pl.ANY)],
        out_specs=pl.BlockSpec(memory_space=pl.ANY),
        scratch_shapes=[
            pltpu.SemaphoreType.DMA((3, chunks)),
            pltpu.SemaphoreType.DMA((2, chunks)),
            pltpu.SemaphoreType.DMA((chunks,)),
            pltpu.SemaphoreType.DMA((chunks,)),
            buf,
            buf,
            buf,
        ],
        compiler_params=pltpu.CompilerParams(collective_id=collective_id, has_side_effects=True),
    )(p)


def _peer_id(axes, peer):
    if axes == ("tp",):
        return (lax.axis_index("req"), peer)
    if axes == ("req",):
        return (peer, lax.axis_index("tp"))
    n_tp = lax.axis_size("tp")
    return (peer // n_tp, peer % n_tp)


def _direct_kernel(axes, scatter, x_ref, out_ref, send_sem, recv_sem, local_sem):
    n = out_ref.shape[0]
    me = lax.axis_index(axes)
    barrier = pltpu.get_barrier_semaphore()

    def greet(d, carry):
        peer = (me + d) % n
        pl.semaphore_signal(barrier, inc=1, device_id=_peer_id(axes, peer), device_id_type=MESH_ID)
        return carry

    lax.fori_loop(1, n, greet, 0)
    pl.semaphore_wait(barrier, n - 1)

    def source(peer):
        return x_ref.at[peer] if scatter else x_ref

    local = pltpu.make_async_copy(source(me), out_ref.at[me], local_sem)
    local.start()

    def send(d, carry):
        peer = (me + d) % n
        pltpu.make_async_remote_copy(
            source(peer), out_ref.at[me], send_sem.at[d], recv_sem.at[me],
            device_id=_peer_id(axes, peer), device_id_type=MESH_ID,
        ).start()
        return carry

    lax.fori_loop(1, n, send, 0)

    def receive(d, carry):
        src = (me + n - d) % n
        pltpu.make_async_remote_copy(
            source(src), out_ref.at[src], send_sem.at[d], recv_sem.at[src],
            device_id=_peer_id(axes, src), device_id_type=MESH_ID,
        ).wait_recv()
        return carry

    lax.fori_loop(1, n, receive, 0)

    def sent(d, carry):
        peer = (me + d) % n
        pltpu.make_async_remote_copy(
            source(peer), out_ref.at[me], send_sem.at[d], recv_sem.at[me],
            device_id=_peer_id(axes, peer), device_id_type=MESH_ID,
        ).wait_send()
        return carry

    lax.fori_loop(1, n, sent, 0)
    local.wait()


def direct_exchange(x, axes, collective_id, scatter=False):
    n = 1
    for name in axes:
        n *= lax.axis_size(name)
    block = x.shape[1:] if scatter else x.shape
    return pl.pallas_call(
        functools.partial(_direct_kernel, axes, scatter),
        out_shape=jax.ShapeDtypeStruct((n,) + block, x.dtype),
        in_specs=[pl.BlockSpec(memory_space=pl.ANY)],
        out_specs=pl.BlockSpec(memory_space=pl.ANY),
        scratch_shapes=[
            pltpu.SemaphoreType.DMA((n,)),
            pltpu.SemaphoreType.DMA((n,)),
            pltpu.SemaphoreType.DMA,
        ],
        compiler_params=pltpu.CompilerParams(collective_id=collective_id, has_side_effects=True),
    )(x)


HEAD_DIM = 64
RING_CHUNKS = 4
SPARSE_PAIRS = 128
WINDOW = 512


layer_eps = 1e-05
norm_eps = 1e-06


def layer_norm(values, gain, shift):
    centre = values - jnp.mean(values, axis=-1, keepdims=True)
    spread = jnp.mean(centre * centre, axis=-1, keepdims=True)
    return centre * lax.rsqrt(spread + layer_eps) * gain + shift


def window_attention(queries_h, keys_h, values_h, lengths):
    seq_len = queries_h.shape[1]
    half_window = WINDOW // 2
    scale_factor = HEAD_DIM ** (-0.5)
    pos = jnp.arange(seq_len, dtype=jnp.int32)
    near = jnp.abs(pos[:, None] - pos[None, :]) <= half_window
    keep_mask = near[None] & (pos[None, None, :] < lengths[:, None, None])
    logits = (
        jnp.einsum("tqhe,tkhe->thqk", queries_h, keys_h, preferred_element_type=jnp.float32)
        * scale_factor
    )
    logits = jnp.where(keep_mask[:, None], logits, jnp.float32(-1e30))
    top_val = jnp.max(logits, axis=-1, keepdims=True)
    expo = jnp.exp(logits - top_val)
    attn_weights = (expo / jnp.sum(expo, axis=-1, keepdims=True)).astype(jnp.bfloat16)
    context = jnp.einsum(
        "thqk,tkhe->tqhe", attn_weights, values_h, preferred_element_type=jnp.float32
    )
    context = jnp.where(
        (pos[None, :] < lengths[:, None])[:, :, None, None], context, jnp.float32(0.0)
    )
    return context.astype(jnp.bfloat16).reshape(
        queries_h.shape[0], seq_len, queries_h.shape[2] * HEAD_DIM
    )


def per_device(
    states,
    lengths,
    w_qkv,
    b_qkv,
    w_out,
    b_out,
    ln1_gain,
    ln1_shift,
    w_up,
    b_up,
    w_down,
    b_down,
    ln2_gain,
    ln2_shift,
    index_rows,
    cand_ids,
):
    tp_count = lax.axis_size("tp")
    tp_rank = lax.axis_index("tp")
    req_count = lax.axis_size("req")
    req_rank = lax.axis_index("req")
    text_count, row_share, model_width = states.shape
    quarter = cand_ids.shape[1]
    full_states = ring_all_gather(states, 0, RING_CHUNKS)
    device_count = req_count * tp_count
    seq_len = full_states.shape[1]
    local_width = w_qkv.shape[2]
    heads_here = local_width // HEAD_DIM
    projected = (
        jnp.einsum("tsd,dce->tsce", full_states, w_qkv, preferred_element_type=jnp.float32) + b_qkv
    ).astype(jnp.bfloat16)
    queries_h = projected[:, :, 0].reshape(text_count, seq_len, heads_here, HEAD_DIM)
    keys_h = projected[:, :, 1].reshape(text_count, seq_len, heads_here, HEAD_DIM)
    values_h = projected[:, :, 2].reshape(text_count, seq_len, heads_here, HEAD_DIM)

    context = window_attention(queries_h, keys_h, values_h, lengths)
    partial_value = jnp.einsum("tsk,kd->tsd", context, w_out, preferred_element_type=jnp.float32)
    partial_value = partial_value.astype(jnp.bfloat16)
    attn_recv = ring_reduce_scatter_add(partial_value, 1, RING_CHUNKS)
    attn_sum = lax.dynamic_slice_in_dim(partial_value, tp_rank * row_share, row_share, 1).astype(
        jnp.float32
    ) + jnp.sum(attn_recv.astype(jnp.float32), axis=0)
    normed_local = layer_norm(
        states.astype(jnp.float32) + attn_sum + b_out, ln1_gain, ln1_shift
    ).astype(jnp.bfloat16)
    normed_full = ring_all_gather(normed_local, 2, RING_CHUNKS)
    up_act = jax.nn.gelu(
        jnp.einsum("tsd,df->tsf", normed_full, w_up, preferred_element_type=jnp.float32) + b_up,
        approximate=False,
    ).astype(jnp.bfloat16)
    up_act = lax.optimization_barrier(up_act)
    down_part = jnp.einsum(
        "tsf,fd->tsd", up_act, w_down, preferred_element_type=jnp.float32
    ).astype(jnp.bfloat16)
    down_recv = ring_reduce_scatter_add(down_part, 3, RING_CHUNKS)
    down_sum = lax.dynamic_slice_in_dim(down_part, tp_rank * row_share, row_share, 1).astype(
        jnp.float32
    ) + jnp.sum(down_recv.astype(jnp.float32), axis=0)
    hidden_out = layer_norm(
        normed_local.astype(jnp.float32) + down_sum + b_down, ln2_gain, ln2_shift
    ).astype(jnp.bfloat16)
    positions = tp_rank * row_share + jnp.arange(row_share, dtype=jnp.int32)
    is_valid = positions[None, :] < lengths[:, None]
    local_pool = jnp.sum(
        jnp.where(is_valid[:, :, None], hidden_out.astype(jnp.float32), jnp.float32(0.0)), axis=1
    )
    pool_and_ids = direct_exchange(
        jnp.concatenate([local_pool, cand_ids.astype(jnp.float32)], axis=1), ("tp",), 5
    )
    text_ids = jnp.swapaxes(pool_and_ids[:, :, model_width:], 0, 1)
    pooled = jnp.sum(pool_and_ids[:, :, :model_width], axis=0) / lengths.astype(
        jnp.float32
    )[:, None]
    query_vec = (
        pooled * lax.rsqrt(jnp.mean(pooled * pooled, axis=-1, keepdims=True) + norm_eps)
    ).astype(jnp.bfloat16)
    bundle = jnp.concatenate(
        [query_vec.astype(jnp.float32), text_ids.reshape(text_count, -1)], axis=1
    )
    bundle = direct_exchange(bundle, ("req",), 6).reshape(req_count * text_count, bundle.shape[1])
    all_queries = bundle[:, :model_width].astype(jnp.bfloat16)
    all_ids = bundle[:, model_width:].astype(jnp.int32)
    rows_here = index_rows.shape[0]
    first_row = (req_rank * tp_count + tp_rank) * rows_here
    local_ids = all_ids - first_row
    is_owned = (local_ids >= 0) & (local_ids < rows_here)
    safe_ids = jnp.clip(local_ids, 0, rows_here - 1)
    owned_count = jnp.sum(is_owned.astype(jnp.int32))

    def few_owned(_):
        flat_owned = is_owned.reshape(-1)
        owned_int = is_owned.astype(jnp.int32)
        row_counts = jnp.cumsum(owned_int, axis=1)
        row_totals = row_counts[:, -1]
        running = (row_counts + (jnp.cumsum(row_totals) - row_totals)[:, None]).reshape(-1)
        rank = jnp.arange(SPARSE_PAIRS, dtype=jnp.int32)
        chosen = flat_owned[None, :] & (running[None, :] == rank[:, None] + 1)
        pair_index = jnp.arange(flat_owned.shape[0], dtype=jnp.int32)
        pair_at = jnp.sum(jnp.where(chosen, pair_index[None, :], 0), axis=1)
        rows = jnp.take(index_rows, safe_ids.reshape(-1)[pair_at], axis=0)
        queries = jnp.take(all_queries, pair_at // all_ids.shape[1], axis=0)
        values = jnp.sum(rows.astype(jnp.float32) * queries.astype(jnp.float32), axis=-1)
        return jnp.sum(
            jnp.where(chosen, values[:, None], jnp.float32(0.0)), axis=0
        ).reshape(all_ids.shape)

    def many_owned(_):
        all_scores = jnp.einsum(
            "td,rd->tr", all_queries, index_rows, preferred_element_type=jnp.float32
        )
        score_rows = jnp.take(all_scores.T, safe_ids.reshape(-1), axis=0).reshape(
            safe_ids.shape[0], safe_ids.shape[1], safe_ids.shape[0]
        )
        picked = jnp.einsum("tct->tc", score_rows)
        return jnp.where(is_owned, picked, jnp.float32(0.0))

    owner_terms = lax.cond(owned_count <= SPARSE_PAIRS, few_owned, many_owned, None)
    owner_terms = (
        owner_terms.reshape(req_count, text_count, tp_count, quarter)
        .transpose(0, 2, 1, 3)
        .reshape(device_count, text_count, quarter)
    )
    scores = jnp.sum(lax.all_to_all(owner_terms, ("req", "tp"), 0, 0, tiled=True), axis=0)
    return (hidden_out, scores)


def solution(mesh):
    placed = (
        P("req", "tp", None),
        P("req"),
        P(None, None, "tp"),
        P(None, "tp"),
        P("tp", None),
        P(),
        P(),
        P(),
        P(None, "tp"),
        P("tp"),
        P("tp", None),
        P(),
        P(),
        P(),
        P(("req", "tp"), None),
        P("req", "tp"),
    )
    return jax.shard_map(
        per_device,
        mesh=mesh,
        in_specs=placed,
        out_specs=(P("req", "tp", None), P("req", "tp")),
        check_vma=False,
    )
```

```python
import functools
import jax
import jax.numpy as jnp
from jax import lax
from jax.experimental import pallas as pl
from jax.experimental.pallas import tpu as pltpu
from jax.sharding import PartitionSpec as P

MESH_ID = pl.DeviceIdType.MESH


def _ring_peers():
    n = lax.axis_size("tp")
    me = lax.axis_index("tp")
    rq = lax.axis_index("req")
    core = rq % 2
    right = (me + 1) % n
    left = (me + n - 1) % n
    opp = (me + 2) % n
    relay_to = (me + 1 + 2 * core) % n
    relay_from = (me + n - 1 - 2 * core) % n
    barrier = pltpu.get_barrier_semaphore()
    for peer in (left, right):
        pl.semaphore_signal(barrier, inc=1, device_id=(rq, peer), device_id_type=MESH_ID)
    pl.semaphore_wait(barrier, 2)
    return me, rq, core, right, left, opp, relay_to, relay_from


def _gather_kernel(chunks, x_ref, out_ref, send_sem, recv_sem, local_sem):
    me, rq, core, right, left, opp, relay_to, relay_from = _ring_peers()
    rows = x_ref.shape[1]
    step = rows // chunks

    def part(ref, k):
        return ref.at[:, pl.ds(k * step, step), :]

    def slot(src, k):
        return out_ref.at[:, pl.ds(src * rows + k * step, step), :]

    def copy(src, dst, send, recv, peer):
        return pltpu.make_async_remote_copy(
            src, dst, send, recv, device_id=(rq, peer), device_id_type=MESH_ID
        )

    local = pltpu.make_async_copy(x_ref, out_ref.at[:, pl.ds(me * rows, rows), :], local_sem)
    local.start()
    sends = []
    for k in range(chunks):
        to_right = copy(part(x_ref, k), slot(me, k), send_sem.at[0, k], recv_sem.at[0, k], right)
        to_left = copy(part(x_ref, k), slot(me, k), send_sem.at[1, k], recv_sem.at[1, k], left)
        to_right.start()
        to_left.start()
        sends += [to_right, to_left]
    for k in range(chunks):
        copy(part(x_ref, k), slot(relay_from, k), send_sem.at[2, k], recv_sem.at[core, k], right).wait_recv()
        forward = copy(
            slot(relay_from, k), slot(relay_from, k), send_sem.at[2, k], recv_sem.at[2, k], relay_to
        )
        forward.start()
        sends.append(forward)
    other_side = (me + 1 + 2 * (1 - core)) % lax.axis_size("tp")
    for k in range(chunks):
        copy(part(x_ref, k), slot(other_side, k), send_sem.at[0, k], recv_sem.at[1 - core, k], right).wait_recv()
    for k in range(chunks):
        copy(part(x_ref, k), slot(opp, k), send_sem.at[0, k], recv_sem.at[2, k], right).wait_recv()
    for c in sends:
        c.wait_send()
    local.wait()


def ring_all_gather(x, collective_id, chunks=1):
    texts, rows, width = x.shape
    n = lax.axis_size("tp")
    return pl.pallas_call(
        functools.partial(_gather_kernel, chunks),
        out_shape=jax.ShapeDtypeStruct((texts, n * rows, width), x.dtype),
        in_specs=[pl.BlockSpec(memory_space=pl.ANY)],
        out_specs=pl.BlockSpec(memory_space=pl.ANY),
        scratch_shapes=[
            pltpu.SemaphoreType.DMA((3, chunks)),
            pltpu.SemaphoreType.DMA((3, chunks)),
            pltpu.SemaphoreType.DMA,
        ],
        compiler_params=pltpu.CompilerParams(collective_id=collective_id, has_side_effects=True),
    )(x)


def _scatter_add_kernel(chunks, p_ref, recv_ref, send_sem, recv_sem, relay_sem, local_sem,
                        own_buf, relay_buf, sum_buf):
    me, rq, core, right, left, opp, relay_to, relay_from = _ring_peers()
    rows = recv_ref.shape[2]
    step = rows // chunks

    def block(dst, k):
        return p_ref.at[:, pl.ds(dst * rows + k * step, step), :]

    def part(ref, k):
        return ref.at[:, pl.ds(k * step, step), :]

    def copy(src, dst, send, recv, peer):
        return pltpu.make_async_remote_copy(
            src, dst, send, recv, device_id=(rq, peer), device_id_type=MESH_ID
        )

    sends = []
    loads = []
    for k in range(chunks):
        to_relay = copy(block(opp, k), relay_buf.at[k], send_sem.at[0, k], relay_sem.at[k], relay_to)
        to_other = copy(
            block(relay_from, k), part(recv_ref.at[1], k), send_sem.at[1, k], recv_sem.at[1, k], relay_from
        )
        to_relay.start()
        to_other.start()
        load = pltpu.make_async_copy(block(relay_to, k), own_buf.at[k], local_sem.at[k])
        load.start()
        sends += [to_relay, to_other]
        loads.append(load)
    forwards = []
    for k in range(chunks):
        sends[2 * k].wait_recv()
        loads[k].wait()
        sum_buf[k] = (
            own_buf[k].astype(jnp.float32) + relay_buf[k].astype(jnp.float32)
        ).astype(sum_buf.dtype)
        forward = copy(sum_buf.at[k], part(recv_ref.at[0], k), send_sem.at[2, k], recv_sem.at[0, k], relay_to)
        forward.start()
        forwards.append(forward)
    for k in range(chunks):
        sends[2 * k + 1].wait_recv()
        forwards[k].wait_recv()
    for c in sends + forwards:
        c.wait_send()


def ring_reduce_scatter_add(p, collective_id, chunks=1):
    texts, all_rows, width = p.shape
    n = lax.axis_size("tp")
    rows = all_rows // n
    step = rows // chunks
    buf = pltpu.VMEM((chunks, texts, step, width), p.dtype)
    return pl.pallas_call(
        functools.partial(_scatter_add_kernel, chunks),
        out_shape=jax.ShapeDtypeStruct((2, texts, rows, width), p.dtype),
        in_specs=[pl.BlockSpec(memory_space=pl.ANY)],
        out_specs=pl.BlockSpec(memory_space=pl.ANY),
        scratch_shapes=[
            pltpu.SemaphoreType.DMA((3, chunks)),
            pltpu.SemaphoreType.DMA((2, chunks)),
            pltpu.SemaphoreType.DMA((chunks,)),
            pltpu.SemaphoreType.DMA((chunks,)),
            buf,
            buf,
            buf,
        ],
        compiler_params=pltpu.CompilerParams(collective_id=collective_id, has_side_effects=True),
    )(p)


def _peer_id(axes, peer):
    if axes == ("tp",):
        return (lax.axis_index("req"), peer)
    if axes == ("req",):
        return (peer, lax.axis_index("tp"))
    n_tp = lax.axis_size("tp")
    return (peer // n_tp, peer % n_tp)


def _direct_kernel(axes, scatter, x_ref, out_ref, send_sem, recv_sem, local_sem):
    n = out_ref.shape[0]
    me = lax.axis_index(axes)
    barrier = pltpu.get_barrier_semaphore()

    def greet(d, carry):
        peer = (me + d) % n
        pl.semaphore_signal(barrier, inc=1, device_id=_peer_id(axes, peer), device_id_type=MESH_ID)
        return carry

    lax.fori_loop(1, n, greet, 0)
    pl.semaphore_wait(barrier, n - 1)

    def source(peer):
        return x_ref.at[peer] if scatter else x_ref

    local = pltpu.make_async_copy(source(me), out_ref.at[me], local_sem)
    local.start()

    def send(d, carry):
        peer = (me + d) % n
        pltpu.make_async_remote_copy(
            source(peer), out_ref.at[me], send_sem.at[d], recv_sem.at[me],
            device_id=_peer_id(axes, peer), device_id_type=MESH_ID,
        ).start()
        return carry

    lax.fori_loop(1, n, send, 0)

    def receive(d, carry):
        src = (me + n - d) % n
        pltpu.make_async_remote_copy(
            source(src), out_ref.at[src], send_sem.at[d], recv_sem.at[src],
            device_id=_peer_id(axes, src), device_id_type=MESH_ID,
        ).wait_recv()
        return carry

    lax.fori_loop(1, n, receive, 0)

    def sent(d, carry):
        peer = (me + d) % n
        pltpu.make_async_remote_copy(
            source(peer), out_ref.at[me], send_sem.at[d], recv_sem.at[me],
            device_id=_peer_id(axes, peer), device_id_type=MESH_ID,
        ).wait_send()
        return carry

    lax.fori_loop(1, n, sent, 0)
    local.wait()


def direct_exchange(x, axes, collective_id, scatter=False):
    n = 1
    for name in axes:
        n *= lax.axis_size(name)
    block = x.shape[1:] if scatter else x.shape
    return pl.pallas_call(
        functools.partial(_direct_kernel, axes, scatter),
        out_shape=jax.ShapeDtypeStruct((n,) + block, x.dtype),
        in_specs=[pl.BlockSpec(memory_space=pl.ANY)],
        out_specs=pl.BlockSpec(memory_space=pl.ANY),
        scratch_shapes=[
            pltpu.SemaphoreType.DMA((n,)),
            pltpu.SemaphoreType.DMA((n,)),
            pltpu.SemaphoreType.DMA,
        ],
        compiler_params=pltpu.CompilerParams(collective_id=collective_id, has_side_effects=True),
    )(x)


HEAD_DIM = 64
RING_CHUNKS = 8
SPARSE_PAIRS = 64
WINDOW = 512


layer_eps = 1e-05
norm_eps = 1e-06


def layer_norm(values, gain, shift):
    centre = values - jnp.mean(values, axis=-1, keepdims=True)
    spread = jnp.mean(centre * centre, axis=-1, keepdims=True)
    return centre * lax.rsqrt(spread + layer_eps) * gain + shift


def window_attention(queries_h, keys_h, values_h, lengths):
    seq_len = queries_h.shape[1]
    half_window = WINDOW // 2
    scale_factor = HEAD_DIM ** (-0.5)
    pos = jnp.arange(seq_len, dtype=jnp.int32)
    near = jnp.abs(pos[:, None] - pos[None, :]) <= half_window
    keep_mask = near[None] & (pos[None, None, :] < lengths[:, None, None])
    logits = (
        jnp.einsum("tqhe,tkhe->thqk", queries_h, keys_h, preferred_element_type=jnp.float32)
        * scale_factor
    )
    logits = jnp.where(keep_mask[:, None], logits, jnp.float32(-1e30))
    top_val = jnp.max(logits, axis=-1, keepdims=True)
    expo = jnp.exp(logits - top_val)
    attn_weights = (expo / jnp.sum(expo, axis=-1, keepdims=True)).astype(jnp.bfloat16)
    context = jnp.einsum(
        "thqk,tkhe->tqhe", attn_weights, values_h, preferred_element_type=jnp.float32
    )
    context = jnp.where(
        (pos[None, :] < lengths[:, None])[:, :, None, None], context, jnp.float32(0.0)
    )
    return context.astype(jnp.bfloat16).reshape(
        queries_h.shape[0], seq_len, queries_h.shape[2] * HEAD_DIM
    )


def per_device(
    states,
    lengths,
    w_qkv,
    b_qkv,
    w_out,
    b_out,
    ln1_gain,
    ln1_shift,
    w_up,
    b_up,
    w_down,
    b_down,
    ln2_gain,
    ln2_shift,
    index_rows,
    cand_ids,
):
    tp_count = lax.axis_size("tp")
    tp_rank = lax.axis_index("tp")
    req_count = lax.axis_size("req")
    req_rank = lax.axis_index("req")
    text_count, row_share, model_width = states.shape
    quarter = cand_ids.shape[1]
    full_states = ring_all_gather(states, 0, RING_CHUNKS)
    device_count = req_count * tp_count
    seq_len = full_states.shape[1]
    local_width = w_qkv.shape[2]
    heads_here = local_width // HEAD_DIM
    projected = (
        jnp.einsum("tsd,dce->tsce", full_states, w_qkv, preferred_element_type=jnp.float32) + b_qkv
    ).astype(jnp.bfloat16)
    queries_h = projected[:, :, 0].reshape(text_count, seq_len, heads_here, HEAD_DIM)
    keys_h = projected[:, :, 1].reshape(text_count, seq_len, heads_here, HEAD_DIM)
    values_h = projected[:, :, 2].reshape(text_count, seq_len, heads_here, HEAD_DIM)

    context = window_attention(queries_h, keys_h, values_h, lengths)
    partial_value = jnp.einsum("tsk,kd->tsd", context, w_out, preferred_element_type=jnp.float32)
    partial_value = partial_value.astype(jnp.bfloat16)
    attn_recv = ring_reduce_scatter_add(partial_value, 1, RING_CHUNKS)
    attn_sum = lax.dynamic_slice_in_dim(partial_value, tp_rank * row_share, row_share, 1).astype(
        jnp.float32
    ) + jnp.sum(attn_recv.astype(jnp.float32), axis=0)
    normed_local = layer_norm(
        states.astype(jnp.float32) + attn_sum + b_out, ln1_gain, ln1_shift
    ).astype(jnp.bfloat16)
    normed_full = ring_all_gather(normed_local, 2, RING_CHUNKS)
    up_act = jax.nn.gelu(
        jnp.einsum("tsd,df->tsf", normed_full, w_up, preferred_element_type=jnp.float32) + b_up,
        approximate=False,
    ).astype(jnp.bfloat16)
    up_act = lax.optimization_barrier(up_act)
    down_part = jnp.einsum(
        "tsf,fd->tsd", up_act, w_down, preferred_element_type=jnp.float32
    ).astype(jnp.bfloat16)
    down_recv = ring_reduce_scatter_add(down_part, 3, RING_CHUNKS)
    down_sum = lax.dynamic_slice_in_dim(down_part, tp_rank * row_share, row_share, 1).astype(
        jnp.float32
    ) + jnp.sum(down_recv.astype(jnp.float32), axis=0)
    hidden_out = layer_norm(
        normed_local.astype(jnp.float32) + down_sum + b_down, ln2_gain, ln2_shift
    ).astype(jnp.bfloat16)
    positions = tp_rank * row_share + jnp.arange(row_share, dtype=jnp.int32)
    is_valid = positions[None, :] < lengths[:, None]
    local_pool = jnp.sum(
        jnp.where(is_valid[:, :, None], hidden_out.astype(jnp.float32), jnp.float32(0.0)), axis=1
    )
    pool_and_ids = direct_exchange(
        jnp.concatenate([local_pool, cand_ids.astype(jnp.float32)], axis=1), ("tp",), 5
    )
    text_ids = jnp.swapaxes(pool_and_ids[:, :, model_width:], 0, 1)
    pooled = jnp.sum(pool_and_ids[:, :, :model_width], axis=0) / lengths.astype(
        jnp.float32
    )[:, None]
    query_vec = (
        pooled * lax.rsqrt(jnp.mean(pooled * pooled, axis=-1, keepdims=True) + norm_eps)
    ).astype(jnp.bfloat16)
    bundle = jnp.concatenate(
        [query_vec.astype(jnp.float32), text_ids.reshape(text_count, -1)], axis=1
    )
    bundle = direct_exchange(bundle, ("req",), 6).reshape(req_count * text_count, bundle.shape[1])
    all_queries = bundle[:, :model_width].astype(jnp.bfloat16)
    all_ids = bundle[:, model_width:].astype(jnp.int32)
    rows_here = index_rows.shape[0]
    first_row = (req_rank * tp_count + tp_rank) * rows_here
    local_ids = all_ids - first_row
    is_owned = (local_ids >= 0) & (local_ids < rows_here)
    safe_ids = jnp.clip(local_ids, 0, rows_here - 1)
    owned_count = jnp.sum(is_owned.astype(jnp.int32))

    def few_owned(_):
        flat_owned = is_owned.reshape(-1)
        owned_int = is_owned.astype(jnp.int32)
        row_counts = jnp.cumsum(owned_int, axis=1)
        row_totals = row_counts[:, -1]
        running = (row_counts + (jnp.cumsum(row_totals) - row_totals)[:, None]).reshape(-1)
        rank = jnp.arange(SPARSE_PAIRS, dtype=jnp.int32)
        chosen = flat_owned[None, :] & (running[None, :] == rank[:, None] + 1)
        pair_index = jnp.arange(flat_owned.shape[0], dtype=jnp.int32)
        pair_at = jnp.sum(jnp.where(chosen, pair_index[None, :], 0), axis=1)
        rows = jnp.take(index_rows, safe_ids.reshape(-1)[pair_at], axis=0)
        queries = jnp.take(all_queries, pair_at // all_ids.shape[1], axis=0)
        values = jnp.sum(rows.astype(jnp.float32) * queries.astype(jnp.float32), axis=-1)
        return jnp.sum(
            jnp.where(chosen, values[:, None], jnp.float32(0.0)), axis=0
        ).reshape(all_ids.shape)

    def many_owned(_):
        all_scores = jnp.einsum(
            "td,rd->tr", all_queries, index_rows, preferred_element_type=jnp.float32
        )
        score_rows = jnp.take(all_scores.T, safe_ids.reshape(-1), axis=0).reshape(
            safe_ids.shape[0], safe_ids.shape[1], safe_ids.shape[0]
        )
        picked = jnp.einsum("tct->tc", score_rows)
        return jnp.where(is_owned, picked, jnp.float32(0.0))

    owner_terms = lax.cond(owned_count <= SPARSE_PAIRS, few_owned, many_owned, None)
    owner_terms = (
        owner_terms.reshape(req_count, text_count, tp_count, quarter)
        .transpose(0, 2, 1, 3)
        .reshape(device_count, text_count, quarter)
    )
    scores = jnp.sum(lax.all_to_all(owner_terms, ("req", "tp"), 0, 0, tiled=True), axis=0)
    return (hidden_out, scores)


def solution(mesh):
    placed = (
        P("req", "tp", None),
        P("req"),
        P(None, None, "tp"),
        P(None, "tp"),
        P("tp", None),
        P(),
        P(),
        P(),
        P(None, "tp"),
        P("tp"),
        P("tp", None),
        P(),
        P(),
        P(),
        P(("req", "tp"), None),
        P("req", "tp"),
    )
    return jax.shard_map(
        per_device,
        mesh=mesh,
        in_specs=placed,
        out_specs=(P("req", "tp", None), P("req", "tp")),
        check_vma=False,
    )
```

```python
import functools
import jax
import jax.numpy as jnp
from jax import lax
from jax.experimental import pallas as pl
from jax.experimental.pallas import tpu as pltpu
from jax.sharding import PartitionSpec as P

MESH_ID = pl.DeviceIdType.MESH


def _ring_peers():
    n = lax.axis_size("tp")
    me = lax.axis_index("tp")
    rq = lax.axis_index("req")
    core = rq % 2
    right = (me + 1) % n
    left = (me + n - 1) % n
    opp = (me + 2) % n
    relay_to = (me + 1 + 2 * core) % n
    relay_from = (me + n - 1 - 2 * core) % n
    barrier = pltpu.get_barrier_semaphore()
    for peer in (left, right):
        pl.semaphore_signal(barrier, inc=1, device_id=(rq, peer), device_id_type=MESH_ID)
    pl.semaphore_wait(barrier, 2)
    return me, rq, core, right, left, opp, relay_to, relay_from


def _gather_kernel(chunks, x_ref, out_ref, send_sem, recv_sem, local_sem):
    me, rq, core, right, left, opp, relay_to, relay_from = _ring_peers()
    rows = x_ref.shape[1]
    step = rows // chunks

    def part(ref, k):
        return ref.at[:, pl.ds(k * step, step), :]

    def slot(src, k):
        return out_ref.at[:, pl.ds(src * rows + k * step, step), :]

    def copy(src, dst, send, recv, peer):
        return pltpu.make_async_remote_copy(
            src, dst, send, recv, device_id=(rq, peer), device_id_type=MESH_ID
        )

    local = pltpu.make_async_copy(x_ref, out_ref.at[:, pl.ds(me * rows, rows), :], local_sem)
    local.start()
    sends = []
    for k in range(chunks):
        to_right = copy(part(x_ref, k), slot(me, k), send_sem.at[0, k], recv_sem.at[0, k], right)
        to_left = copy(part(x_ref, k), slot(me, k), send_sem.at[1, k], recv_sem.at[1, k], left)
        to_right.start()
        to_left.start()
        sends += [to_right, to_left]
    for k in range(chunks):
        copy(part(x_ref, k), slot(relay_from, k), send_sem.at[2, k], recv_sem.at[core, k], right).wait_recv()
        forward = copy(
            slot(relay_from, k), slot(relay_from, k), send_sem.at[2, k], recv_sem.at[2, k], relay_to
        )
        forward.start()
        sends.append(forward)
    other_side = (me + 1 + 2 * (1 - core)) % lax.axis_size("tp")
    for k in range(chunks):
        copy(part(x_ref, k), slot(other_side, k), send_sem.at[0, k], recv_sem.at[1 - core, k], right).wait_recv()
    for k in range(chunks):
        copy(part(x_ref, k), slot(opp, k), send_sem.at[0, k], recv_sem.at[2, k], right).wait_recv()
    for c in sends:
        c.wait_send()
    local.wait()


def ring_all_gather(x, collective_id, chunks=1):
    texts, rows, width = x.shape
    n = lax.axis_size("tp")
    return pl.pallas_call(
        functools.partial(_gather_kernel, chunks),
        out_shape=jax.ShapeDtypeStruct((texts, n * rows, width), x.dtype),
        in_specs=[pl.BlockSpec(memory_space=pl.ANY)],
        out_specs=pl.BlockSpec(memory_space=pl.ANY),
        scratch_shapes=[
            pltpu.SemaphoreType.DMA((3, chunks)),
            pltpu.SemaphoreType.DMA((3, chunks)),
            pltpu.SemaphoreType.DMA,
        ],
        compiler_params=pltpu.CompilerParams(collective_id=collective_id, has_side_effects=True),
    )(x)


def _scatter_add_kernel(chunks, p_ref, recv_ref, send_sem, recv_sem, relay_sem, local_sem,
                        own_buf, relay_buf, sum_buf):
    me, rq, core, right, left, opp, relay_to, relay_from = _ring_peers()
    rows = recv_ref.shape[2]
    step = rows // chunks

    def block(dst, k):
        return p_ref.at[:, pl.ds(dst * rows + k * step, step), :]

    def part(ref, k):
        return ref.at[:, pl.ds(k * step, step), :]

    def copy(src, dst, send, recv, peer):
        return pltpu.make_async_remote_copy(
            src, dst, send, recv, device_id=(rq, peer), device_id_type=MESH_ID
        )

    sends = []
    loads = []
    for k in range(chunks):
        to_relay = copy(block(opp, k), relay_buf.at[k], send_sem.at[0, k], relay_sem.at[k], relay_to)
        to_other = copy(
            block(relay_from, k), part(recv_ref.at[1], k), send_sem.at[1, k], recv_sem.at[1, k], relay_from
        )
        to_relay.start()
        to_other.start()
        load = pltpu.make_async_copy(block(relay_to, k), own_buf.at[k], local_sem.at[k])
        load.start()
        sends += [to_relay, to_other]
        loads.append(load)
    forwards = []
    for k in range(chunks):
        sends[2 * k].wait_recv()
        loads[k].wait()
        sum_buf[k] = (
            own_buf[k].astype(jnp.float32) + relay_buf[k].astype(jnp.float32)
        ).astype(sum_buf.dtype)
        forward = copy(sum_buf.at[k], part(recv_ref.at[0], k), send_sem.at[2, k], recv_sem.at[0, k], relay_to)
        forward.start()
        forwards.append(forward)
    for k in range(chunks):
        sends[2 * k + 1].wait_recv()
        forwards[k].wait_recv()
    for c in sends + forwards:
        c.wait_send()


def ring_reduce_scatter_add(p, collective_id, chunks=1):
    texts, all_rows, width = p.shape
    n = lax.axis_size("tp")
    rows = all_rows // n
    step = rows // chunks
    buf = pltpu.VMEM((chunks, texts, step, width), p.dtype)
    return pl.pallas_call(
        functools.partial(_scatter_add_kernel, chunks),
        out_shape=jax.ShapeDtypeStruct((2, texts, rows, width), p.dtype),
        in_specs=[pl.BlockSpec(memory_space=pl.ANY)],
        out_specs=pl.BlockSpec(memory_space=pl.ANY),
        scratch_shapes=[
            pltpu.SemaphoreType.DMA((3, chunks)),
            pltpu.SemaphoreType.DMA((2, chunks)),
            pltpu.SemaphoreType.DMA((chunks,)),
            pltpu.SemaphoreType.DMA((chunks,)),
            buf,
            buf,
            buf,
        ],
        compiler_params=pltpu.CompilerParams(collective_id=collective_id, has_side_effects=True),
    )(p)


def _peer_id(axes, peer):
    if axes == ("tp",):
        return (lax.axis_index("req"), peer)
    if axes == ("req",):
        return (peer, lax.axis_index("tp"))
    n_tp = lax.axis_size("tp")
    return (peer // n_tp, peer % n_tp)


def _direct_kernel(axes, scatter, x_ref, out_ref, send_sem, recv_sem, local_sem):
    n = out_ref.shape[0]
    me = lax.axis_index(axes)
    barrier = pltpu.get_barrier_semaphore()

    def greet(d, carry):
        peer = (me + d) % n
        pl.semaphore_signal(barrier, inc=1, device_id=_peer_id(axes, peer), device_id_type=MESH_ID)
        return carry

    lax.fori_loop(1, n, greet, 0)
    pl.semaphore_wait(barrier, n - 1)

    def source(peer):
        return x_ref.at[peer] if scatter else x_ref

    local = pltpu.make_async_copy(source(me), out_ref.at[me], local_sem)
    local.start()

    def send(d, carry):
        peer = (me + d) % n
        pltpu.make_async_remote_copy(
            source(peer), out_ref.at[me], send_sem.at[d], recv_sem.at[me],
            device_id=_peer_id(axes, peer), device_id_type=MESH_ID,
        ).start()
        return carry

    lax.fori_loop(1, n, send, 0)

    def receive(d, carry):
        src = (me + n - d) % n
        pltpu.make_async_remote_copy(
            source(src), out_ref.at[src], send_sem.at[d], recv_sem.at[src],
            device_id=_peer_id(axes, src), device_id_type=MESH_ID,
        ).wait_recv()
        return carry

    lax.fori_loop(1, n, receive, 0)

    def sent(d, carry):
        peer = (me + d) % n
        pltpu.make_async_remote_copy(
            source(peer), out_ref.at[me], send_sem.at[d], recv_sem.at[me],
            device_id=_peer_id(axes, peer), device_id_type=MESH_ID,
        ).wait_send()
        return carry

    lax.fori_loop(1, n, sent, 0)
    local.wait()


def direct_exchange(x, axes, collective_id, scatter=False):
    n = 1
    for name in axes:
        n *= lax.axis_size(name)
    block = x.shape[1:] if scatter else x.shape
    return pl.pallas_call(
        functools.partial(_direct_kernel, axes, scatter),
        out_shape=jax.ShapeDtypeStruct((n,) + block, x.dtype),
        in_specs=[pl.BlockSpec(memory_space=pl.ANY)],
        out_specs=pl.BlockSpec(memory_space=pl.ANY),
        scratch_shapes=[
            pltpu.SemaphoreType.DMA((n,)),
            pltpu.SemaphoreType.DMA((n,)),
            pltpu.SemaphoreType.DMA,
        ],
        compiler_params=pltpu.CompilerParams(collective_id=collective_id, has_side_effects=True),
    )(x)


HEAD_DIM = 64
RING_CHUNKS = 4
SPARSE_PAIRS = 64
WINDOW = 512


layer_eps = 1e-05
norm_eps = 1e-06


def layer_norm(values, gain, shift):
    centre = values - jnp.mean(values, axis=-1, keepdims=True)
    spread = jnp.mean(centre * centre, axis=-1, keepdims=True)
    return centre * lax.rsqrt(spread + layer_eps) * gain + shift


def window_attention(queries_h, keys_h, values_h, lengths):
    seq_len = queries_h.shape[1]
    half_window = WINDOW // 2
    scale_factor = HEAD_DIM ** (-0.5)
    pos = jnp.arange(seq_len, dtype=jnp.int32)
    near = jnp.abs(pos[:, None] - pos[None, :]) <= half_window
    keep_mask = near[None] & (pos[None, None, :] < lengths[:, None, None])
    logits = (
        jnp.einsum("tqhe,tkhe->thqk", queries_h, keys_h, preferred_element_type=jnp.float32)
        * scale_factor
    )
    logits = jnp.where(keep_mask[:, None], logits, jnp.float32(-1e30))
    top_val = jnp.max(logits, axis=-1, keepdims=True)
    expo = jnp.exp(logits - top_val)
    attn_weights = (expo / jnp.sum(expo, axis=-1, keepdims=True)).astype(jnp.bfloat16)
    context = jnp.einsum(
        "thqk,tkhe->tqhe", attn_weights, values_h, preferred_element_type=jnp.float32
    )
    context = jnp.where(
        (pos[None, :] < lengths[:, None])[:, :, None, None], context, jnp.float32(0.0)
    )
    return context.astype(jnp.bfloat16).reshape(
        queries_h.shape[0], seq_len, queries_h.shape[2] * HEAD_DIM
    )


def per_device(
    states,
    lengths,
    w_qkv,
    b_qkv,
    w_out,
    b_out,
    ln1_gain,
    ln1_shift,
    w_up,
    b_up,
    w_down,
    b_down,
    ln2_gain,
    ln2_shift,
    index_rows,
    cand_ids,
):
    tp_count = lax.axis_size("tp")
    tp_rank = lax.axis_index("tp")
    req_count = lax.axis_size("req")
    req_rank = lax.axis_index("req")
    text_count, row_share, model_width = states.shape
    quarter = cand_ids.shape[1]
    full_states = ring_all_gather(states, 0, RING_CHUNKS)
    device_count = req_count * tp_count
    seq_len = full_states.shape[1]
    local_width = w_qkv.shape[2]
    heads_here = local_width // HEAD_DIM
    projected = (
        jnp.einsum("tsd,dce->tsce", full_states, w_qkv, preferred_element_type=jnp.float32) + b_qkv
    ).astype(jnp.bfloat16)
    queries_h = projected[:, :, 0].reshape(text_count, seq_len, heads_here, HEAD_DIM)
    keys_h = projected[:, :, 1].reshape(text_count, seq_len, heads_here, HEAD_DIM)
    values_h = projected[:, :, 2].reshape(text_count, seq_len, heads_here, HEAD_DIM)

    context = window_attention(queries_h, keys_h, values_h, lengths)
    partial_value = jnp.einsum("tsk,kd->tsd", context, w_out, preferred_element_type=jnp.float32)
    partial_value = partial_value.astype(jnp.bfloat16)
    attn_recv = ring_reduce_scatter_add(partial_value, 1, RING_CHUNKS)
    attn_sum = lax.dynamic_slice_in_dim(partial_value, tp_rank * row_share, row_share, 1).astype(
        jnp.float32
    ) + jnp.sum(attn_recv.astype(jnp.float32), axis=0)
    normed_local = layer_norm(
        states.astype(jnp.float32) + attn_sum + b_out, ln1_gain, ln1_shift
    ).astype(jnp.bfloat16)
    normed_full = ring_all_gather(normed_local, 2, RING_CHUNKS)
    up_act = jax.nn.gelu(
        jnp.einsum("tsd,df->tsf", normed_full, w_up, preferred_element_type=jnp.float32) + b_up,
        approximate=False,
    ).astype(jnp.bfloat16)
    up_act = lax.optimization_barrier(up_act)
    down_part = jnp.einsum(
        "tsf,fd->tsd", up_act, w_down, preferred_element_type=jnp.float32
    ).astype(jnp.bfloat16)
    down_recv = ring_reduce_scatter_add(down_part, 3, RING_CHUNKS)
    down_sum = lax.dynamic_slice_in_dim(down_part, tp_rank * row_share, row_share, 1).astype(
        jnp.float32
    ) + jnp.sum(down_recv.astype(jnp.float32), axis=0)
    hidden_out = layer_norm(
        normed_local.astype(jnp.float32) + down_sum + b_down, ln2_gain, ln2_shift
    ).astype(jnp.bfloat16)
    positions = tp_rank * row_share + jnp.arange(row_share, dtype=jnp.int32)
    is_valid = positions[None, :] < lengths[:, None]
    local_pool = jnp.sum(
        jnp.where(is_valid[:, :, None], hidden_out.astype(jnp.float32), jnp.float32(0.0)), axis=1
    )
    pool_and_ids = direct_exchange(
        jnp.concatenate([local_pool, cand_ids.astype(jnp.float32)], axis=1), ("tp",), 5
    )
    text_ids = jnp.swapaxes(pool_and_ids[:, :, model_width:], 0, 1)
    pooled = jnp.sum(pool_and_ids[:, :, :model_width], axis=0) / lengths.astype(
        jnp.float32
    )[:, None]
    query_vec = (
        pooled * lax.rsqrt(jnp.mean(pooled * pooled, axis=-1, keepdims=True) + norm_eps)
    ).astype(jnp.bfloat16)
    bundle = jnp.concatenate(
        [query_vec.astype(jnp.float32), text_ids.reshape(text_count, -1)], axis=1
    )
    bundle = direct_exchange(bundle, ("req",), 6).reshape(req_count * text_count, bundle.shape[1])
    all_queries = bundle[:, :model_width].astype(jnp.bfloat16)
    all_ids = bundle[:, model_width:].astype(jnp.int32)
    rows_here = index_rows.shape[0]
    first_row = (req_rank * tp_count + tp_rank) * rows_here
    local_ids = all_ids - first_row
    is_owned = (local_ids >= 0) & (local_ids < rows_here)
    safe_ids = jnp.clip(local_ids, 0, rows_here - 1)
    owned_count = jnp.sum(is_owned.astype(jnp.int32))

    def few_owned(_):
        flat_owned = is_owned.reshape(-1)
        owned_int = is_owned.astype(jnp.int32)
        row_counts = jnp.cumsum(owned_int, axis=1)
        row_totals = row_counts[:, -1]
        running = (row_counts + (jnp.cumsum(row_totals) - row_totals)[:, None]).reshape(-1)
        rank = jnp.arange(SPARSE_PAIRS, dtype=jnp.int32)
        chosen = flat_owned[None, :] & (running[None, :] == rank[:, None] + 1)
        pair_index = jnp.arange(flat_owned.shape[0], dtype=jnp.int32)
        pair_at = jnp.sum(jnp.where(chosen, pair_index[None, :], 0), axis=1)
        row_of = jnp.sum(jnp.where(chosen, safe_ids.reshape(-1)[None, :], 0), axis=1)
        row_pick = jnp.arange(rows_here, dtype=jnp.int32)[None, :] == row_of[:, None]
        rows = jnp.dot(row_pick.astype(index_rows.dtype), index_rows, preferred_element_type=jnp.float32)
        text_of = pair_at // all_ids.shape[1]
        text_pick = jnp.arange(all_queries.shape[0], dtype=jnp.int32)[None, :] == text_of[:, None]
        queries = jnp.dot(
            text_pick.astype(all_queries.dtype), all_queries, preferred_element_type=jnp.float32
        )
        values = jnp.sum(rows.astype(jnp.float32) * queries.astype(jnp.float32), axis=-1)
        return jnp.sum(
            jnp.where(chosen, values[:, None], jnp.float32(0.0)), axis=0
        ).reshape(all_ids.shape)

    def many_owned(_):
        all_scores = jnp.einsum(
            "td,rd->tr", all_queries, index_rows, preferred_element_type=jnp.float32
        )
        score_rows = jnp.take(all_scores.T, safe_ids.reshape(-1), axis=0).reshape(
            safe_ids.shape[0], safe_ids.shape[1], safe_ids.shape[0]
        )
        picked = jnp.einsum("tct->tc", score_rows)
        return jnp.where(is_owned, picked, jnp.float32(0.0))

    owner_terms = lax.cond(owned_count <= SPARSE_PAIRS, few_owned, many_owned, None)
    owner_terms = (
        owner_terms.reshape(req_count, text_count, tp_count, quarter)
        .transpose(0, 2, 1, 3)
        .reshape(device_count, text_count, quarter)
    )
    scores = jnp.sum(lax.all_to_all(owner_terms, ("req", "tp"), 0, 0, tiled=True), axis=0)
    return (hidden_out, scores)


def solution(mesh):
    placed = (
        P("req", "tp", None),
        P("req"),
        P(None, None, "tp"),
        P(None, "tp"),
        P("tp", None),
        P(),
        P(),
        P(),
        P(None, "tp"),
        P("tp"),
        P("tp", None),
        P(),
        P(),
        P(),
        P(("req", "tp"), None),
        P("req", "tp"),
    )
    return jax.shard_map(
        per_device,
        mesh=mesh,
        in_specs=placed,
        out_specs=(P("req", "tp", None), P("req", "tp")),
        check_vma=False,
    )
```

```python
import functools
import jax
import jax.numpy as jnp
from jax import lax
from jax.experimental import pallas as pl
from jax.experimental.pallas import tpu as pltpu
from jax.sharding import PartitionSpec as P

MESH_ID = pl.DeviceIdType.MESH


def _ring_peers():
    n = lax.axis_size("tp")
    me = lax.axis_index("tp")
    rq = lax.axis_index("req")
    core = rq % 2
    right = (me + 1) % n
    left = (me + n - 1) % n
    opp = (me + 2) % n
    relay_to = (me + 1 + 2 * core) % n
    relay_from = (me + n - 1 - 2 * core) % n
    barrier = pltpu.get_barrier_semaphore()
    for peer in (left, right):
        pl.semaphore_signal(barrier, inc=1, device_id=(rq, peer), device_id_type=MESH_ID)
    pl.semaphore_wait(barrier, 2)
    return me, rq, core, right, left, opp, relay_to, relay_from


def _gather_kernel(chunks, x_ref, out_ref, send_sem, recv_sem):
    me, rq, core, right, left, opp, relay_to, relay_from = _ring_peers()
    rows = x_ref.shape[1]
    step = rows // chunks

    def part(ref, k):
        return ref.at[:, pl.ds(k * step, step), :]

    def slot(src, k):
        return out_ref.at[:, pl.ds(src * rows + k * step, step), :]

    def copy(src, dst, send, recv, peer):
        return pltpu.make_async_remote_copy(
            src, dst, send, recv, device_id=(rq, peer), device_id_type=MESH_ID
        )

    sends = []
    for k in range(chunks):
        to_right = copy(part(x_ref, k), slot(me, k), send_sem.at[0, k], recv_sem.at[0, k], right)
        to_left = copy(part(x_ref, k), slot(me, k), send_sem.at[1, k], recv_sem.at[1, k], left)
        to_right.start()
        to_left.start()
        sends += [to_right, to_left]
    for k in range(chunks):
        copy(part(x_ref, k), slot(relay_from, k), send_sem.at[2, k], recv_sem.at[core, k], right).wait_recv()
        forward = copy(
            slot(relay_from, k), slot(relay_from, k), send_sem.at[2, k], recv_sem.at[2, k], relay_to
        )
        forward.start()
        sends.append(forward)
    other_side = (me + 1 + 2 * (1 - core)) % lax.axis_size("tp")
    for k in range(chunks):
        copy(part(x_ref, k), slot(other_side, k), send_sem.at[0, k], recv_sem.at[1 - core, k], right).wait_recv()
    for k in range(chunks):
        copy(part(x_ref, k), slot(opp, k), send_sem.at[0, k], recv_sem.at[2, k], right).wait_recv()
    for c in sends:
        c.wait_send()


def ring_all_gather(x, collective_id, chunks=1):
    texts, rows, width = x.shape
    n = lax.axis_size("tp")
    gathered = pl.pallas_call(
        functools.partial(_gather_kernel, chunks),
        out_shape=jax.ShapeDtypeStruct((texts, n * rows, width), x.dtype),
        in_specs=[pl.BlockSpec(memory_space=pl.ANY)],
        out_specs=pl.BlockSpec(memory_space=pl.ANY),
        scratch_shapes=[
            pltpu.SemaphoreType.DMA((3, chunks)),
            pltpu.SemaphoreType.DMA((3, chunks)),
        ],
        compiler_params=pltpu.CompilerParams(collective_id=collective_id, has_side_effects=True),
    )(x)
    me = lax.axis_index("tp")
    return lax.dynamic_update_slice_in_dim(gathered, x, me * rows, 1)


def _scatter_add_kernel(chunks, p_ref, recv_ref, send_sem, recv_sem, relay_sem, local_sem,
                        own_buf, relay_buf, sum_buf):
    me, rq, core, right, left, opp, relay_to, relay_from = _ring_peers()
    rows = recv_ref.shape[2]
    step = rows // chunks

    def block(dst, k):
        return p_ref.at[:, pl.ds(dst * rows + k * step, step), :]

    def part(ref, k):
        return ref.at[:, pl.ds(k * step, step), :]

    def copy(src, dst, send, recv, peer):
        return pltpu.make_async_remote_copy(
            src, dst, send, recv, device_id=(rq, peer), device_id_type=MESH_ID
        )

    sends = []
    loads = []
    for k in range(chunks):
        to_relay = copy(block(opp, k), relay_buf.at[k], send_sem.at[0, k], relay_sem.at[k], relay_to)
        to_other = copy(
            block(relay_from, k), part(recv_ref.at[1], k), send_sem.at[1, k], recv_sem.at[1, k], relay_from
        )
        to_relay.start()
        to_other.start()
        load = pltpu.make_async_copy(block(relay_to, k), own_buf.at[k], local_sem.at[k])
        load.start()
        sends += [to_relay, to_other]
        loads.append(load)
    forwards = []
    for k in range(chunks):
        sends[2 * k].wait_recv()
        loads[k].wait()
        sum_buf[k] = (
            own_buf[k].astype(jnp.float32) + relay_buf[k].astype(jnp.float32)
        ).astype(sum_buf.dtype)
        forward = copy(sum_buf.at[k], part(recv_ref.at[0], k), send_sem.at[2, k], recv_sem.at[0, k], relay_to)
        forward.start()
        forwards.append(forward)
    for k in range(chunks):
        sends[2 * k + 1].wait_recv()
        forwards[k].wait_recv()
    for c in sends + forwards:
        c.wait_send()


def ring_reduce_scatter_add(p, collective_id, chunks=1):
    texts, all_rows, width = p.shape
    n = lax.axis_size("tp")
    rows = all_rows // n
    step = rows // chunks
    buf = pltpu.VMEM((chunks, texts, step, width), p.dtype)
    return pl.pallas_call(
        functools.partial(_scatter_add_kernel, chunks),
        out_shape=jax.ShapeDtypeStruct((2, texts, rows, width), p.dtype),
        in_specs=[pl.BlockSpec(memory_space=pl.ANY)],
        out_specs=pl.BlockSpec(memory_space=pl.ANY),
        scratch_shapes=[
            pltpu.SemaphoreType.DMA((3, chunks)),
            pltpu.SemaphoreType.DMA((2, chunks)),
            pltpu.SemaphoreType.DMA((chunks,)),
            pltpu.SemaphoreType.DMA((chunks,)),
            buf,
            buf,
            buf,
        ],
        compiler_params=pltpu.CompilerParams(collective_id=collective_id, has_side_effects=True),
    )(p)


def _peer_id(axes, peer):
    if axes == ("tp",):
        return (lax.axis_index("req"), peer)
    if axes == ("req",):
        return (peer, lax.axis_index("tp"))
    n_tp = lax.axis_size("tp")
    return (peer // n_tp, peer % n_tp)


def _direct_kernel(axes, scatter, x_ref, out_ref, send_sem, recv_sem, local_sem):
    n = out_ref.shape[0]
    me = lax.axis_index(axes)
    barrier = pltpu.get_barrier_semaphore()

    def greet(d, carry):
        peer = (me + d) % n
        pl.semaphore_signal(barrier, inc=1, device_id=_peer_id(axes, peer), device_id_type=MESH_ID)
        return carry

    lax.fori_loop(1, n, greet, 0)
    pl.semaphore_wait(barrier, n - 1)

    def source(peer):
        return x_ref.at[peer] if scatter else x_ref

    local = pltpu.make_async_copy(source(me), out_ref.at[me], local_sem)
    local.start()

    def send(d, carry):
        peer = (me + d) % n
        pltpu.make_async_remote_copy(
            source(peer), out_ref.at[me], send_sem.at[d], recv_sem.at[me],
            device_id=_peer_id(axes, peer), device_id_type=MESH_ID,
        ).start()
        return carry

    lax.fori_loop(1, n, send, 0)

    def receive(d, carry):
        src = (me + n - d) % n
        pltpu.make_async_remote_copy(
            source(src), out_ref.at[src], send_sem.at[d], recv_sem.at[src],
            device_id=_peer_id(axes, src), device_id_type=MESH_ID,
        ).wait_recv()
        return carry

    lax.fori_loop(1, n, receive, 0)

    def sent(d, carry):
        peer = (me + d) % n
        pltpu.make_async_remote_copy(
            source(peer), out_ref.at[me], send_sem.at[d], recv_sem.at[me],
            device_id=_peer_id(axes, peer), device_id_type=MESH_ID,
        ).wait_send()
        return carry

    lax.fori_loop(1, n, sent, 0)
    local.wait()


def direct_exchange(x, axes, collective_id, scatter=False):
    n = 1
    for name in axes:
        n *= lax.axis_size(name)
    block = x.shape[1:] if scatter else x.shape
    return pl.pallas_call(
        functools.partial(_direct_kernel, axes, scatter),
        out_shape=jax.ShapeDtypeStruct((n,) + block, x.dtype),
        in_specs=[pl.BlockSpec(memory_space=pl.ANY)],
        out_specs=pl.BlockSpec(memory_space=pl.ANY),
        scratch_shapes=[
            pltpu.SemaphoreType.DMA((n,)),
            pltpu.SemaphoreType.DMA((n,)),
            pltpu.SemaphoreType.DMA,
        ],
        compiler_params=pltpu.CompilerParams(collective_id=collective_id, has_side_effects=True),
    )(x)


HEAD_DIM = 64
RING_CHUNKS = 4
SPARSE_PAIRS = 64
WINDOW = 512


layer_eps = 1e-05
norm_eps = 1e-06


def layer_norm(values, gain, shift):
    centre = values - jnp.mean(values, axis=-1, keepdims=True)
    spread = jnp.mean(centre * centre, axis=-1, keepdims=True)
    return centre * lax.rsqrt(spread + layer_eps) * gain + shift


def window_attention(queries_h, keys_h, values_h, lengths):
    seq_len = queries_h.shape[1]
    half_window = WINDOW // 2
    scale_factor = HEAD_DIM ** (-0.5)
    pos = jnp.arange(seq_len, dtype=jnp.int32)
    near = jnp.abs(pos[:, None] - pos[None, :]) <= half_window
    keep_mask = near[None] & (pos[None, None, :] < lengths[:, None, None])
    logits = (
        jnp.einsum("tqhe,tkhe->thqk", queries_h, keys_h, preferred_element_type=jnp.float32)
        * scale_factor
    )
    logits = jnp.where(keep_mask[:, None], logits, jnp.float32(-1e30))
    top_val = jnp.max(logits, axis=-1, keepdims=True)
    expo = jnp.exp(logits - top_val)
    attn_weights = (expo / jnp.sum(expo, axis=-1, keepdims=True)).astype(jnp.bfloat16)
    context = jnp.einsum(
        "thqk,tkhe->tqhe", attn_weights, values_h, preferred_element_type=jnp.float32
    )
    context = jnp.where(
        (pos[None, :] < lengths[:, None])[:, :, None, None], context, jnp.float32(0.0)
    )
    return context.astype(jnp.bfloat16).reshape(
        queries_h.shape[0], seq_len, queries_h.shape[2] * HEAD_DIM
    )


def per_device(
    states,
    lengths,
    w_qkv,
    b_qkv,
    w_out,
    b_out,
    ln1_gain,
    ln1_shift,
    w_up,
    b_up,
    w_down,
    b_down,
    ln2_gain,
    ln2_shift,
    index_rows,
    cand_ids,
):
    tp_count = lax.axis_size("tp")
    tp_rank = lax.axis_index("tp")
    req_count = lax.axis_size("req")
    req_rank = lax.axis_index("req")
    text_count, row_share, model_width = states.shape
    quarter = cand_ids.shape[1]
    full_states = ring_all_gather(states, 0, RING_CHUNKS)
    device_count = req_count * tp_count
    seq_len = full_states.shape[1]
    local_width = w_qkv.shape[2]
    heads_here = local_width // HEAD_DIM
    projected = (
        jnp.einsum("tsd,dce->tsce", full_states, w_qkv, preferred_element_type=jnp.float32) + b_qkv
    ).astype(jnp.bfloat16)
    queries_h = projected[:, :, 0].reshape(text_count, seq_len, heads_here, HEAD_DIM)
    keys_h = projected[:, :, 1].reshape(text_count, seq_len, heads_here, HEAD_DIM)
    values_h = projected[:, :, 2].reshape(text_count, seq_len, heads_here, HEAD_DIM)

    context = window_attention(queries_h, keys_h, values_h, lengths)
    partial_value = jnp.einsum("tsk,kd->tsd", context, w_out, preferred_element_type=jnp.float32)
    partial_value = partial_value.astype(jnp.bfloat16)
    attn_recv = ring_reduce_scatter_add(partial_value, 1, RING_CHUNKS)
    attn_sum = lax.dynamic_slice_in_dim(partial_value, tp_rank * row_share, row_share, 1).astype(
        jnp.float32
    ) + jnp.sum(attn_recv.astype(jnp.float32), axis=0)
    normed_local = layer_norm(
        states.astype(jnp.float32) + attn_sum + b_out, ln1_gain, ln1_shift
    ).astype(jnp.bfloat16)
    normed_full = ring_all_gather(normed_local, 2, RING_CHUNKS)
    up_act = jax.nn.gelu(
        jnp.einsum("tsd,df->tsf", normed_full, w_up, preferred_element_type=jnp.float32) + b_up,
        approximate=False,
    ).astype(jnp.bfloat16)
    up_act = lax.optimization_barrier(up_act)
    down_part = jnp.einsum(
        "tsf,fd->tsd", up_act, w_down, preferred_element_type=jnp.float32
    ).astype(jnp.bfloat16)
    down_recv = ring_reduce_scatter_add(down_part, 3, RING_CHUNKS)
    down_sum = lax.dynamic_slice_in_dim(down_part, tp_rank * row_share, row_share, 1).astype(
        jnp.float32
    ) + jnp.sum(down_recv.astype(jnp.float32), axis=0)
    hidden_out = layer_norm(
        normed_local.astype(jnp.float32) + down_sum + b_down, ln2_gain, ln2_shift
    ).astype(jnp.bfloat16)
    positions = tp_rank * row_share + jnp.arange(row_share, dtype=jnp.int32)
    is_valid = positions[None, :] < lengths[:, None]
    local_pool = jnp.sum(
        jnp.where(is_valid[:, :, None], hidden_out.astype(jnp.float32), jnp.float32(0.0)), axis=1
    )
    pool_and_ids = direct_exchange(
        jnp.concatenate([local_pool, cand_ids.astype(jnp.float32)], axis=1), ("tp",), 5
    )
    text_ids = jnp.swapaxes(pool_and_ids[:, :, model_width:], 0, 1)
    pooled = jnp.sum(pool_and_ids[:, :, :model_width], axis=0) / lengths.astype(
        jnp.float32
    )[:, None]
    query_vec = (
        pooled * lax.rsqrt(jnp.mean(pooled * pooled, axis=-1, keepdims=True) + norm_eps)
    ).astype(jnp.bfloat16)
    bundle = jnp.concatenate(
        [query_vec.astype(jnp.float32), text_ids.reshape(text_count, -1)], axis=1
    )
    bundle = direct_exchange(bundle, ("req",), 6).reshape(req_count * text_count, bundle.shape[1])
    all_queries = bundle[:, :model_width].astype(jnp.bfloat16)
    all_ids = bundle[:, model_width:].astype(jnp.int32)
    rows_here = index_rows.shape[0]
    first_row = (req_rank * tp_count + tp_rank) * rows_here
    local_ids = all_ids - first_row
    is_owned = (local_ids >= 0) & (local_ids < rows_here)
    safe_ids = jnp.clip(local_ids, 0, rows_here - 1)
    owned_count = jnp.sum(is_owned.astype(jnp.int32))

    def few_owned(_):
        flat_owned = is_owned.reshape(-1)
        owned_int = is_owned.astype(jnp.int32)
        row_counts = jnp.cumsum(owned_int, axis=1)
        row_totals = row_counts[:, -1]
        running = (row_counts + (jnp.cumsum(row_totals) - row_totals)[:, None]).reshape(-1)
        rank = jnp.arange(SPARSE_PAIRS, dtype=jnp.int32)
        chosen = flat_owned[None, :] & (running[None, :] == rank[:, None] + 1)
        pair_index = jnp.arange(flat_owned.shape[0], dtype=jnp.int32)
        pair_at = jnp.sum(jnp.where(chosen, pair_index[None, :], 0), axis=1)
        row_of = jnp.sum(jnp.where(chosen, safe_ids.reshape(-1)[None, :], 0), axis=1)
        row_pick = jnp.arange(rows_here, dtype=jnp.int32)[None, :] == row_of[:, None]
        rows = jnp.dot(row_pick.astype(index_rows.dtype), index_rows, preferred_element_type=jnp.float32)
        text_of = pair_at // all_ids.shape[1]
        text_pick = jnp.arange(all_queries.shape[0], dtype=jnp.int32)[None, :] == text_of[:, None]
        queries = jnp.dot(
            text_pick.astype(all_queries.dtype), all_queries, preferred_element_type=jnp.float32
        )
        values = jnp.sum(rows.astype(jnp.float32) * queries.astype(jnp.float32), axis=-1)
        return jnp.sum(
            jnp.where(chosen, values[:, None], jnp.float32(0.0)), axis=0
        ).reshape(all_ids.shape)

    def many_owned(_):
        all_scores = jnp.einsum(
            "td,rd->tr", all_queries, index_rows, preferred_element_type=jnp.float32
        )
        score_rows = jnp.take(all_scores.T, safe_ids.reshape(-1), axis=0).reshape(
            safe_ids.shape[0], safe_ids.shape[1], safe_ids.shape[0]
        )
        picked = jnp.einsum("tct->tc", score_rows)
        return jnp.where(is_owned, picked, jnp.float32(0.0))

    owner_terms = lax.cond(owned_count <= SPARSE_PAIRS, few_owned, many_owned, None)
    owner_terms = (
        owner_terms.reshape(req_count, text_count, tp_count, quarter)
        .transpose(0, 2, 1, 3)
        .reshape(device_count, text_count, quarter)
    )
    scores = jnp.sum(lax.all_to_all(owner_terms, ("req", "tp"), 0, 0, tiled=True), axis=0)
    return (hidden_out, scores)


def solution(mesh):
    placed = (
        P("req", "tp", None),
        P("req"),
        P(None, None, "tp"),
        P(None, "tp"),
        P("tp", None),
        P(),
        P(),
        P(),
        P(None, "tp"),
        P("tp"),
        P("tp", None),
        P(),
        P(),
        P(),
        P(("req", "tp"), None),
        P("req", "tp"),
    )
    return jax.shard_map(
        per_device,
        mesh=mesh,
        in_specs=placed,
        out_specs=(P("req", "tp", None), P("req", "tp")),
        check_vma=False,
    )
```

```python
import functools
import jax
import jax.numpy as jnp
from jax import lax
from jax.experimental import pallas as pl
from jax.experimental.pallas import tpu as pltpu
from jax.sharding import PartitionSpec as P

MESH_ID = pl.DeviceIdType.MESH


def _ring_peers():
    n = lax.axis_size("tp")
    me = lax.axis_index("tp")
    rq = lax.axis_index("req")
    core = rq % 2
    right = (me + 1) % n
    left = (me + n - 1) % n
    opp = (me + 2) % n
    relay_to = (me + 1 + 2 * core) % n
    relay_from = (me + n - 1 - 2 * core) % n
    barrier = pltpu.get_barrier_semaphore()
    for peer in (left, right):
        pl.semaphore_signal(barrier, inc=1, device_id=(rq, peer), device_id_type=MESH_ID)
    pl.semaphore_wait(barrier, 2)
    return me, rq, core, right, left, opp, relay_to, relay_from


def _gather_kernel(chunks, x_ref, out_ref, send_sem, recv_sem, local_sem):
    me, rq, core, right, left, opp, relay_to, relay_from = _ring_peers()
    rows = x_ref.shape[1]
    step = rows // chunks

    def part(ref, k):
        return ref.at[:, pl.ds(k * step, step), :]

    def slot(src, k):
        return out_ref.at[:, pl.ds(src * rows + k * step, step), :]

    def copy(src, dst, send, recv, peer):
        return pltpu.make_async_remote_copy(
            src, dst, send, recv, device_id=(rq, peer), device_id_type=MESH_ID
        )

    local = pltpu.make_async_copy(x_ref, out_ref.at[:, pl.ds(me * rows, rows), :], local_sem)
    local.start()
    sends = []
    for k in range(chunks):
        to_right = copy(part(x_ref, k), slot(me, k), send_sem.at[0, k], recv_sem.at[0, k], right)
        to_left = copy(part(x_ref, k), slot(me, k), send_sem.at[1, k], recv_sem.at[1, k], left)
        to_right.start()
        to_left.start()
        sends += [to_right, to_left]
    for k in range(chunks):
        copy(part(x_ref, k), slot(relay_from, k), send_sem.at[2, k], recv_sem.at[core, k], right).wait_recv()
        forward = copy(
            slot(relay_from, k), slot(relay_from, k), send_sem.at[2, k], recv_sem.at[2, k], relay_to
        )
        forward.start()
        sends.append(forward)
    other_side = (me + 1 + 2 * (1 - core)) % lax.axis_size("tp")
    for k in range(chunks):
        copy(part(x_ref, k), slot(other_side, k), send_sem.at[0, k], recv_sem.at[1 - core, k], right).wait_recv()
    for k in range(chunks):
        copy(part(x_ref, k), slot(opp, k), send_sem.at[0, k], recv_sem.at[2, k], right).wait_recv()
    for c in sends:
        c.wait_send()
    local.wait()


def ring_all_gather(x, collective_id, chunks=1):
    texts, rows, width = x.shape
    n = lax.axis_size("tp")
    return pl.pallas_call(
        functools.partial(_gather_kernel, chunks),
        out_shape=jax.ShapeDtypeStruct((texts, n * rows, width), x.dtype),
        in_specs=[pl.BlockSpec(memory_space=pl.ANY)],
        out_specs=pl.BlockSpec(memory_space=pl.ANY),
        scratch_shapes=[
            pltpu.SemaphoreType.DMA((3, chunks)),
            pltpu.SemaphoreType.DMA((3, chunks)),
            pltpu.SemaphoreType.DMA,
        ],
        compiler_params=pltpu.CompilerParams(collective_id=collective_id, has_side_effects=True),
    )(x)


def _scatter_add_kernel(chunks, p_ref, recv_ref, send_sem, recv_sem, relay_sem, local_sem,
                        own_buf, relay_buf, sum_buf):
    me, rq, core, right, left, opp, relay_to, relay_from = _ring_peers()
    rows = recv_ref.shape[2]
    step = rows // chunks

    def block(dst, k):
        return p_ref.at[:, pl.ds(dst * rows + k * step, step), :]

    def part(ref, k):
        return ref.at[:, pl.ds(k * step, step), :]

    def copy(src, dst, send, recv, peer):
        return pltpu.make_async_remote_copy(
            src, dst, send, recv, device_id=(rq, peer), device_id_type=MESH_ID
        )

    sends = []
    loads = []
    for k in range(chunks):
        to_relay = copy(block(opp, k), relay_buf.at[k], send_sem.at[0, k], relay_sem.at[k], relay_to)
        to_other = copy(
            block(relay_from, k), part(recv_ref.at[1], k), send_sem.at[1, k], recv_sem.at[1, k], relay_from
        )
        to_relay.start()
        to_other.start()
        load = pltpu.make_async_copy(block(relay_to, k), own_buf.at[k], local_sem.at[k])
        load.start()
        sends += [to_relay, to_other]
        loads.append(load)
    forwards = []
    for k in range(chunks):
        sends[2 * k].wait_recv()
        loads[k].wait()
        sum_buf[k] = (
            own_buf[k].astype(jnp.float32) + relay_buf[k].astype(jnp.float32)
        ).astype(sum_buf.dtype)
        forward = copy(sum_buf.at[k], part(recv_ref.at[0], k), send_sem.at[2, k], recv_sem.at[0, k], relay_to)
        forward.start()
        forwards.append(forward)
    for k in range(chunks):
        sends[2 * k + 1].wait_recv()
        forwards[k].wait_recv()
    for c in sends + forwards:
        c.wait_send()


def ring_reduce_scatter_add(p, collective_id, chunks=1):
    texts, all_rows, width = p.shape
    n = lax.axis_size("tp")
    rows = all_rows // n
    step = rows // chunks
    buf = pltpu.VMEM((chunks, texts, step, width), p.dtype)
    return pl.pallas_call(
        functools.partial(_scatter_add_kernel, chunks),
        out_shape=jax.ShapeDtypeStruct((2, texts, rows, width), p.dtype),
        in_specs=[pl.BlockSpec(memory_space=pl.ANY)],
        out_specs=pl.BlockSpec(memory_space=pl.ANY),
        scratch_shapes=[
            pltpu.SemaphoreType.DMA((3, chunks)),
            pltpu.SemaphoreType.DMA((2, chunks)),
            pltpu.SemaphoreType.DMA((chunks,)),
            pltpu.SemaphoreType.DMA((chunks,)),
            buf,
            buf,
            buf,
        ],
        compiler_params=pltpu.CompilerParams(collective_id=collective_id, has_side_effects=True),
    )(p)


def _peer_id(axes, peer):
    if axes == ("tp",):
        return (lax.axis_index("req"), peer)
    if axes == ("req",):
        return (peer, lax.axis_index("tp"))
    n_tp = lax.axis_size("tp")
    return (peer // n_tp, peer % n_tp)


def _direct_kernel(axes, scatter, x_ref, out_ref, send_sem, recv_sem, local_sem):
    n = out_ref.shape[0]
    me = lax.axis_index(axes)
    barrier = pltpu.get_barrier_semaphore()

    def greet(d, carry):
        peer = (me + d) % n
        pl.semaphore_signal(barrier, inc=1, device_id=_peer_id(axes, peer), device_id_type=MESH_ID)
        return carry

    lax.fori_loop(1, n, greet, 0)
    pl.semaphore_wait(barrier, n - 1)

    def source(peer):
        return x_ref.at[peer] if scatter else x_ref

    local = pltpu.make_async_copy(source(me), out_ref.at[me], local_sem)
    local.start()

    def send(d, carry):
        peer = (me + d) % n
        pltpu.make_async_remote_copy(
            source(peer), out_ref.at[me], send_sem.at[d], recv_sem.at[me],
            device_id=_peer_id(axes, peer), device_id_type=MESH_ID,
        ).start()
        return carry

    lax.fori_loop(1, n, send, 0)

    def receive(d, carry):
        src = (me + n - d) % n
        pltpu.make_async_remote_copy(
            source(src), out_ref.at[src], send_sem.at[d], recv_sem.at[src],
            device_id=_peer_id(axes, src), device_id_type=MESH_ID,
        ).wait_recv()
        return carry

    lax.fori_loop(1, n, receive, 0)

    def sent(d, carry):
        peer = (me + d) % n
        pltpu.make_async_remote_copy(
            source(peer), out_ref.at[me], send_sem.at[d], recv_sem.at[me],
            device_id=_peer_id(axes, peer), device_id_type=MESH_ID,
        ).wait_send()
        return carry

    lax.fori_loop(1, n, sent, 0)
    local.wait()


def direct_exchange(x, axes, collective_id, scatter=False):
    n = 1
    for name in axes:
        n *= lax.axis_size(name)
    block = x.shape[1:] if scatter else x.shape
    return pl.pallas_call(
        functools.partial(_direct_kernel, axes, scatter),
        out_shape=jax.ShapeDtypeStruct((n,) + block, x.dtype),
        in_specs=[pl.BlockSpec(memory_space=pl.ANY)],
        out_specs=pl.BlockSpec(memory_space=pl.ANY),
        scratch_shapes=[
            pltpu.SemaphoreType.DMA((n,)),
            pltpu.SemaphoreType.DMA((n,)),
            pltpu.SemaphoreType.DMA,
        ],
        compiler_params=pltpu.CompilerParams(collective_id=collective_id, has_side_effects=True),
    )(x)


def _row_pick_kernel(ids_ref, rows_hbm, out_hbm, sem):
    count = ids_ref.shape[0]

    def start(k, carry):
        first = pl.multiple_of((ids_ref[k] // ROW_GROUP) * ROW_GROUP, ROW_GROUP)
        pltpu.make_async_copy(
            rows_hbm.at[pl.ds(first, ROW_GROUP)],
            out_hbm.at[pl.ds(pl.multiple_of(k * ROW_GROUP, ROW_GROUP), ROW_GROUP)],
            sem,
        ).start()
        return carry

    lax.fori_loop(0, count, start, 0)
    pltpu.make_async_copy(rows_hbm.at[pl.ds(0, count * ROW_GROUP)], out_hbm, sem).wait()


def pick_rows(rows, ids):
    groups = pl.pallas_call(
        _row_pick_kernel,
        out_shape=jax.ShapeDtypeStruct((ids.shape[0] * ROW_GROUP, rows.shape[1]), rows.dtype),
        grid_spec=pltpu.PrefetchScalarGridSpec(
            num_scalar_prefetch=1,
            grid=(1,),
            in_specs=[pl.BlockSpec(memory_space=pl.ANY)],
            out_specs=pl.BlockSpec(memory_space=pl.ANY),
            scratch_shapes=[pltpu.SemaphoreType.DMA],
        ),
    )(ids, rows).reshape(ids.shape[0], ROW_GROUP, rows.shape[1])
    within = jnp.arange(ROW_GROUP, dtype=jnp.int32)[None, :, None] == (ids % ROW_GROUP)[:, None, None]
    return jnp.sum(jnp.where(within, groups.astype(jnp.float32), jnp.float32(0.0)), axis=1)


HEAD_DIM = 64
RING_CHUNKS = 4
SPARSE_PAIRS = 64
ROW_GROUP = 8
WINDOW = 512


layer_eps = 1e-05
norm_eps = 1e-06


def layer_norm(values, gain, shift):
    centre = values - jnp.mean(values, axis=-1, keepdims=True)
    spread = jnp.mean(centre * centre, axis=-1, keepdims=True)
    return centre * lax.rsqrt(spread + layer_eps) * gain + shift


def window_attention(queries_h, keys_h, values_h, lengths):
    seq_len = queries_h.shape[1]
    half_window = WINDOW // 2
    scale_factor = HEAD_DIM ** (-0.5)
    pos = jnp.arange(seq_len, dtype=jnp.int32)
    near = jnp.abs(pos[:, None] - pos[None, :]) <= half_window
    keep_mask = near[None] & (pos[None, None, :] < lengths[:, None, None])
    logits = (
        jnp.einsum("tqhe,tkhe->thqk", queries_h, keys_h, preferred_element_type=jnp.float32)
        * scale_factor
    )
    logits = jnp.where(keep_mask[:, None], logits, jnp.float32(-1e30))
    top_val = jnp.max(logits, axis=-1, keepdims=True)
    expo = jnp.exp(logits - top_val)
    attn_weights = (expo / jnp.sum(expo, axis=-1, keepdims=True)).astype(jnp.bfloat16)
    context = jnp.einsum(
        "thqk,tkhe->tqhe", attn_weights, values_h, preferred_element_type=jnp.float32
    )
    context = jnp.where(
        (pos[None, :] < lengths[:, None])[:, :, None, None], context, jnp.float32(0.0)
    )
    return context.astype(jnp.bfloat16).reshape(
        queries_h.shape[0], seq_len, queries_h.shape[2] * HEAD_DIM
    )


def per_device(
    states,
    lengths,
    w_qkv,
    b_qkv,
    w_out,
    b_out,
    ln1_gain,
    ln1_shift,
    w_up,
    b_up,
    w_down,
    b_down,
    ln2_gain,
    ln2_shift,
    index_rows,
    cand_ids,
):
    tp_count = lax.axis_size("tp")
    tp_rank = lax.axis_index("tp")
    req_count = lax.axis_size("req")
    req_rank = lax.axis_index("req")
    text_count, row_share, model_width = states.shape
    quarter = cand_ids.shape[1]
    full_states = ring_all_gather(states, 0, RING_CHUNKS)
    device_count = req_count * tp_count
    seq_len = full_states.shape[1]
    local_width = w_qkv.shape[2]
    heads_here = local_width // HEAD_DIM
    projected = (
        jnp.einsum("tsd,dce->tsce", full_states, w_qkv, preferred_element_type=jnp.float32) + b_qkv
    ).astype(jnp.bfloat16)
    queries_h = projected[:, :, 0].reshape(text_count, seq_len, heads_here, HEAD_DIM)
    keys_h = projected[:, :, 1].reshape(text_count, seq_len, heads_here, HEAD_DIM)
    values_h = projected[:, :, 2].reshape(text_count, seq_len, heads_here, HEAD_DIM)

    context = window_attention(queries_h, keys_h, values_h, lengths)
    partial_value = jnp.einsum("tsk,kd->tsd", context, w_out, preferred_element_type=jnp.float32)
    partial_value = partial_value.astype(jnp.bfloat16)
    attn_recv = ring_reduce_scatter_add(partial_value, 1, RING_CHUNKS)
    attn_sum = lax.dynamic_slice_in_dim(partial_value, tp_rank * row_share, row_share, 1).astype(
        jnp.float32
    ) + jnp.sum(attn_recv.astype(jnp.float32), axis=0)
    normed_local = layer_norm(
        states.astype(jnp.float32) + attn_sum + b_out, ln1_gain, ln1_shift
    ).astype(jnp.bfloat16)
    normed_full = ring_all_gather(normed_local, 2, RING_CHUNKS)
    up_act = jax.nn.gelu(
        jnp.einsum("tsd,df->tsf", normed_full, w_up, preferred_element_type=jnp.float32) + b_up,
        approximate=False,
    ).astype(jnp.bfloat16)
    up_act = lax.optimization_barrier(up_act)
    down_part = jnp.einsum(
        "tsf,fd->tsd", up_act, w_down, preferred_element_type=jnp.float32
    ).astype(jnp.bfloat16)
    down_recv = ring_reduce_scatter_add(down_part, 3, RING_CHUNKS)
    down_sum = lax.dynamic_slice_in_dim(down_part, tp_rank * row_share, row_share, 1).astype(
        jnp.float32
    ) + jnp.sum(down_recv.astype(jnp.float32), axis=0)
    hidden_out = layer_norm(
        normed_local.astype(jnp.float32) + down_sum + b_down, ln2_gain, ln2_shift
    ).astype(jnp.bfloat16)
    positions = tp_rank * row_share + jnp.arange(row_share, dtype=jnp.int32)
    is_valid = positions[None, :] < lengths[:, None]
    local_pool = jnp.sum(
        jnp.where(is_valid[:, :, None], hidden_out.astype(jnp.float32), jnp.float32(0.0)), axis=1
    )
    pool_and_ids = direct_exchange(
        jnp.concatenate([local_pool, cand_ids.astype(jnp.float32)], axis=1), ("tp",), 5
    )
    text_ids = jnp.swapaxes(pool_and_ids[:, :, model_width:], 0, 1)
    pooled = jnp.sum(pool_and_ids[:, :, :model_width], axis=0) / lengths.astype(
        jnp.float32
    )[:, None]
    query_vec = (
        pooled * lax.rsqrt(jnp.mean(pooled * pooled, axis=-1, keepdims=True) + norm_eps)
    ).astype(jnp.bfloat16)
    bundle = jnp.concatenate(
        [query_vec.astype(jnp.float32), text_ids.reshape(text_count, -1)], axis=1
    )
    bundle = direct_exchange(bundle, ("req",), 6).reshape(req_count * text_count, bundle.shape[1])
    all_queries = bundle[:, :model_width].astype(jnp.bfloat16)
    all_ids = bundle[:, model_width:].astype(jnp.int32)
    rows_here = index_rows.shape[0]
    first_row = (req_rank * tp_count + tp_rank) * rows_here
    local_ids = all_ids - first_row
    is_owned = (local_ids >= 0) & (local_ids < rows_here)
    safe_ids = jnp.clip(local_ids, 0, rows_here - 1)
    owned_count = jnp.sum(is_owned.astype(jnp.int32))

    def few_owned(_):
        flat_owned = is_owned.reshape(-1)
        owned_int = is_owned.astype(jnp.int32)
        row_counts = jnp.cumsum(owned_int, axis=1)
        row_totals = row_counts[:, -1]
        running = (row_counts + (jnp.cumsum(row_totals) - row_totals)[:, None]).reshape(-1)
        rank = jnp.arange(SPARSE_PAIRS, dtype=jnp.int32)
        chosen = flat_owned[None, :] & (running[None, :] == rank[:, None] + 1)
        pair_index = jnp.arange(flat_owned.shape[0], dtype=jnp.int32)
        pair_at = jnp.sum(jnp.where(chosen, pair_index[None, :], 0), axis=1)
        row_of = jnp.sum(jnp.where(chosen, safe_ids.reshape(-1)[None, :], 0), axis=1)
        rows = pick_rows(index_rows, jnp.clip(row_of, 0, rows_here - 1))
        text_of = pair_at // all_ids.shape[1]
        text_pick = jnp.arange(all_queries.shape[0], dtype=jnp.int32)[None, :] == text_of[:, None]
        queries = jnp.dot(
            text_pick.astype(all_queries.dtype), all_queries, preferred_element_type=jnp.float32
        )
        values = jnp.sum(rows.astype(jnp.float32) * queries.astype(jnp.float32), axis=-1)
        return jnp.sum(
            jnp.where(chosen, values[:, None], jnp.float32(0.0)), axis=0
        ).reshape(all_ids.shape)

    def many_owned(_):
        all_scores = jnp.einsum(
            "td,rd->tr", all_queries, index_rows, preferred_element_type=jnp.float32
        )
        score_rows = jnp.take(all_scores.T, safe_ids.reshape(-1), axis=0).reshape(
            safe_ids.shape[0], safe_ids.shape[1], safe_ids.shape[0]
        )
        picked = jnp.einsum("tct->tc", score_rows)
        return jnp.where(is_owned, picked, jnp.float32(0.0))

    owner_terms = lax.cond(owned_count <= SPARSE_PAIRS, few_owned, many_owned, None)
    owner_terms = (
        owner_terms.reshape(req_count, text_count, tp_count, quarter)
        .transpose(0, 2, 1, 3)
        .reshape(device_count, text_count, quarter)
    )
    scores = jnp.sum(lax.all_to_all(owner_terms, ("req", "tp"), 0, 0, tiled=True), axis=0)
    return (hidden_out, scores)


def solution(mesh):
    placed = (
        P("req", "tp", None),
        P("req"),
        P(None, None, "tp"),
        P(None, "tp"),
        P("tp", None),
        P(),
        P(),
        P(),
        P(None, "tp"),
        P("tp"),
        P("tp", None),
        P(),
        P(),
        P(),
        P(("req", "tp"), None),
        P("req", "tp"),
    )
    return jax.shard_map(
        per_device,
        mesh=mesh,
        in_specs=placed,
        out_specs=(P("req", "tp", None), P("req", "tp")),
        check_vma=False,
    )
```

```python
import functools
import jax
import jax.numpy as jnp
from jax import lax
from jax.experimental import pallas as pl
from jax.experimental.pallas import tpu as pltpu
from jax.sharding import PartitionSpec as P

MESH_ID = pl.DeviceIdType.MESH


def _ring_peers():
    n = lax.axis_size("tp")
    me = lax.axis_index("tp")
    rq = lax.axis_index("req")
    core = rq % 2
    right = (me + 1) % n
    left = (me + n - 1) % n
    opp = (me + 2) % n
    relay_to = (me + 1 + 2 * core) % n
    relay_from = (me + n - 1 - 2 * core) % n
    barrier = pltpu.get_barrier_semaphore()
    for peer in (left, right):
        pl.semaphore_signal(barrier, inc=1, device_id=(rq, peer), device_id_type=MESH_ID)
    pl.semaphore_wait(barrier, 2)
    return me, rq, core, right, left, opp, relay_to, relay_from


def _gather_kernel(chunks, x_ref, out_ref, send_sem, recv_sem, local_sem):
    me, rq, core, right, left, opp, relay_to, relay_from = _ring_peers()
    rows = x_ref.shape[1]
    step = rows // chunks

    def part(ref, k):
        return ref.at[:, pl.ds(k * step, step), :]

    def slot(src, k):
        return out_ref.at[:, pl.ds(src * rows + k * step, step), :]

    def copy(src, dst, send, recv, peer):
        return pltpu.make_async_remote_copy(
            src, dst, send, recv, device_id=(rq, peer), device_id_type=MESH_ID
        )

    local = pltpu.make_async_copy(x_ref, out_ref.at[:, pl.ds(me * rows, rows), :], local_sem)
    local.start()
    sends = []
    for k in range(chunks):
        to_right = copy(part(x_ref, k), slot(me, k), send_sem.at[0, k], recv_sem.at[0, k], right)
        to_left = copy(part(x_ref, k), slot(me, k), send_sem.at[1, k], recv_sem.at[1, k], left)
        to_right.start()
        to_left.start()
        sends += [to_right, to_left]
    for k in range(chunks):
        copy(part(x_ref, k), slot(relay_from, k), send_sem.at[2, k], recv_sem.at[core, k], right).wait_recv()
        forward = copy(
            slot(relay_from, k), slot(relay_from, k), send_sem.at[2, k], recv_sem.at[2, k], relay_to
        )
        forward.start()
        sends.append(forward)
    other_side = (me + 1 + 2 * (1 - core)) % lax.axis_size("tp")
    for k in range(chunks):
        copy(part(x_ref, k), slot(other_side, k), send_sem.at[0, k], recv_sem.at[1 - core, k], right).wait_recv()
    for k in range(chunks):
        copy(part(x_ref, k), slot(opp, k), send_sem.at[0, k], recv_sem.at[2, k], right).wait_recv()
    for c in sends:
        c.wait_send()
    local.wait()


def ring_all_gather(x, collective_id, chunks=1):
    texts, rows, width = x.shape
    n = lax.axis_size("tp")
    return pl.pallas_call(
        functools.partial(_gather_kernel, chunks),
        out_shape=jax.ShapeDtypeStruct((texts, n * rows, width), x.dtype),
        in_specs=[pl.BlockSpec(memory_space=pl.ANY)],
        out_specs=pl.BlockSpec(memory_space=pl.ANY),
        scratch_shapes=[
            pltpu.SemaphoreType.DMA((3, chunks)),
            pltpu.SemaphoreType.DMA((3, chunks)),
            pltpu.SemaphoreType.DMA,
        ],
        compiler_params=pltpu.CompilerParams(collective_id=collective_id, has_side_effects=True),
    )(x)


def _scatter_add_kernel(chunks, p_ref, recv_ref, send_sem, recv_sem, relay_sem, local_sem,
                        own_buf, relay_buf, sum_buf):
    me, rq, core, right, left, opp, relay_to, relay_from = _ring_peers()
    rows = recv_ref.shape[2]
    step = rows // chunks

    def block(dst, k):
        return p_ref.at[:, pl.ds(dst * rows + k * step, step), :]

    def part(ref, k):
        return ref.at[:, pl.ds(k * step, step), :]

    def copy(src, dst, send, recv, peer):
        return pltpu.make_async_remote_copy(
            src, dst, send, recv, device_id=(rq, peer), device_id_type=MESH_ID
        )

    sends = []
    loads = []
    for k in range(chunks):
        to_relay = copy(block(opp, k), relay_buf.at[k], send_sem.at[0, k], relay_sem.at[k], relay_to)
        to_other = copy(
            block(relay_from, k), part(recv_ref.at[1], k), send_sem.at[1, k], recv_sem.at[1, k], relay_from
        )
        to_relay.start()
        to_other.start()
        load = pltpu.make_async_copy(block(relay_to, k), own_buf.at[k], local_sem.at[k])
        load.start()
        sends += [to_relay, to_other]
        loads.append(load)
    forwards = []
    for k in range(chunks):
        sends[2 * k].wait_recv()
        loads[k].wait()
        sum_buf[k] = (
            own_buf[k].astype(jnp.float32) + relay_buf[k].astype(jnp.float32)
        ).astype(sum_buf.dtype)
        forward = copy(sum_buf.at[k], part(recv_ref.at[0], k), send_sem.at[2, k], recv_sem.at[0, k], relay_to)
        forward.start()
        forwards.append(forward)
    for k in range(chunks):
        sends[2 * k + 1].wait_recv()
        forwards[k].wait_recv()
    for c in sends + forwards:
        c.wait_send()


def ring_reduce_scatter_add(p, collective_id, chunks=1):
    texts, all_rows, width = p.shape
    n = lax.axis_size("tp")
    rows = all_rows // n
    step = rows // chunks
    buf = pltpu.VMEM((chunks, texts, step, width), p.dtype)
    return pl.pallas_call(
        functools.partial(_scatter_add_kernel, chunks),
        out_shape=jax.ShapeDtypeStruct((2, texts, rows, width), p.dtype),
        in_specs=[pl.BlockSpec(memory_space=pl.ANY)],
        out_specs=pl.BlockSpec(memory_space=pl.ANY),
        scratch_shapes=[
            pltpu.SemaphoreType.DMA((3, chunks)),
            pltpu.SemaphoreType.DMA((2, chunks)),
            pltpu.SemaphoreType.DMA((chunks,)),
            pltpu.SemaphoreType.DMA((chunks,)),
            buf,
            buf,
            buf,
        ],
        compiler_params=pltpu.CompilerParams(collective_id=collective_id, has_side_effects=True),
    )(p)


def _peer_id(axes, peer):
    if axes == ("tp",):
        return (lax.axis_index("req"), peer)
    if axes == ("req",):
        return (peer, lax.axis_index("tp"))
    n_tp = lax.axis_size("tp")
    return (peer // n_tp, peer % n_tp)


def _direct_kernel(axes, scatter, x_ref, out_ref, send_sem, recv_sem, local_sem):
    n = out_ref.shape[0]
    me = lax.axis_index(axes)
    barrier = pltpu.get_barrier_semaphore()

    def greet(d, carry):
        peer = (me + d) % n
        pl.semaphore_signal(barrier, inc=1, device_id=_peer_id(axes, peer), device_id_type=MESH_ID)
        return carry

    lax.fori_loop(1, n, greet, 0)
    pl.semaphore_wait(barrier, n - 1)

    def source(peer):
        return x_ref.at[peer] if scatter else x_ref

    local = pltpu.make_async_copy(source(me), out_ref.at[me], local_sem)
    local.start()

    def send(d, carry):
        peer = (me + d) % n
        pltpu.make_async_remote_copy(
            source(peer), out_ref.at[me], send_sem.at[d], recv_sem.at[me],
            device_id=_peer_id(axes, peer), device_id_type=MESH_ID,
        ).start()
        return carry

    lax.fori_loop(1, n, send, 0)

    def receive(d, carry):
        src = (me + n - d) % n
        pltpu.make_async_remote_copy(
            source(src), out_ref.at[src], send_sem.at[d], recv_sem.at[src],
            device_id=_peer_id(axes, src), device_id_type=MESH_ID,
        ).wait_recv()
        return carry

    lax.fori_loop(1, n, receive, 0)

    def sent(d, carry):
        peer = (me + d) % n
        pltpu.make_async_remote_copy(
            source(peer), out_ref.at[me], send_sem.at[d], recv_sem.at[me],
            device_id=_peer_id(axes, peer), device_id_type=MESH_ID,
        ).wait_send()
        return carry

    lax.fori_loop(1, n, sent, 0)
    local.wait()


def direct_exchange(x, axes, collective_id, scatter=False):
    n = 1
    for name in axes:
        n *= lax.axis_size(name)
    block = x.shape[1:] if scatter else x.shape
    return pl.pallas_call(
        functools.partial(_direct_kernel, axes, scatter),
        out_shape=jax.ShapeDtypeStruct((n,) + block, x.dtype),
        in_specs=[pl.BlockSpec(memory_space=pl.ANY)],
        out_specs=pl.BlockSpec(memory_space=pl.ANY),
        scratch_shapes=[
            pltpu.SemaphoreType.DMA((n,)),
            pltpu.SemaphoreType.DMA((n,)),
            pltpu.SemaphoreType.DMA,
        ],
        compiler_params=pltpu.CompilerParams(collective_id=collective_id, has_side_effects=True),
    )(x)


def _row_pick_kernel(ids_ref, rows_hbm, out_hbm, sem):
    count = ids_ref.shape[0]

    def start(k, carry):
        first = pl.multiple_of((ids_ref[k] // ROW_GROUP) * ROW_GROUP, ROW_GROUP)
        pltpu.make_async_copy(
            rows_hbm.at[pl.ds(first, ROW_GROUP)],
            out_hbm.at[pl.ds(pl.multiple_of(k * ROW_GROUP, ROW_GROUP), ROW_GROUP)],
            sem,
        ).start()
        return carry

    lax.fori_loop(0, count, start, 0)
    pltpu.make_async_copy(rows_hbm.at[pl.ds(0, count * ROW_GROUP)], out_hbm, sem).wait()


def pick_rows(rows, ids):
    groups = pl.pallas_call(
        _row_pick_kernel,
        out_shape=jax.ShapeDtypeStruct((ids.shape[0] * ROW_GROUP, rows.shape[1]), rows.dtype),
        grid_spec=pltpu.PrefetchScalarGridSpec(
            num_scalar_prefetch=1,
            grid=(1,),
            in_specs=[pl.BlockSpec(memory_space=pl.ANY)],
            out_specs=pl.BlockSpec((ids.shape[0] * ROW_GROUP, rows.shape[1]), lambda i, ids_ref: (0, 0)),
            scratch_shapes=[pltpu.SemaphoreType.DMA],
        ),
    )(ids, rows).reshape(ids.shape[0], ROW_GROUP, rows.shape[1])
    within = jnp.arange(ROW_GROUP, dtype=jnp.int32)[None, :, None] == (ids % ROW_GROUP)[:, None, None]
    return jnp.sum(jnp.where(within, groups.astype(jnp.float32), jnp.float32(0.0)), axis=1)


HEAD_DIM = 64
RING_CHUNKS = 4
SPARSE_PAIRS = 64
ROW_GROUP = 16
WINDOW = 512


layer_eps = 1e-05
norm_eps = 1e-06


def layer_norm(values, gain, shift):
    centre = values - jnp.mean(values, axis=-1, keepdims=True)
    spread = jnp.mean(centre * centre, axis=-1, keepdims=True)
    return centre * lax.rsqrt(spread + layer_eps) * gain + shift


def window_attention(queries_h, keys_h, values_h, lengths):
    seq_len = queries_h.shape[1]
    half_window = WINDOW // 2
    scale_factor = HEAD_DIM ** (-0.5)
    pos = jnp.arange(seq_len, dtype=jnp.int32)
    near = jnp.abs(pos[:, None] - pos[None, :]) <= half_window
    keep_mask = near[None] & (pos[None, None, :] < lengths[:, None, None])
    logits = (
        jnp.einsum("tqhe,tkhe->thqk", queries_h, keys_h, preferred_element_type=jnp.float32)
        * scale_factor
    )
    logits = jnp.where(keep_mask[:, None], logits, jnp.float32(-1e30))
    top_val = jnp.max(logits, axis=-1, keepdims=True)
    expo = jnp.exp(logits - top_val)
    attn_weights = (expo / jnp.sum(expo, axis=-1, keepdims=True)).astype(jnp.bfloat16)
    context = jnp.einsum(
        "thqk,tkhe->tqhe", attn_weights, values_h, preferred_element_type=jnp.float32
    )
    context = jnp.where(
        (pos[None, :] < lengths[:, None])[:, :, None, None], context, jnp.float32(0.0)
    )
    return context.astype(jnp.bfloat16).reshape(
        queries_h.shape[0], seq_len, queries_h.shape[2] * HEAD_DIM
    )


def per_device(
    states,
    lengths,
    w_qkv,
    b_qkv,
    w_out,
    b_out,
    ln1_gain,
    ln1_shift,
    w_up,
    b_up,
    w_down,
    b_down,
    ln2_gain,
    ln2_shift,
    index_rows,
    cand_ids,
):
    tp_count = lax.axis_size("tp")
    tp_rank = lax.axis_index("tp")
    req_count = lax.axis_size("req")
    req_rank = lax.axis_index("req")
    text_count, row_share, model_width = states.shape
    quarter = cand_ids.shape[1]
    full_states = ring_all_gather(states, 0, RING_CHUNKS)
    device_count = req_count * tp_count
    seq_len = full_states.shape[1]
    local_width = w_qkv.shape[2]
    heads_here = local_width // HEAD_DIM
    projected = (
        jnp.einsum("tsd,dce->tsce", full_states, w_qkv, preferred_element_type=jnp.float32) + b_qkv
    ).astype(jnp.bfloat16)
    queries_h = projected[:, :, 0].reshape(text_count, seq_len, heads_here, HEAD_DIM)
    keys_h = projected[:, :, 1].reshape(text_count, seq_len, heads_here, HEAD_DIM)
    values_h = projected[:, :, 2].reshape(text_count, seq_len, heads_here, HEAD_DIM)

    context = window_attention(queries_h, keys_h, values_h, lengths)
    partial_value = jnp.einsum("tsk,kd->tsd", context, w_out, preferred_element_type=jnp.float32)
    partial_value = partial_value.astype(jnp.bfloat16)
    attn_recv = ring_reduce_scatter_add(partial_value, 1, RING_CHUNKS)
    attn_sum = lax.dynamic_slice_in_dim(partial_value, tp_rank * row_share, row_share, 1).astype(
        jnp.float32
    ) + jnp.sum(attn_recv.astype(jnp.float32), axis=0)
    normed_local = layer_norm(
        states.astype(jnp.float32) + attn_sum + b_out, ln1_gain, ln1_shift
    ).astype(jnp.bfloat16)
    normed_full = ring_all_gather(normed_local, 2, RING_CHUNKS)
    up_act = jax.nn.gelu(
        jnp.einsum("tsd,df->tsf", normed_full, w_up, preferred_element_type=jnp.float32) + b_up,
        approximate=False,
    ).astype(jnp.bfloat16)
    up_act = lax.optimization_barrier(up_act)
    down_part = jnp.einsum(
        "tsf,fd->tsd", up_act, w_down, preferred_element_type=jnp.float32
    ).astype(jnp.bfloat16)
    down_recv = ring_reduce_scatter_add(down_part, 3, RING_CHUNKS)
    down_sum = lax.dynamic_slice_in_dim(down_part, tp_rank * row_share, row_share, 1).astype(
        jnp.float32
    ) + jnp.sum(down_recv.astype(jnp.float32), axis=0)
    hidden_out = layer_norm(
        normed_local.astype(jnp.float32) + down_sum + b_down, ln2_gain, ln2_shift
    ).astype(jnp.bfloat16)
    positions = tp_rank * row_share + jnp.arange(row_share, dtype=jnp.int32)
    is_valid = positions[None, :] < lengths[:, None]
    local_pool = jnp.sum(
        jnp.where(is_valid[:, :, None], hidden_out.astype(jnp.float32), jnp.float32(0.0)), axis=1
    )
    pool_and_ids = direct_exchange(
        jnp.concatenate([local_pool, cand_ids.astype(jnp.float32)], axis=1), ("tp",), 5
    )
    text_ids = jnp.swapaxes(pool_and_ids[:, :, model_width:], 0, 1)
    pooled = jnp.sum(pool_and_ids[:, :, :model_width], axis=0) / lengths.astype(
        jnp.float32
    )[:, None]
    query_vec = (
        pooled * lax.rsqrt(jnp.mean(pooled * pooled, axis=-1, keepdims=True) + norm_eps)
    ).astype(jnp.bfloat16)
    bundle = jnp.concatenate(
        [query_vec.astype(jnp.float32), text_ids.reshape(text_count, -1)], axis=1
    )
    bundle = direct_exchange(bundle, ("req",), 6).reshape(req_count * text_count, bundle.shape[1])
    all_queries = bundle[:, :model_width].astype(jnp.bfloat16)
    all_ids = bundle[:, model_width:].astype(jnp.int32)
    rows_here = index_rows.shape[0]
    first_row = (req_rank * tp_count + tp_rank) * rows_here
    local_ids = all_ids - first_row
    is_owned = (local_ids >= 0) & (local_ids < rows_here)
    safe_ids = jnp.clip(local_ids, 0, rows_here - 1)
    owned_count = jnp.sum(is_owned.astype(jnp.int32))

    def few_owned(_):
        flat_owned = is_owned.reshape(-1)
        owned_int = is_owned.astype(jnp.int32)
        row_counts = jnp.cumsum(owned_int, axis=1)
        row_totals = row_counts[:, -1]
        running = (row_counts + (jnp.cumsum(row_totals) - row_totals)[:, None]).reshape(-1)
        rank = jnp.arange(SPARSE_PAIRS, dtype=jnp.int32)
        chosen = flat_owned[None, :] & (running[None, :] == rank[:, None] + 1)
        pair_index = jnp.arange(flat_owned.shape[0], dtype=jnp.int32)
        pair_at = jnp.sum(jnp.where(chosen, pair_index[None, :], 0), axis=1)
        row_of = jnp.sum(jnp.where(chosen, safe_ids.reshape(-1)[None, :], 0), axis=1)
        rows = pick_rows(index_rows, jnp.clip(row_of, 0, rows_here - 1))
        text_of = pair_at // all_ids.shape[1]
        text_pick = jnp.arange(all_queries.shape[0], dtype=jnp.int32)[None, :] == text_of[:, None]
        queries = jnp.dot(
            text_pick.astype(all_queries.dtype), all_queries, preferred_element_type=jnp.float32
        )
        values = jnp.sum(rows.astype(jnp.float32) * queries.astype(jnp.float32), axis=-1)
        return jnp.sum(
            jnp.where(chosen, values[:, None], jnp.float32(0.0)), axis=0
        ).reshape(all_ids.shape)

    def many_owned(_):
        all_scores = jnp.einsum(
            "td,rd->tr", all_queries, index_rows, preferred_element_type=jnp.float32
        )
        score_rows = jnp.take(all_scores.T, safe_ids.reshape(-1), axis=0).reshape(
            safe_ids.shape[0], safe_ids.shape[1], safe_ids.shape[0]
        )
        picked = jnp.einsum("tct->tc", score_rows)
        return jnp.where(is_owned, picked, jnp.float32(0.0))

    owner_terms = lax.cond(owned_count <= SPARSE_PAIRS, few_owned, many_owned, None)
    owner_terms = (
        owner_terms.reshape(req_count, text_count, tp_count, quarter)
        .transpose(0, 2, 1, 3)
        .reshape(device_count, text_count, quarter)
    )
    scores = jnp.sum(lax.all_to_all(owner_terms, ("req", "tp"), 0, 0, tiled=True), axis=0)
    return (hidden_out, scores)


def solution(mesh):
    placed = (
        P("req", "tp", None),
        P("req"),
        P(None, None, "tp"),
        P(None, "tp"),
        P("tp", None),
        P(),
        P(),
        P(),
        P(None, "tp"),
        P("tp"),
        P("tp", None),
        P(),
        P(),
        P(),
        P(("req", "tp"), None),
        P("req", "tp"),
    )
    return jax.shard_map(
        per_device,
        mesh=mesh,
        in_specs=placed,
        out_specs=(P("req", "tp", None), P("req", "tp")),
        check_vma=False,
    )
```

```python
import functools
import jax
import jax.numpy as jnp
from jax import lax
from jax.experimental import pallas as pl
from jax.experimental.pallas import tpu as pltpu
from jax.sharding import PartitionSpec as P

MESH_ID = pl.DeviceIdType.MESH


def _ring_peers():
    n = lax.axis_size("tp")
    me = lax.axis_index("tp")
    rq = lax.axis_index("req")
    core = rq % 2
    right = (me + 1) % n
    left = (me + n - 1) % n
    opp = (me + 2) % n
    relay_to = (me + 1 + 2 * core) % n
    relay_from = (me + n - 1 - 2 * core) % n
    barrier = pltpu.get_barrier_semaphore()
    for peer in (left, right):
        pl.semaphore_signal(barrier, inc=1, device_id=(rq, peer), device_id_type=MESH_ID)
    pl.semaphore_wait(barrier, 2)
    return me, rq, core, right, left, opp, relay_to, relay_from


def _gather_kernel(chunks, x_ref, out_ref, send_sem, recv_sem, local_sem):
    me, rq, core, right, left, opp, relay_to, relay_from = _ring_peers()
    rows = x_ref.shape[1]
    step = rows // chunks

    def part(ref, k):
        return ref.at[:, pl.ds(k * step, step), :]

    def slot(src, k):
        return out_ref.at[:, pl.ds(src * rows + k * step, step), :]

    def copy(src, dst, send, recv, peer):
        return pltpu.make_async_remote_copy(
            src, dst, send, recv, device_id=(rq, peer), device_id_type=MESH_ID
        )

    local = pltpu.make_async_copy(x_ref, out_ref.at[:, pl.ds(me * rows, rows), :], local_sem)
    local.start()
    sends = []
    for k in range(chunks):
        to_right = copy(part(x_ref, k), slot(me, k), send_sem.at[0, k], recv_sem.at[0, k], right)
        to_left = copy(part(x_ref, k), slot(me, k), send_sem.at[1, k], recv_sem.at[1, k], left)
        to_right.start()
        to_left.start()
        sends += [to_right, to_left]
    for k in range(chunks):
        copy(part(x_ref, k), slot(relay_from, k), send_sem.at[2, k], recv_sem.at[core, k], right).wait_recv()
        forward = copy(
            slot(relay_from, k), slot(relay_from, k), send_sem.at[2, k], recv_sem.at[2, k], relay_to
        )
        forward.start()
        sends.append(forward)
    other_side = (me + 1 + 2 * (1 - core)) % lax.axis_size("tp")
    for k in range(chunks):
        copy(part(x_ref, k), slot(other_side, k), send_sem.at[0, k], recv_sem.at[1 - core, k], right).wait_recv()
    for k in range(chunks):
        copy(part(x_ref, k), slot(opp, k), send_sem.at[0, k], recv_sem.at[2, k], right).wait_recv()
    for c in sends:
        c.wait_send()
    local.wait()


def ring_all_gather(x, collective_id, chunks=1):
    texts, rows, width = x.shape
    n = lax.axis_size("tp")
    return pl.pallas_call(
        functools.partial(_gather_kernel, chunks),
        out_shape=jax.ShapeDtypeStruct((texts, n * rows, width), x.dtype),
        in_specs=[pl.BlockSpec(memory_space=pl.ANY)],
        out_specs=pl.BlockSpec(memory_space=pl.ANY),
        scratch_shapes=[
            pltpu.SemaphoreType.DMA((3, chunks)),
            pltpu.SemaphoreType.DMA((3, chunks)),
            pltpu.SemaphoreType.DMA,
        ],
        compiler_params=pltpu.CompilerParams(collective_id=collective_id, has_side_effects=True),
    )(x)


def _scatter_add_kernel(chunks, p_ref, recv_ref, send_sem, recv_sem, relay_sem, local_sem,
                        own_buf, relay_buf, sum_buf):
    me, rq, core, right, left, opp, relay_to, relay_from = _ring_peers()
    rows = recv_ref.shape[2]
    step = rows // chunks

    def block(dst, k):
        return p_ref.at[:, pl.ds(dst * rows + k * step, step), :]

    def part(ref, k):
        return ref.at[:, pl.ds(k * step, step), :]

    def copy(src, dst, send, recv, peer):
        return pltpu.make_async_remote_copy(
            src, dst, send, recv, device_id=(rq, peer), device_id_type=MESH_ID
        )

    sends = []
    loads = []
    for k in range(chunks):
        to_relay = copy(block(opp, k), relay_buf.at[k], send_sem.at[0, k], relay_sem.at[k], relay_to)
        to_other = copy(
            block(relay_from, k), part(recv_ref.at[1], k), send_sem.at[1, k], recv_sem.at[1, k], relay_from
        )
        to_relay.start()
        to_other.start()
        load = pltpu.make_async_copy(block(relay_to, k), own_buf.at[k], local_sem.at[k])
        load.start()
        sends += [to_relay, to_other]
        loads.append(load)
    forwards = []
    for k in range(chunks):
        sends[2 * k].wait_recv()
        loads[k].wait()
        sum_buf[k] = (
            own_buf[k].astype(jnp.float32) + relay_buf[k].astype(jnp.float32)
        ).astype(sum_buf.dtype)
        forward = copy(sum_buf.at[k], part(recv_ref.at[0], k), send_sem.at[2, k], recv_sem.at[0, k], relay_to)
        forward.start()
        forwards.append(forward)
    for k in range(chunks):
        sends[2 * k + 1].wait_recv()
        forwards[k].wait_recv()
    for c in sends + forwards:
        c.wait_send()


def ring_reduce_scatter_add(p, collective_id, chunks=1):
    texts, all_rows, width = p.shape
    n = lax.axis_size("tp")
    rows = all_rows // n
    step = rows // chunks
    buf = pltpu.VMEM((chunks, texts, step, width), p.dtype)
    return pl.pallas_call(
        functools.partial(_scatter_add_kernel, chunks),
        out_shape=jax.ShapeDtypeStruct((2, texts, rows, width), p.dtype),
        in_specs=[pl.BlockSpec(memory_space=pl.ANY)],
        out_specs=pl.BlockSpec(memory_space=pl.ANY),
        scratch_shapes=[
            pltpu.SemaphoreType.DMA((3, chunks)),
            pltpu.SemaphoreType.DMA((2, chunks)),
            pltpu.SemaphoreType.DMA((chunks,)),
            pltpu.SemaphoreType.DMA((chunks,)),
            buf,
            buf,
            buf,
        ],
        compiler_params=pltpu.CompilerParams(collective_id=collective_id, has_side_effects=True),
    )(p)


def _peer_id(axes, peer):
    if axes == ("tp",):
        return (lax.axis_index("req"), peer)
    if axes == ("req",):
        return (peer, lax.axis_index("tp"))
    n_tp = lax.axis_size("tp")
    return (peer // n_tp, peer % n_tp)


def _direct_kernel(axes, scatter, x_ref, out_ref, send_sem, recv_sem, local_sem):
    n = out_ref.shape[0]
    me = lax.axis_index(axes)
    barrier = pltpu.get_barrier_semaphore()

    def greet(d, carry):
        peer = (me + d) % n
        pl.semaphore_signal(barrier, inc=1, device_id=_peer_id(axes, peer), device_id_type=MESH_ID)
        return carry

    lax.fori_loop(1, n, greet, 0)
    pl.semaphore_wait(barrier, n - 1)

    def source(peer):
        return x_ref.at[peer] if scatter else x_ref

    local = pltpu.make_async_copy(source(me), out_ref.at[me], local_sem)
    local.start()

    def send(d, carry):
        peer = (me + d) % n
        pltpu.make_async_remote_copy(
            source(peer), out_ref.at[me], send_sem.at[d], recv_sem.at[me],
            device_id=_peer_id(axes, peer), device_id_type=MESH_ID,
        ).start()
        return carry

    lax.fori_loop(1, n, send, 0)

    def receive(d, carry):
        src = (me + n - d) % n
        pltpu.make_async_remote_copy(
            source(src), out_ref.at[src], send_sem.at[d], recv_sem.at[src],
            device_id=_peer_id(axes, src), device_id_type=MESH_ID,
        ).wait_recv()
        return carry

    lax.fori_loop(1, n, receive, 0)

    def sent(d, carry):
        peer = (me + d) % n
        pltpu.make_async_remote_copy(
            source(peer), out_ref.at[me], send_sem.at[d], recv_sem.at[me],
            device_id=_peer_id(axes, peer), device_id_type=MESH_ID,
        ).wait_send()
        return carry

    lax.fori_loop(1, n, sent, 0)
    local.wait()


def direct_exchange(x, axes, collective_id, scatter=False):
    n = 1
    for name in axes:
        n *= lax.axis_size(name)
    block = x.shape[1:] if scatter else x.shape
    return pl.pallas_call(
        functools.partial(_direct_kernel, axes, scatter),
        out_shape=jax.ShapeDtypeStruct((n,) + block, x.dtype),
        in_specs=[pl.BlockSpec(memory_space=pl.ANY)],
        out_specs=pl.BlockSpec(memory_space=pl.ANY),
        scratch_shapes=[
            pltpu.SemaphoreType.DMA((n,)),
            pltpu.SemaphoreType.DMA((n,)),
            pltpu.SemaphoreType.DMA,
        ],
        compiler_params=pltpu.CompilerParams(collective_id=collective_id, has_side_effects=True),
    )(x)


HEAD_DIM = 64
RING_CHUNKS = 2
SPARSE_PAIRS = 64
WINDOW = 512


layer_eps = 1e-05
norm_eps = 1e-06


def layer_norm(values, gain, shift):
    centre = values - jnp.mean(values, axis=-1, keepdims=True)
    spread = jnp.mean(centre * centre, axis=-1, keepdims=True)
    return centre * lax.rsqrt(spread + layer_eps) * gain + shift


def window_attention(queries_h, keys_h, values_h, lengths):
    seq_len = queries_h.shape[1]
    half_window = WINDOW // 2
    scale_factor = HEAD_DIM ** (-0.5)
    pos = jnp.arange(seq_len, dtype=jnp.int32)
    near = jnp.abs(pos[:, None] - pos[None, :]) <= half_window
    keep_mask = near[None] & (pos[None, None, :] < lengths[:, None, None])
    logits = (
        jnp.einsum("tqhe,tkhe->thqk", queries_h, keys_h, preferred_element_type=jnp.float32)
        * scale_factor
    )
    logits = jnp.where(keep_mask[:, None], logits, jnp.float32(-1e30))
    top_val = jnp.max(logits, axis=-1, keepdims=True)
    expo = jnp.exp(logits - top_val)
    attn_weights = (expo / jnp.sum(expo, axis=-1, keepdims=True)).astype(jnp.bfloat16)
    context = jnp.einsum(
        "thqk,tkhe->tqhe", attn_weights, values_h, preferred_element_type=jnp.float32
    )
    context = jnp.where(
        (pos[None, :] < lengths[:, None])[:, :, None, None], context, jnp.float32(0.0)
    )
    return context.astype(jnp.bfloat16).reshape(
        queries_h.shape[0], seq_len, queries_h.shape[2] * HEAD_DIM
    )


def per_device(
    states,
    lengths,
    w_qkv,
    b_qkv,
    w_out,
    b_out,
    ln1_gain,
    ln1_shift,
    w_up,
    b_up,
    w_down,
    b_down,
    ln2_gain,
    ln2_shift,
    index_rows,
    cand_ids,
):
    tp_count = lax.axis_size("tp")
    tp_rank = lax.axis_index("tp")
    req_count = lax.axis_size("req")
    req_rank = lax.axis_index("req")
    text_count, row_share, model_width = states.shape
    quarter = cand_ids.shape[1]
    full_states = ring_all_gather(states, 0, RING_CHUNKS)
    device_count = req_count * tp_count
    seq_len = full_states.shape[1]
    local_width = w_qkv.shape[2]
    heads_here = local_width // HEAD_DIM
    projected = (
        jnp.einsum("tsd,dce->tsce", full_states, w_qkv, preferred_element_type=jnp.float32) + b_qkv
    ).astype(jnp.bfloat16)
    queries_h = projected[:, :, 0].reshape(text_count, seq_len, heads_here, HEAD_DIM)
    keys_h = projected[:, :, 1].reshape(text_count, seq_len, heads_here, HEAD_DIM)
    values_h = projected[:, :, 2].reshape(text_count, seq_len, heads_here, HEAD_DIM)

    context = window_attention(queries_h, keys_h, values_h, lengths)
    partial_value = jnp.einsum("tsk,kd->tsd", context, w_out, preferred_element_type=jnp.float32)
    partial_value = partial_value.astype(jnp.bfloat16)
    attn_recv = ring_reduce_scatter_add(partial_value, 1, RING_CHUNKS)
    attn_sum = lax.dynamic_slice_in_dim(partial_value, tp_rank * row_share, row_share, 1).astype(
        jnp.float32
    ) + jnp.sum(attn_recv.astype(jnp.float32), axis=0)
    normed_local = layer_norm(
        states.astype(jnp.float32) + attn_sum + b_out, ln1_gain, ln1_shift
    ).astype(jnp.bfloat16)
    normed_full = ring_all_gather(normed_local, 2, RING_CHUNKS)
    up_act = jax.nn.gelu(
        jnp.einsum("tsd,df->tsf", normed_full, w_up, preferred_element_type=jnp.float32) + b_up,
        approximate=False,
    ).astype(jnp.bfloat16)
    up_act = lax.optimization_barrier(up_act)
    down_part = jnp.einsum(
        "tsf,fd->tsd", up_act, w_down, preferred_element_type=jnp.float32
    ).astype(jnp.bfloat16)
    down_recv = ring_reduce_scatter_add(down_part, 3, RING_CHUNKS)
    down_sum = lax.dynamic_slice_in_dim(down_part, tp_rank * row_share, row_share, 1).astype(
        jnp.float32
    ) + jnp.sum(down_recv.astype(jnp.float32), axis=0)
    hidden_out = layer_norm(
        normed_local.astype(jnp.float32) + down_sum + b_down, ln2_gain, ln2_shift
    ).astype(jnp.bfloat16)
    positions = tp_rank * row_share + jnp.arange(row_share, dtype=jnp.int32)
    is_valid = positions[None, :] < lengths[:, None]
    local_pool = jnp.sum(
        jnp.where(is_valid[:, :, None], hidden_out.astype(jnp.float32), jnp.float32(0.0)), axis=1
    )
    pool_and_ids = direct_exchange(
        jnp.concatenate([local_pool, cand_ids.astype(jnp.float32)], axis=1), ("tp",), 5
    )
    text_ids = jnp.swapaxes(pool_and_ids[:, :, model_width:], 0, 1)
    pooled = jnp.sum(pool_and_ids[:, :, :model_width], axis=0) / lengths.astype(
        jnp.float32
    )[:, None]
    query_vec = (
        pooled * lax.rsqrt(jnp.mean(pooled * pooled, axis=-1, keepdims=True) + norm_eps)
    ).astype(jnp.bfloat16)
    bundle = jnp.concatenate(
        [query_vec.astype(jnp.float32), text_ids.reshape(text_count, -1)], axis=1
    )
    bundle = direct_exchange(bundle, ("req",), 6).reshape(req_count * text_count, bundle.shape[1])
    all_queries = bundle[:, :model_width].astype(jnp.bfloat16)
    all_ids = bundle[:, model_width:].astype(jnp.int32)
    rows_here = index_rows.shape[0]
    first_row = (req_rank * tp_count + tp_rank) * rows_here
    local_ids = all_ids - first_row
    is_owned = (local_ids >= 0) & (local_ids < rows_here)
    safe_ids = jnp.clip(local_ids, 0, rows_here - 1)
    owned_count = jnp.sum(is_owned.astype(jnp.int32))

    def few_owned(_):
        flat_owned = is_owned.reshape(-1)
        owned_int = is_owned.astype(jnp.int32)
        row_counts = jnp.cumsum(owned_int, axis=1)
        row_totals = row_counts[:, -1]
        running = (row_counts + (jnp.cumsum(row_totals) - row_totals)[:, None]).reshape(-1)
        rank = jnp.arange(SPARSE_PAIRS, dtype=jnp.int32)
        chosen = flat_owned[None, :] & (running[None, :] == rank[:, None] + 1)
        pair_index = jnp.arange(flat_owned.shape[0], dtype=jnp.int32)
        pair_at = jnp.sum(jnp.where(chosen, pair_index[None, :], 0), axis=1)
        row_of = jnp.sum(jnp.where(chosen, safe_ids.reshape(-1)[None, :], 0), axis=1)
        row_pick = jnp.arange(rows_here, dtype=jnp.int32)[None, :] == row_of[:, None]
        rows = jnp.dot(row_pick.astype(index_rows.dtype), index_rows, preferred_element_type=jnp.float32)
        text_of = pair_at // all_ids.shape[1]
        text_pick = jnp.arange(all_queries.shape[0], dtype=jnp.int32)[None, :] == text_of[:, None]
        queries = jnp.dot(
            text_pick.astype(all_queries.dtype), all_queries, preferred_element_type=jnp.float32
        )
        values = jnp.sum(rows.astype(jnp.float32) * queries.astype(jnp.float32), axis=-1)
        return jnp.sum(
            jnp.where(chosen, values[:, None], jnp.float32(0.0)), axis=0
        ).reshape(all_ids.shape)

    def many_owned(_):
        all_scores = jnp.einsum(
            "td,rd->tr", all_queries, index_rows, preferred_element_type=jnp.float32
        )
        score_rows = jnp.take(all_scores.T, safe_ids.reshape(-1), axis=0).reshape(
            safe_ids.shape[0], safe_ids.shape[1], safe_ids.shape[0]
        )
        picked = jnp.einsum("tct->tc", score_rows)
        return jnp.where(is_owned, picked, jnp.float32(0.0))

    owner_terms = lax.cond(owned_count <= SPARSE_PAIRS, few_owned, many_owned, None)
    owner_terms = (
        owner_terms.reshape(req_count, text_count, tp_count, quarter)
        .transpose(0, 2, 1, 3)
        .reshape(device_count, text_count, quarter)
    )
    scores = jnp.sum(lax.all_to_all(owner_terms, ("req", "tp"), 0, 0, tiled=True), axis=0)
    return (hidden_out, scores)


def solution(mesh):
    placed = (
        P("req", "tp", None),
        P("req"),
        P(None, None, "tp"),
        P(None, "tp"),
        P("tp", None),
        P(),
        P(),
        P(),
        P(None, "tp"),
        P("tp"),
        P("tp", None),
        P(),
        P(),
        P(),
        P(("req", "tp"), None),
        P("req", "tp"),
    )
    return jax.shard_map(
        per_device,
        mesh=mesh,
        in_specs=placed,
        out_specs=(P("req", "tp", None), P("req", "tp")),
        check_vma=False,
    )
```

```python
import functools
import jax
import jax.numpy as jnp
from jax import lax
from jax.experimental import pallas as pl
from jax.experimental.pallas import tpu as pltpu
from jax.sharding import PartitionSpec as P

MESH_ID = pl.DeviceIdType.MESH


def _ring_peers():
    n = lax.axis_size("tp")
    me = lax.axis_index("tp")
    rq = lax.axis_index("req")
    core = rq % 2
    right = (me + 1) % n
    left = (me + n - 1) % n
    opp = (me + 2) % n
    relay_to = (me + 1 + 2 * core) % n
    relay_from = (me + n - 1 - 2 * core) % n
    barrier = pltpu.get_barrier_semaphore()
    for peer in (left, right):
        pl.semaphore_signal(barrier, inc=1, device_id=(rq, peer), device_id_type=MESH_ID)
    pl.semaphore_wait(barrier, 2)
    return me, rq, core, right, left, opp, relay_to, relay_from


def _gather_kernel(chunks, x_ref, out_ref, send_sem, recv_sem, local_sem):
    me, rq, core, right, left, opp, relay_to, relay_from = _ring_peers()
    rows = x_ref.shape[1]
    step = rows // chunks

    def part(ref, k):
        return ref.at[:, pl.ds(k * step, step), :]

    def slot(src, k):
        return out_ref.at[:, pl.ds(src * rows + k * step, step), :]

    def copy(src, dst, send, recv, peer):
        return pltpu.make_async_remote_copy(
            src, dst, send, recv, device_id=(rq, peer), device_id_type=MESH_ID
        )

    local = pltpu.make_async_copy(x_ref, out_ref.at[:, pl.ds(me * rows, rows), :], local_sem)
    local.start()
    sends = []
    for k in range(chunks):
        to_right = copy(part(x_ref, k), slot(me, k), send_sem.at[0, k], recv_sem.at[0, k], right)
        to_left = copy(part(x_ref, k), slot(me, k), send_sem.at[1, k], recv_sem.at[1, k], left)
        to_right.start()
        to_left.start()
        sends += [to_right, to_left]
    for k in range(chunks):
        copy(part(x_ref, k), slot(relay_from, k), send_sem.at[2, k], recv_sem.at[core, k], right).wait_recv()
        forward = copy(
            slot(relay_from, k), slot(relay_from, k), send_sem.at[2, k], recv_sem.at[2, k], relay_to
        )
        forward.start()
        sends.append(forward)
    other_side = (me + 1 + 2 * (1 - core)) % lax.axis_size("tp")
    for k in range(chunks):
        copy(part(x_ref, k), slot(other_side, k), send_sem.at[0, k], recv_sem.at[1 - core, k], right).wait_recv()
    for k in range(chunks):
        copy(part(x_ref, k), slot(opp, k), send_sem.at[0, k], recv_sem.at[2, k], right).wait_recv()
    for c in sends:
        c.wait_send()
    local.wait()


def ring_all_gather(x, collective_id, chunks=1):
    texts, rows, width = x.shape
    n = lax.axis_size("tp")
    return pl.pallas_call(
        functools.partial(_gather_kernel, chunks),
        out_shape=jax.ShapeDtypeStruct((texts, n * rows, width), x.dtype),
        in_specs=[pl.BlockSpec(memory_space=pl.ANY)],
        out_specs=pl.BlockSpec(memory_space=pl.ANY),
        scratch_shapes=[
            pltpu.SemaphoreType.DMA((3, chunks)),
            pltpu.SemaphoreType.DMA((3, chunks)),
            pltpu.SemaphoreType.DMA,
        ],
        compiler_params=pltpu.CompilerParams(collective_id=collective_id, has_side_effects=True),
    )(x)


def _scatter_add_kernel(chunks, p_ref, recv_ref, send_sem, recv_sem, relay_sem, local_sem,
                        own_buf, relay_buf, sum_buf):
    me, rq, core, right, left, opp, relay_to, relay_from = _ring_peers()
    rows = recv_ref.shape[2]
    step = rows // chunks

    def block(dst, k):
        return p_ref.at[:, pl.ds(dst * rows + k * step, step), :]

    def part(ref, k):
        return ref.at[:, pl.ds(k * step, step), :]

    def copy(src, dst, send, recv, peer):
        return pltpu.make_async_remote_copy(
            src, dst, send, recv, device_id=(rq, peer), device_id_type=MESH_ID
        )

    sends = []
    loads = []
    for k in range(chunks):
        to_relay = copy(block(opp, k), relay_buf.at[k], send_sem.at[0, k], relay_sem.at[k], relay_to)
        to_other = copy(
            block(relay_from, k), part(recv_ref.at[1], k), send_sem.at[1, k], recv_sem.at[1, k], relay_from
        )
        to_relay.start()
        to_other.start()
        load = pltpu.make_async_copy(block(relay_to, k), own_buf.at[k], local_sem.at[k])
        load.start()
        sends += [to_relay, to_other]
        loads.append(load)
    forwards = []
    for k in range(chunks):
        sends[2 * k].wait_recv()
        loads[k].wait()
        sum_buf[k] = (
            own_buf[k].astype(jnp.float32) + relay_buf[k].astype(jnp.float32)
        ).astype(sum_buf.dtype)
        forward = copy(sum_buf.at[k], part(recv_ref.at[0], k), send_sem.at[2, k], recv_sem.at[0, k], relay_to)
        forward.start()
        forwards.append(forward)
    for k in range(chunks):
        sends[2 * k + 1].wait_recv()
        forwards[k].wait_recv()
    for c in sends + forwards:
        c.wait_send()


def ring_reduce_scatter_add(p, collective_id, chunks=1):
    texts, all_rows, width = p.shape
    n = lax.axis_size("tp")
    rows = all_rows // n
    step = rows // chunks
    buf = pltpu.VMEM((chunks, texts, step, width), p.dtype)
    return pl.pallas_call(
        functools.partial(_scatter_add_kernel, chunks),
        out_shape=jax.ShapeDtypeStruct((2, texts, rows, width), p.dtype),
        in_specs=[pl.BlockSpec(memory_space=pl.ANY)],
        out_specs=pl.BlockSpec(memory_space=pl.ANY),
        scratch_shapes=[
            pltpu.SemaphoreType.DMA((3, chunks)),
            pltpu.SemaphoreType.DMA((2, chunks)),
            pltpu.SemaphoreType.DMA((chunks,)),
            pltpu.SemaphoreType.DMA((chunks,)),
            buf,
            buf,
            buf,
        ],
        compiler_params=pltpu.CompilerParams(collective_id=collective_id, has_side_effects=True),
    )(p)


def _peer_id(axes, peer):
    if axes == ("tp",):
        return (lax.axis_index("req"), peer)
    if axes == ("req",):
        return (peer, lax.axis_index("tp"))
    n_tp = lax.axis_size("tp")
    return (peer // n_tp, peer % n_tp)


def _direct_kernel(axes, scatter, x_ref, out_ref, send_sem, recv_sem):
    n = out_ref.shape[0]
    me = lax.axis_index(axes)
    barrier = pltpu.get_barrier_semaphore()

    def greet(d, carry):
        peer = (me + d) % n
        pl.semaphore_signal(barrier, inc=1, device_id=_peer_id(axes, peer), device_id_type=MESH_ID)
        return carry

    lax.fori_loop(1, n, greet, 0)
    pl.semaphore_wait(barrier, n - 1)

    def source(peer):
        return x_ref.at[peer] if scatter else x_ref

    def send(d, carry):
        peer = (me + d) % n
        pltpu.make_async_remote_copy(
            source(peer), out_ref.at[me], send_sem.at[d], recv_sem.at[me],
            device_id=_peer_id(axes, peer), device_id_type=MESH_ID,
        ).start()
        return carry

    lax.fori_loop(1, n, send, 0)

    def receive(d, carry):
        src = (me + n - d) % n
        pltpu.make_async_remote_copy(
            source(src), out_ref.at[src], send_sem.at[d], recv_sem.at[src],
            device_id=_peer_id(axes, src), device_id_type=MESH_ID,
        ).wait_recv()
        return carry

    lax.fori_loop(1, n, receive, 0)

    def sent(d, carry):
        peer = (me + d) % n
        pltpu.make_async_remote_copy(
            source(peer), out_ref.at[me], send_sem.at[d], recv_sem.at[me],
            device_id=_peer_id(axes, peer), device_id_type=MESH_ID,
        ).wait_send()
        return carry

    lax.fori_loop(1, n, sent, 0)


def direct_exchange(x, axes, collective_id, scatter=False):
    n = 1
    for name in axes:
        n *= lax.axis_size(name)
    block = x.shape[1:] if scatter else x.shape
    received = pl.pallas_call(
        functools.partial(_direct_kernel, axes, scatter),
        out_shape=jax.ShapeDtypeStruct((n,) + block, x.dtype),
        in_specs=[pl.BlockSpec(memory_space=pl.ANY)],
        out_specs=pl.BlockSpec(memory_space=pl.ANY),
        scratch_shapes=[
            pltpu.SemaphoreType.DMA((n,)),
            pltpu.SemaphoreType.DMA((n,)),
        ],
        compiler_params=pltpu.CompilerParams(collective_id=collective_id, has_side_effects=True),
    )(x)
    own = x[lax.axis_index(axes)] if scatter else x
    slot = jnp.arange(n, dtype=jnp.int32).reshape((n,) + (1,) * len(block))
    return jnp.where(slot == lax.axis_index(axes), own[None], received)


HEAD_DIM = 64
RING_CHUNKS = 2
SPARSE_PAIRS = 64
WINDOW = 512


layer_eps = 1e-05
norm_eps = 1e-06


def layer_norm(values, gain, shift):
    centre = values - jnp.mean(values, axis=-1, keepdims=True)
    spread = jnp.mean(centre * centre, axis=-1, keepdims=True)
    return centre * lax.rsqrt(spread + layer_eps) * gain + shift


def window_attention(queries_h, keys_h, values_h, lengths):
    seq_len = queries_h.shape[1]
    half_window = WINDOW // 2
    scale_factor = HEAD_DIM ** (-0.5)
    pos = jnp.arange(seq_len, dtype=jnp.int32)
    near = jnp.abs(pos[:, None] - pos[None, :]) <= half_window
    keep_mask = near[None] & (pos[None, None, :] < lengths[:, None, None])
    logits = (
        jnp.einsum("tqhe,tkhe->thqk", queries_h, keys_h, preferred_element_type=jnp.float32)
        * scale_factor
    )
    logits = jnp.where(keep_mask[:, None], logits, jnp.float32(-1e30))
    top_val = jnp.max(logits, axis=-1, keepdims=True)
    expo = jnp.exp(logits - top_val)
    attn_weights = (expo / jnp.sum(expo, axis=-1, keepdims=True)).astype(jnp.bfloat16)
    context = jnp.einsum(
        "thqk,tkhe->tqhe", attn_weights, values_h, preferred_element_type=jnp.float32
    )
    context = jnp.where(
        (pos[None, :] < lengths[:, None])[:, :, None, None], context, jnp.float32(0.0)
    )
    return context.astype(jnp.bfloat16).reshape(
        queries_h.shape[0], seq_len, queries_h.shape[2] * HEAD_DIM
    )


def per_device(
    states,
    lengths,
    w_qkv,
    b_qkv,
    w_out,
    b_out,
    ln1_gain,
    ln1_shift,
    w_up,
    b_up,
    w_down,
    b_down,
    ln2_gain,
    ln2_shift,
    index_rows,
    cand_ids,
):
    tp_count = lax.axis_size("tp")
    tp_rank = lax.axis_index("tp")
    req_count = lax.axis_size("req")
    req_rank = lax.axis_index("req")
    text_count, row_share, model_width = states.shape
    quarter = cand_ids.shape[1]
    full_states = ring_all_gather(states, 0, RING_CHUNKS)
    device_count = req_count * tp_count
    seq_len = full_states.shape[1]
    local_width = w_qkv.shape[2]
    heads_here = local_width // HEAD_DIM
    projected = (
        jnp.einsum("tsd,dce->tsce", full_states, w_qkv, preferred_element_type=jnp.float32) + b_qkv
    ).astype(jnp.bfloat16)
    queries_h = projected[:, :, 0].reshape(text_count, seq_len, heads_here, HEAD_DIM)
    keys_h = projected[:, :, 1].reshape(text_count, seq_len, heads_here, HEAD_DIM)
    values_h = projected[:, :, 2].reshape(text_count, seq_len, heads_here, HEAD_DIM)

    context = window_attention(queries_h, keys_h, values_h, lengths)
    partial_value = jnp.einsum("tsk,kd->tsd", context, w_out, preferred_element_type=jnp.float32)
    partial_value = partial_value.astype(jnp.bfloat16)
    attn_recv = ring_reduce_scatter_add(partial_value, 1, RING_CHUNKS)
    attn_sum = lax.dynamic_slice_in_dim(partial_value, tp_rank * row_share, row_share, 1).astype(
        jnp.float32
    ) + jnp.sum(attn_recv.astype(jnp.float32), axis=0)
    normed_local = layer_norm(
        states.astype(jnp.float32) + attn_sum + b_out, ln1_gain, ln1_shift
    ).astype(jnp.bfloat16)
    normed_full = ring_all_gather(normed_local, 2, RING_CHUNKS)
    up_act = jax.nn.gelu(
        jnp.einsum("tsd,df->tsf", normed_full, w_up, preferred_element_type=jnp.float32) + b_up,
        approximate=False,
    ).astype(jnp.bfloat16)
    up_act = lax.optimization_barrier(up_act)
    down_part = jnp.einsum(
        "tsf,fd->tsd", up_act, w_down, preferred_element_type=jnp.float32
    ).astype(jnp.bfloat16)
    down_recv = ring_reduce_scatter_add(down_part, 3, RING_CHUNKS)
    down_sum = lax.dynamic_slice_in_dim(down_part, tp_rank * row_share, row_share, 1).astype(
        jnp.float32
    ) + jnp.sum(down_recv.astype(jnp.float32), axis=0)
    hidden_out = layer_norm(
        normed_local.astype(jnp.float32) + down_sum + b_down, ln2_gain, ln2_shift
    ).astype(jnp.bfloat16)
    positions = tp_rank * row_share + jnp.arange(row_share, dtype=jnp.int32)
    is_valid = positions[None, :] < lengths[:, None]
    local_pool = jnp.sum(
        jnp.where(is_valid[:, :, None], hidden_out.astype(jnp.float32), jnp.float32(0.0)), axis=1
    )
    pool_and_ids = direct_exchange(
        jnp.concatenate([local_pool, cand_ids.astype(jnp.float32)], axis=1), ("tp",), 5
    )
    text_ids = jnp.swapaxes(pool_and_ids[:, :, model_width:], 0, 1)
    pooled = jnp.sum(pool_and_ids[:, :, :model_width], axis=0) / lengths.astype(
        jnp.float32
    )[:, None]
    query_vec = (
        pooled * lax.rsqrt(jnp.mean(pooled * pooled, axis=-1, keepdims=True) + norm_eps)
    ).astype(jnp.bfloat16)
    bundle = jnp.concatenate(
        [query_vec.astype(jnp.float32), text_ids.reshape(text_count, -1)], axis=1
    )
    bundle = direct_exchange(bundle, ("req",), 6).reshape(req_count * text_count, bundle.shape[1])
    all_queries = bundle[:, :model_width].astype(jnp.bfloat16)
    all_ids = bundle[:, model_width:].astype(jnp.int32)
    rows_here = index_rows.shape[0]
    first_row = (req_rank * tp_count + tp_rank) * rows_here
    local_ids = all_ids - first_row
    is_owned = (local_ids >= 0) & (local_ids < rows_here)
    safe_ids = jnp.clip(local_ids, 0, rows_here - 1)
    owned_count = jnp.sum(is_owned.astype(jnp.int32))

    def few_owned(_):
        flat_owned = is_owned.reshape(-1)
        owned_int = is_owned.astype(jnp.int32)
        row_counts = jnp.cumsum(owned_int, axis=1)
        row_totals = row_counts[:, -1]
        running = (row_counts + (jnp.cumsum(row_totals) - row_totals)[:, None]).reshape(-1)
        rank = jnp.arange(SPARSE_PAIRS, dtype=jnp.int32)
        chosen = flat_owned[None, :] & (running[None, :] == rank[:, None] + 1)
        pair_index = jnp.arange(flat_owned.shape[0], dtype=jnp.int32)
        pair_at = jnp.sum(jnp.where(chosen, pair_index[None, :], 0), axis=1)
        row_of = jnp.sum(jnp.where(chosen, safe_ids.reshape(-1)[None, :], 0), axis=1)
        row_pick = jnp.arange(rows_here, dtype=jnp.int32)[None, :] == row_of[:, None]
        rows = jnp.dot(row_pick.astype(index_rows.dtype), index_rows, preferred_element_type=jnp.float32)
        text_of = pair_at // all_ids.shape[1]
        text_pick = jnp.arange(all_queries.shape[0], dtype=jnp.int32)[None, :] == text_of[:, None]
        queries = jnp.dot(
            text_pick.astype(all_queries.dtype), all_queries, preferred_element_type=jnp.float32
        )
        values = jnp.sum(rows.astype(jnp.float32) * queries.astype(jnp.float32), axis=-1)
        return jnp.sum(
            jnp.where(chosen, values[:, None], jnp.float32(0.0)), axis=0
        ).reshape(all_ids.shape)

    def many_owned(_):
        all_scores = jnp.einsum(
            "td,rd->tr", all_queries, index_rows, preferred_element_type=jnp.float32
        )
        score_rows = jnp.take(all_scores.T, safe_ids.reshape(-1), axis=0).reshape(
            safe_ids.shape[0], safe_ids.shape[1], safe_ids.shape[0]
        )
        picked = jnp.einsum("tct->tc", score_rows)
        return jnp.where(is_owned, picked, jnp.float32(0.0))

    owner_terms = lax.cond(owned_count <= SPARSE_PAIRS, few_owned, many_owned, None)
    owner_terms = (
        owner_terms.reshape(req_count, text_count, tp_count, quarter)
        .transpose(0, 2, 1, 3)
        .reshape(device_count, text_count, quarter)
    )
    scores = jnp.sum(lax.all_to_all(owner_terms, ("req", "tp"), 0, 0, tiled=True), axis=0)
    return (hidden_out, scores)


def solution(mesh):
    placed = (
        P("req", "tp", None),
        P("req"),
        P(None, None, "tp"),
        P(None, "tp"),
        P("tp", None),
        P(),
        P(),
        P(),
        P(None, "tp"),
        P("tp"),
        P("tp", None),
        P(),
        P(),
        P(),
        P(("req", "tp"), None),
        P("req", "tp"),
    )
    return jax.shard_map(
        per_device,
        mesh=mesh,
        in_specs=placed,
        out_specs=(P("req", "tp", None), P("req", "tp")),
        check_vma=False,
    )
```

```python
import functools
import jax
import jax.numpy as jnp
from jax import lax
from jax.experimental import pallas as pl
from jax.experimental.pallas import tpu as pltpu
from jax.sharding import PartitionSpec as P

MESH_ID = pl.DeviceIdType.MESH


def _ring_peers():
    n = lax.axis_size("tp")
    me = lax.axis_index("tp")
    rq = lax.axis_index("req")
    core = rq % 2
    right = (me + 1) % n
    left = (me + n - 1) % n
    opp = (me + 2) % n
    relay_to = (me + 1 + 2 * core) % n
    relay_from = (me + n - 1 - 2 * core) % n
    barrier = pltpu.get_barrier_semaphore()
    for peer in (left, right):
        pl.semaphore_signal(barrier, inc=1, device_id=(rq, peer), device_id_type=MESH_ID)
    pl.semaphore_wait(barrier, 2)
    return me, rq, core, right, left, opp, relay_to, relay_from


def _gather_kernel(chunks, x_ref, out_ref, send_sem, recv_sem, local_sem):
    me, rq, core, right, left, opp, relay_to, relay_from = _ring_peers()
    rows = x_ref.shape[1]
    step = rows // chunks

    def part(ref, k):
        return ref.at[:, pl.ds(k * step, step), :]

    def slot(src, k):
        return out_ref.at[:, pl.ds(src * rows + k * step, step), :]

    def copy(src, dst, send, recv, peer):
        return pltpu.make_async_remote_copy(
            src, dst, send, recv, device_id=(rq, peer), device_id_type=MESH_ID
        )

    local = pltpu.make_async_copy(x_ref, out_ref.at[:, pl.ds(me * rows, rows), :], local_sem)
    local.start()
    sends = []
    for k in range(chunks):
        to_right = copy(part(x_ref, k), slot(me, k), send_sem.at[0, k], recv_sem.at[0, k], right)
        to_left = copy(part(x_ref, k), slot(me, k), send_sem.at[1, k], recv_sem.at[1, k], left)
        to_right.start()
        to_left.start()
        sends += [to_right, to_left]
    for k in range(chunks):
        copy(part(x_ref, k), slot(relay_from, k), send_sem.at[2, k], recv_sem.at[core, k], right).wait_recv()
        forward = copy(
            slot(relay_from, k), slot(relay_from, k), send_sem.at[2, k], recv_sem.at[2, k], relay_to
        )
        forward.start()
        sends.append(forward)
    other_side = (me + 1 + 2 * (1 - core)) % lax.axis_size("tp")
    for k in range(chunks):
        copy(part(x_ref, k), slot(other_side, k), send_sem.at[0, k], recv_sem.at[1 - core, k], right).wait_recv()
    for k in range(chunks):
        copy(part(x_ref, k), slot(opp, k), send_sem.at[0, k], recv_sem.at[2, k], right).wait_recv()
    for c in sends:
        c.wait_send()
    local.wait()


def ring_all_gather(x, collective_id, chunks=1):
    texts, rows, width = x.shape
    n = lax.axis_size("tp")
    return pl.pallas_call(
        functools.partial(_gather_kernel, chunks),
        out_shape=jax.ShapeDtypeStruct((texts, n * rows, width), x.dtype),
        in_specs=[pl.BlockSpec(memory_space=pl.ANY)],
        out_specs=pl.BlockSpec(memory_space=pl.ANY),
        scratch_shapes=[
            pltpu.SemaphoreType.DMA((3, chunks)),
            pltpu.SemaphoreType.DMA((3, chunks)),
            pltpu.SemaphoreType.DMA,
        ],
        compiler_params=pltpu.CompilerParams(collective_id=collective_id, has_side_effects=True),
    )(x)


def _scatter_add_kernel(chunks, p_ref, recv_ref, send_sem, recv_sem, relay_sem, local_sem,
                        own_buf, relay_buf, sum_buf):
    me, rq, core, right, left, opp, relay_to, relay_from = _ring_peers()
    rows = recv_ref.shape[2]
    step = rows // chunks

    def block(dst, k):
        return p_ref.at[:, pl.ds(dst * rows + k * step, step), :]

    def part(ref, k):
        return ref.at[:, pl.ds(k * step, step), :]

    def copy(src, dst, send, recv, peer):
        return pltpu.make_async_remote_copy(
            src, dst, send, recv, device_id=(rq, peer), device_id_type=MESH_ID
        )

    sends = []
    loads = []
    for k in range(chunks):
        to_relay = copy(block(opp, k), relay_buf.at[k], send_sem.at[0, k], relay_sem.at[k], relay_to)
        to_other = copy(
            block(relay_from, k), part(recv_ref.at[1], k), send_sem.at[1, k], recv_sem.at[1, k], relay_from
        )
        to_relay.start()
        to_other.start()
        load = pltpu.make_async_copy(block(relay_to, k), own_buf.at[k], local_sem.at[k])
        load.start()
        sends += [to_relay, to_other]
        loads.append(load)
    forwards = []
    for k in range(chunks):
        sends[2 * k].wait_recv()
        loads[k].wait()
        sum_buf[k] = (
            own_buf[k].astype(jnp.float32) + relay_buf[k].astype(jnp.float32)
        ).astype(sum_buf.dtype)
        forward = copy(sum_buf.at[k], part(recv_ref.at[0], k), send_sem.at[2, k], recv_sem.at[0, k], relay_to)
        forward.start()
        forwards.append(forward)
    for k in range(chunks):
        sends[2 * k + 1].wait_recv()
        forwards[k].wait_recv()
    for c in sends + forwards:
        c.wait_send()


def ring_reduce_scatter_add(p, collective_id, chunks=1):
    texts, all_rows, width = p.shape
    n = lax.axis_size("tp")
    rows = all_rows // n
    step = rows // chunks
    buf = pltpu.VMEM((chunks, texts, step, width), p.dtype)
    return pl.pallas_call(
        functools.partial(_scatter_add_kernel, chunks),
        out_shape=jax.ShapeDtypeStruct((2, texts, rows, width), p.dtype),
        in_specs=[pl.BlockSpec(memory_space=pl.ANY)],
        out_specs=pl.BlockSpec(memory_space=pl.ANY),
        scratch_shapes=[
            pltpu.SemaphoreType.DMA((3, chunks)),
            pltpu.SemaphoreType.DMA((2, chunks)),
            pltpu.SemaphoreType.DMA((chunks,)),
            pltpu.SemaphoreType.DMA((chunks,)),
            buf,
            buf,
            buf,
        ],
        compiler_params=pltpu.CompilerParams(collective_id=collective_id, has_side_effects=True),
    )(p)


def _peer_id(axes, peer):
    if axes == ("tp",):
        return (lax.axis_index("req"), peer)
    if axes == ("req",):
        return (peer, lax.axis_index("tp"))
    n_tp = lax.axis_size("tp")
    return (peer // n_tp, peer % n_tp)


def _direct_kernel(axes, scatter, x_ref, out_ref, send_sem, recv_sem):
    n = out_ref.shape[0]
    me = lax.axis_index(axes)
    barrier = pltpu.get_barrier_semaphore()

    def greet(d, carry):
        peer = (me + d) % n
        pl.semaphore_signal(barrier, inc=1, device_id=_peer_id(axes, peer), device_id_type=MESH_ID)
        return carry

    lax.fori_loop(1, n, greet, 0)
    pl.semaphore_wait(barrier, n - 1)

    def source(peer):
        return x_ref.at[peer] if scatter else x_ref

    def send(d, carry):
        peer = (me + d) % n
        pltpu.make_async_remote_copy(
            source(peer), out_ref.at[me], send_sem.at[d], recv_sem.at[me],
            device_id=_peer_id(axes, peer), device_id_type=MESH_ID,
        ).start()
        return carry

    lax.fori_loop(1, n, send, 0)

    def receive(d, carry):
        src = (me + n - d) % n
        pltpu.make_async_remote_copy(
            source(src), out_ref.at[src], send_sem.at[d], recv_sem.at[src],
            device_id=_peer_id(axes, src), device_id_type=MESH_ID,
        ).wait_recv()
        return carry

    lax.fori_loop(1, n, receive, 0)

    def sent(d, carry):
        peer = (me + d) % n
        pltpu.make_async_remote_copy(
            source(peer), out_ref.at[me], send_sem.at[d], recv_sem.at[me],
            device_id=_peer_id(axes, peer), device_id_type=MESH_ID,
        ).wait_send()
        return carry

    lax.fori_loop(1, n, sent, 0)


def direct_exchange(x, axes, collective_id, scatter=False, select=True):
    n = 1
    for name in axes:
        n *= lax.axis_size(name)
    block = x.shape[1:] if scatter else x.shape
    received = pl.pallas_call(
        functools.partial(_direct_kernel, axes, scatter),
        out_shape=jax.ShapeDtypeStruct((n,) + block, x.dtype),
        in_specs=[pl.BlockSpec(memory_space=pl.ANY)],
        out_specs=pl.BlockSpec(memory_space=pl.ANY),
        scratch_shapes=[
            pltpu.SemaphoreType.DMA((n,)),
            pltpu.SemaphoreType.DMA((n,)),
        ],
        compiler_params=pltpu.CompilerParams(collective_id=collective_id, has_side_effects=True),
    )(x)
    if not select:
        return received
    own = x[lax.axis_index(axes)] if scatter else x
    slot = jnp.arange(n, dtype=jnp.int32).reshape((n,) + (1,) * len(block))
    return jnp.where(slot == lax.axis_index(axes), own[None], received)


HEAD_DIM = 64
RING_CHUNKS = 2
SPARSE_PAIRS = 64
WINDOW = 512


layer_eps = 1e-05
norm_eps = 1e-06


def layer_norm(values, gain, shift):
    centre = values - jnp.mean(values, axis=-1, keepdims=True)
    spread = jnp.mean(centre * centre, axis=-1, keepdims=True)
    return centre * lax.rsqrt(spread + layer_eps) * gain + shift


def window_attention(queries_h, keys_h, values_h, lengths):
    seq_len = queries_h.shape[1]
    half_window = WINDOW // 2
    scale_factor = HEAD_DIM ** (-0.5)
    pos = jnp.arange(seq_len, dtype=jnp.int32)
    near = jnp.abs(pos[:, None] - pos[None, :]) <= half_window
    keep_mask = near[None] & (pos[None, None, :] < lengths[:, None, None])
    logits = (
        jnp.einsum("tqhe,tkhe->thqk", queries_h, keys_h, preferred_element_type=jnp.float32)
        * scale_factor
    )
    logits = jnp.where(keep_mask[:, None], logits, jnp.float32(-1e30))
    top_val = jnp.max(logits, axis=-1, keepdims=True)
    expo = jnp.exp(logits - top_val)
    attn_weights = (expo / jnp.sum(expo, axis=-1, keepdims=True)).astype(jnp.bfloat16)
    context = jnp.einsum(
        "thqk,tkhe->tqhe", attn_weights, values_h, preferred_element_type=jnp.float32
    )
    context = jnp.where(
        (pos[None, :] < lengths[:, None])[:, :, None, None], context, jnp.float32(0.0)
    )
    return context.astype(jnp.bfloat16).reshape(
        queries_h.shape[0], seq_len, queries_h.shape[2] * HEAD_DIM
    )


def per_device(
    states,
    lengths,
    w_qkv,
    b_qkv,
    w_out,
    b_out,
    ln1_gain,
    ln1_shift,
    w_up,
    b_up,
    w_down,
    b_down,
    ln2_gain,
    ln2_shift,
    index_rows,
    cand_ids,
):
    tp_count = lax.axis_size("tp")
    tp_rank = lax.axis_index("tp")
    req_count = lax.axis_size("req")
    req_rank = lax.axis_index("req")
    text_count, row_share, model_width = states.shape
    quarter = cand_ids.shape[1]
    full_states = ring_all_gather(states, 0, RING_CHUNKS)
    device_count = req_count * tp_count
    seq_len = full_states.shape[1]
    local_width = w_qkv.shape[2]
    heads_here = local_width // HEAD_DIM
    projected = (
        jnp.einsum("tsd,dce->tsce", full_states, w_qkv, preferred_element_type=jnp.float32) + b_qkv
    ).astype(jnp.bfloat16)
    queries_h = projected[:, :, 0].reshape(text_count, seq_len, heads_here, HEAD_DIM)
    keys_h = projected[:, :, 1].reshape(text_count, seq_len, heads_here, HEAD_DIM)
    values_h = projected[:, :, 2].reshape(text_count, seq_len, heads_here, HEAD_DIM)

    context = window_attention(queries_h, keys_h, values_h, lengths)
    partial_value = jnp.einsum("tsk,kd->tsd", context, w_out, preferred_element_type=jnp.float32)
    partial_value = partial_value.astype(jnp.bfloat16)
    attn_recv = ring_reduce_scatter_add(partial_value, 1, RING_CHUNKS)
    attn_sum = lax.dynamic_slice_in_dim(partial_value, tp_rank * row_share, row_share, 1).astype(
        jnp.float32
    ) + jnp.sum(attn_recv.astype(jnp.float32), axis=0)
    normed_local = layer_norm(
        states.astype(jnp.float32) + attn_sum + b_out, ln1_gain, ln1_shift
    ).astype(jnp.bfloat16)
    normed_full = ring_all_gather(normed_local, 2, RING_CHUNKS)
    up_act = jax.nn.gelu(
        jnp.einsum("tsd,df->tsf", normed_full, w_up, preferred_element_type=jnp.float32) + b_up,
        approximate=False,
    ).astype(jnp.bfloat16)
    up_act = lax.optimization_barrier(up_act)
    down_part = jnp.einsum(
        "tsf,fd->tsd", up_act, w_down, preferred_element_type=jnp.float32
    ).astype(jnp.bfloat16)
    down_recv = ring_reduce_scatter_add(down_part, 3, RING_CHUNKS)
    down_sum = lax.dynamic_slice_in_dim(down_part, tp_rank * row_share, row_share, 1).astype(
        jnp.float32
    ) + jnp.sum(down_recv.astype(jnp.float32), axis=0)
    hidden_out = layer_norm(
        normed_local.astype(jnp.float32) + down_sum + b_down, ln2_gain, ln2_shift
    ).astype(jnp.bfloat16)
    positions = tp_rank * row_share + jnp.arange(row_share, dtype=jnp.int32)
    is_valid = positions[None, :] < lengths[:, None]
    local_pool = jnp.sum(
        jnp.where(is_valid[:, :, None], hidden_out.astype(jnp.float32), jnp.float32(0.0)), axis=1
    )
    pool_and_ids = direct_exchange(
        jnp.concatenate([local_pool, cand_ids.astype(jnp.float32)], axis=1), ("tp",), 5, select=False
    )
    from_self = (jnp.arange(tp_count, dtype=jnp.int32) == tp_rank)[:, None, None]
    text_ids = jnp.swapaxes(
        jnp.where(from_self, cand_ids.astype(jnp.float32)[None], pool_and_ids[:, :, model_width:]), 0, 1
    )
    pooled = jnp.sum(
        jnp.where(from_self, local_pool[None], pool_and_ids[:, :, :model_width]), axis=0
    ) / lengths.astype(
        jnp.float32
    )[:, None]
    query_vec = (
        pooled * lax.rsqrt(jnp.mean(pooled * pooled, axis=-1, keepdims=True) + norm_eps)
    ).astype(jnp.bfloat16)
    bundle = jnp.concatenate(
        [query_vec.astype(jnp.float32), text_ids.reshape(text_count, -1)], axis=1
    )
    bundle = direct_exchange(bundle, ("req",), 6).reshape(req_count * text_count, bundle.shape[1])
    all_queries = bundle[:, :model_width].astype(jnp.bfloat16)
    all_ids = bundle[:, model_width:].astype(jnp.int32)
    rows_here = index_rows.shape[0]
    first_row = (req_rank * tp_count + tp_rank) * rows_here
    local_ids = all_ids - first_row
    is_owned = (local_ids >= 0) & (local_ids < rows_here)
    safe_ids = jnp.clip(local_ids, 0, rows_here - 1)
    owned_count = jnp.sum(is_owned.astype(jnp.int32))

    def few_owned(_):
        flat_owned = is_owned.reshape(-1)
        owned_int = is_owned.astype(jnp.int32)
        row_counts = jnp.cumsum(owned_int, axis=1)
        row_totals = row_counts[:, -1]
        running = (row_counts + (jnp.cumsum(row_totals) - row_totals)[:, None]).reshape(-1)
        rank = jnp.arange(SPARSE_PAIRS, dtype=jnp.int32)
        chosen = flat_owned[None, :] & (running[None, :] == rank[:, None] + 1)
        pair_index = jnp.arange(flat_owned.shape[0], dtype=jnp.int32)
        pair_at = jnp.sum(jnp.where(chosen, pair_index[None, :], 0), axis=1)
        row_of = jnp.sum(jnp.where(chosen, safe_ids.reshape(-1)[None, :], 0), axis=1)
        row_pick = jnp.arange(rows_here, dtype=jnp.int32)[None, :] == row_of[:, None]
        rows = jnp.dot(row_pick.astype(index_rows.dtype), index_rows, preferred_element_type=jnp.float32)
        text_of = pair_at // all_ids.shape[1]
        text_pick = jnp.arange(all_queries.shape[0], dtype=jnp.int32)[None, :] == text_of[:, None]
        queries = jnp.dot(
            text_pick.astype(all_queries.dtype), all_queries, preferred_element_type=jnp.float32
        )
        values = jnp.sum(rows.astype(jnp.float32) * queries.astype(jnp.float32), axis=-1)
        return jnp.sum(
            jnp.where(chosen, values[:, None], jnp.float32(0.0)), axis=0
        ).reshape(all_ids.shape)

    def many_owned(_):
        all_scores = jnp.einsum(
            "td,rd->tr", all_queries, index_rows, preferred_element_type=jnp.float32
        )
        score_rows = jnp.take(all_scores.T, safe_ids.reshape(-1), axis=0).reshape(
            safe_ids.shape[0], safe_ids.shape[1], safe_ids.shape[0]
        )
        picked = jnp.einsum("tct->tc", score_rows)
        return jnp.where(is_owned, picked, jnp.float32(0.0))

    owner_terms = lax.cond(owned_count <= SPARSE_PAIRS, few_owned, many_owned, None)
    owner_terms = (
        owner_terms.reshape(req_count, text_count, tp_count, quarter)
        .transpose(0, 2, 1, 3)
        .reshape(device_count, text_count, quarter)
    )
    scores = jnp.sum(lax.all_to_all(owner_terms, ("req", "tp"), 0, 0, tiled=True), axis=0)
    return (hidden_out, scores)


def solution(mesh):
    placed = (
        P("req", "tp", None),
        P("req"),
        P(None, None, "tp"),
        P(None, "tp"),
        P("tp", None),
        P(),
        P(),
        P(),
        P(None, "tp"),
        P("tp"),
        P("tp", None),
        P(),
        P(),
        P(),
        P(("req", "tp"), None),
        P("req", "tp"),
    )
    return jax.shard_map(
        per_device,
        mesh=mesh,
        in_specs=placed,
        out_specs=(P("req", "tp", None), P("req", "tp")),
        check_vma=False,
    )
```

```python
import functools
import jax
import jax.numpy as jnp
from jax import lax
from jax.experimental import pallas as pl
from jax.experimental.pallas import tpu as pltpu
from jax.sharding import PartitionSpec as P

MESH_ID = pl.DeviceIdType.MESH


def _ring_peers():
    n = lax.axis_size("tp")
    me = lax.axis_index("tp")
    rq = lax.axis_index("req")
    core = rq % 2
    right = (me + 1) % n
    left = (me + n - 1) % n
    opp = (me + 2) % n
    relay_to = (me + 1 + 2 * core) % n
    relay_from = (me + n - 1 - 2 * core) % n
    barrier = pltpu.get_barrier_semaphore()
    for peer in (left, right):
        pl.semaphore_signal(barrier, inc=1, device_id=(rq, peer), device_id_type=MESH_ID)
    pl.semaphore_wait(barrier, 2)
    return me, rq, core, right, left, opp, relay_to, relay_from


def _gather_kernel(chunks, x_ref, out_ref, send_sem, recv_sem, local_sem):
    me, rq, core, right, left, opp, relay_to, relay_from = _ring_peers()
    rows = x_ref.shape[1]
    step = rows // chunks

    def part(ref, k):
        return ref.at[:, pl.ds(k * step, step), :]

    def slot(src, k):
        return out_ref.at[:, pl.ds(src * rows + k * step, step), :]

    def copy(src, dst, send, recv, peer):
        return pltpu.make_async_remote_copy(
            src, dst, send, recv, device_id=(rq, peer), device_id_type=MESH_ID
        )

    local = pltpu.make_async_copy(x_ref, out_ref.at[:, pl.ds(me * rows, rows), :], local_sem)
    local.start()
    sends = []
    for k in range(chunks):
        to_right = copy(part(x_ref, k), slot(me, k), send_sem.at[0, k], recv_sem.at[0, k], right)
        to_left = copy(part(x_ref, k), slot(me, k), send_sem.at[1, k], recv_sem.at[1, k], left)
        to_right.start()
        to_left.start()
        sends += [to_right, to_left]
    for k in range(chunks):
        copy(part(x_ref, k), slot(relay_from, k), send_sem.at[2, k], recv_sem.at[core, k], right).wait_recv()
        forward = copy(
            slot(relay_from, k), slot(relay_from, k), send_sem.at[2, k], recv_sem.at[2, k], relay_to
        )
        forward.start()
        sends.append(forward)
    other_side = (me + 1 + 2 * (1 - core)) % lax.axis_size("tp")
    for k in range(chunks):
        copy(part(x_ref, k), slot(other_side, k), send_sem.at[0, k], recv_sem.at[1 - core, k], right).wait_recv()
    for k in range(chunks):
        copy(part(x_ref, k), slot(opp, k), send_sem.at[0, k], recv_sem.at[2, k], right).wait_recv()
    for c in sends:
        c.wait_send()
    local.wait()


def ring_all_gather(x, collective_id, chunks=1):
    texts, rows, width = x.shape
    n = lax.axis_size("tp")
    return pl.pallas_call(
        functools.partial(_gather_kernel, chunks),
        out_shape=jax.ShapeDtypeStruct((texts, n * rows, width), x.dtype),
        in_specs=[pl.BlockSpec(memory_space=pl.ANY)],
        out_specs=pl.BlockSpec(memory_space=pl.ANY),
        scratch_shapes=[
            pltpu.SemaphoreType.DMA((3, chunks)),
            pltpu.SemaphoreType.DMA((3, chunks)),
            pltpu.SemaphoreType.DMA,
        ],
        compiler_params=pltpu.CompilerParams(collective_id=collective_id, has_side_effects=True),
    )(x)


def _scatter_add_kernel(chunks, p_ref, recv_ref, send_sem, recv_sem, relay_sem, local_sem,
                        own_buf, relay_buf, sum_buf):
    me, rq, core, right, left, opp, relay_to, relay_from = _ring_peers()
    rows = recv_ref.shape[2]
    step = rows // chunks

    def block(dst, k):
        return p_ref.at[:, pl.ds(dst * rows + k * step, step), :]

    def part(ref, k):
        return ref.at[:, pl.ds(k * step, step), :]

    def copy(src, dst, send, recv, peer):
        return pltpu.make_async_remote_copy(
            src, dst, send, recv, device_id=(rq, peer), device_id_type=MESH_ID
        )

    sends = []
    loads = []
    for k in range(chunks):
        to_relay = copy(block(opp, k), relay_buf.at[k], send_sem.at[0, k], relay_sem.at[k], relay_to)
        to_other = copy(
            block(relay_from, k), part(recv_ref.at[1], k), send_sem.at[1, k], recv_sem.at[1, k], relay_from
        )
        to_relay.start()
        to_other.start()
        load = pltpu.make_async_copy(block(relay_to, k), own_buf.at[k], local_sem.at[k])
        load.start()
        sends += [to_relay, to_other]
        loads.append(load)
    forwards = []
    for k in range(chunks):
        sends[2 * k].wait_recv()
        loads[k].wait()
        sum_buf[k] = (
            own_buf[k].astype(jnp.float32) + relay_buf[k].astype(jnp.float32)
        ).astype(sum_buf.dtype)
        forward = copy(sum_buf.at[k], part(recv_ref.at[0], k), send_sem.at[2, k], recv_sem.at[0, k], relay_to)
        forward.start()
        forwards.append(forward)
    for k in range(chunks):
        sends[2 * k + 1].wait_recv()
        forwards[k].wait_recv()
    for c in sends + forwards:
        c.wait_send()


def ring_reduce_scatter_add(p, collective_id, chunks=1):
    texts, all_rows, width = p.shape
    n = lax.axis_size("tp")
    rows = all_rows // n
    step = rows // chunks
    buf = pltpu.VMEM((chunks, texts, step, width), p.dtype)
    return pl.pallas_call(
        functools.partial(_scatter_add_kernel, chunks),
        out_shape=jax.ShapeDtypeStruct((2, texts, rows, width), p.dtype),
        in_specs=[pl.BlockSpec(memory_space=pl.ANY)],
        out_specs=pl.BlockSpec(memory_space=pl.ANY),
        scratch_shapes=[
            pltpu.SemaphoreType.DMA((3, chunks)),
            pltpu.SemaphoreType.DMA((2, chunks)),
            pltpu.SemaphoreType.DMA((chunks,)),
            pltpu.SemaphoreType.DMA((chunks,)),
            buf,
            buf,
            buf,
        ],
        compiler_params=pltpu.CompilerParams(collective_id=collective_id, has_side_effects=True),
    )(p)


def _peer_id(axes, peer):
    if axes == ("tp",):
        return (lax.axis_index("req"), peer)
    if axes == ("req",):
        return (peer, lax.axis_index("tp"))
    n_tp = lax.axis_size("tp")
    return (peer // n_tp, peer % n_tp)


def _direct_kernel(axes, scatter, x_ref, out_ref, send_sem, recv_sem):
    n = out_ref.shape[0]
    me = lax.axis_index(axes)
    barrier = pltpu.get_barrier_semaphore()

    def greet(d, carry):
        peer = (me + d) % n
        pl.semaphore_signal(barrier, inc=1, device_id=_peer_id(axes, peer), device_id_type=MESH_ID)
        return carry

    lax.fori_loop(1, n, greet, 0)
    pl.semaphore_wait(barrier, n - 1)

    def source(peer):
        return x_ref.at[peer] if scatter else x_ref

    def send(d, carry):
        peer = (me + d) % n
        pltpu.make_async_remote_copy(
            source(peer), out_ref.at[me], send_sem.at[d], recv_sem.at[me],
            device_id=_peer_id(axes, peer), device_id_type=MESH_ID,
        ).start()
        return carry

    lax.fori_loop(1, n, send, 0)

    def receive(d, carry):
        src = (me + n - d) % n
        pltpu.make_async_remote_copy(
            source(src), out_ref.at[src], send_sem.at[d], recv_sem.at[src],
            device_id=_peer_id(axes, src), device_id_type=MESH_ID,
        ).wait_recv()
        return carry

    lax.fori_loop(1, n, receive, 0)

    def sent(d, carry):
        peer = (me + d) % n
        pltpu.make_async_remote_copy(
            source(peer), out_ref.at[me], send_sem.at[d], recv_sem.at[me],
            device_id=_peer_id(axes, peer), device_id_type=MESH_ID,
        ).wait_send()
        return carry

    lax.fori_loop(1, n, sent, 0)


def direct_exchange(x, axes, collective_id, scatter=False):
    n = 1
    for name in axes:
        n *= lax.axis_size(name)
    block = x.shape[1:] if scatter else x.shape
    received = pl.pallas_call(
        functools.partial(_direct_kernel, axes, scatter),
        out_shape=jax.ShapeDtypeStruct((n,) + block, x.dtype),
        in_specs=[pl.BlockSpec(memory_space=pl.ANY)],
        out_specs=pl.BlockSpec(memory_space=pl.ANY),
        scratch_shapes=[
            pltpu.SemaphoreType.DMA((n,)),
            pltpu.SemaphoreType.DMA((n,)),
        ],
        compiler_params=pltpu.CompilerParams(collective_id=collective_id, has_side_effects=True),
    )(x)
    own = x[lax.axis_index(axes)] if scatter else x
    slot = jnp.arange(n, dtype=jnp.int32).reshape((n,) + (1,) * len(block))
    return jnp.where(slot == lax.axis_index(axes), own[None], received)


HEAD_DIM = 64
RING_CHUNKS = 4
SPARSE_PAIRS = 64
WINDOW = 512


layer_eps = 1e-05
norm_eps = 1e-06


def layer_norm(values, gain, shift):
    centre = values - jnp.mean(values, axis=-1, keepdims=True)
    spread = jnp.mean(centre * centre, axis=-1, keepdims=True)
    return centre * lax.rsqrt(spread + layer_eps) * gain + shift


def window_attention(queries_h, keys_h, values_h, lengths):
    seq_len = queries_h.shape[1]
    half_window = WINDOW // 2
    scale_factor = HEAD_DIM ** (-0.5)
    pos = jnp.arange(seq_len, dtype=jnp.int32)
    near = jnp.abs(pos[:, None] - pos[None, :]) <= half_window
    keep_mask = near[None] & (pos[None, None, :] < lengths[:, None, None])
    logits = (
        jnp.einsum("tqhe,tkhe->thqk", queries_h, keys_h, preferred_element_type=jnp.float32)
        * scale_factor
    )
    logits = jnp.where(keep_mask[:, None], logits, jnp.float32(-1e30))
    top_val = jnp.max(logits, axis=-1, keepdims=True)
    expo = jnp.exp(logits - top_val)
    attn_weights = (expo / jnp.sum(expo, axis=-1, keepdims=True)).astype(jnp.bfloat16)
    context = jnp.einsum(
        "thqk,tkhe->tqhe", attn_weights, values_h, preferred_element_type=jnp.float32
    )
    context = jnp.where(
        (pos[None, :] < lengths[:, None])[:, :, None, None], context, jnp.float32(0.0)
    )
    return context.astype(jnp.bfloat16).reshape(
        queries_h.shape[0], seq_len, queries_h.shape[2] * HEAD_DIM
    )


def per_device(
    states,
    lengths,
    w_qkv,
    b_qkv,
    w_out,
    b_out,
    ln1_gain,
    ln1_shift,
    w_up,
    b_up,
    w_down,
    b_down,
    ln2_gain,
    ln2_shift,
    index_rows,
    cand_ids,
):
    tp_count = lax.axis_size("tp")
    tp_rank = lax.axis_index("tp")
    req_count = lax.axis_size("req")
    req_rank = lax.axis_index("req")
    text_count, row_share, model_width = states.shape
    quarter = cand_ids.shape[1]
    full_states = ring_all_gather(states, 0, RING_CHUNKS)
    device_count = req_count * tp_count
    seq_len = full_states.shape[1]
    local_width = w_qkv.shape[2]
    heads_here = local_width // HEAD_DIM
    projected = (
        jnp.einsum("tsd,dce->tsce", full_states, w_qkv, preferred_element_type=jnp.float32) + b_qkv
    ).astype(jnp.bfloat16)
    queries_h = projected[:, :, 0].reshape(text_count, seq_len, heads_here, HEAD_DIM)
    keys_h = projected[:, :, 1].reshape(text_count, seq_len, heads_here, HEAD_DIM)
    values_h = projected[:, :, 2].reshape(text_count, seq_len, heads_here, HEAD_DIM)

    context = window_attention(queries_h, keys_h, values_h, lengths)
    partial_value = jnp.einsum("tsk,kd->tsd", context, w_out, preferred_element_type=jnp.float32)
    partial_value = partial_value.astype(jnp.bfloat16)
    attn_recv = ring_reduce_scatter_add(partial_value, 1, RING_CHUNKS)
    attn_sum = lax.dynamic_slice_in_dim(partial_value, tp_rank * row_share, row_share, 1).astype(
        jnp.float32
    ) + jnp.sum(attn_recv.astype(jnp.float32), axis=0)
    normed_local = layer_norm(
        states.astype(jnp.float32) + attn_sum + b_out, ln1_gain, ln1_shift
    ).astype(jnp.bfloat16)
    normed_full = ring_all_gather(normed_local, 2, RING_CHUNKS)
    up_act = jax.nn.gelu(
        jnp.einsum("tsd,df->tsf", normed_full, w_up, preferred_element_type=jnp.float32) + b_up,
        approximate=False,
    ).astype(jnp.bfloat16)
    up_act = lax.optimization_barrier(up_act)
    down_part = jnp.einsum(
        "tsf,fd->tsd", up_act, w_down, preferred_element_type=jnp.float32
    ).astype(jnp.bfloat16)
    down_recv = ring_reduce_scatter_add(down_part, 3, RING_CHUNKS)
    down_sum = lax.dynamic_slice_in_dim(down_part, tp_rank * row_share, row_share, 1).astype(
        jnp.float32
    ) + jnp.sum(down_recv.astype(jnp.float32), axis=0)
    hidden_out = layer_norm(
        normed_local.astype(jnp.float32) + down_sum + b_down, ln2_gain, ln2_shift
    ).astype(jnp.bfloat16)
    positions = tp_rank * row_share + jnp.arange(row_share, dtype=jnp.int32)
    is_valid = positions[None, :] < lengths[:, None]
    local_pool = jnp.sum(
        jnp.where(is_valid[:, :, None], hidden_out.astype(jnp.float32), jnp.float32(0.0)), axis=1
    )
    pool_and_ids = direct_exchange(
        jnp.concatenate([local_pool, cand_ids.astype(jnp.float32)], axis=1), ("tp",), 5
    )
    text_ids = jnp.swapaxes(pool_and_ids[:, :, model_width:], 0, 1)
    pooled = jnp.sum(pool_and_ids[:, :, :model_width], axis=0) / lengths.astype(
        jnp.float32
    )[:, None]
    query_vec = (
        pooled * lax.rsqrt(jnp.mean(pooled * pooled, axis=-1, keepdims=True) + norm_eps)
    ).astype(jnp.bfloat16)
    bundle = jnp.concatenate(
        [query_vec.astype(jnp.float32), text_ids.reshape(text_count, -1)], axis=1
    )
    bundle = direct_exchange(bundle, ("req",), 6).reshape(req_count * text_count, bundle.shape[1])
    all_queries = bundle[:, :model_width].astype(jnp.bfloat16)
    all_ids = bundle[:, model_width:].astype(jnp.int32)
    rows_here = index_rows.shape[0]
    first_row = (req_rank * tp_count + tp_rank) * rows_here
    local_ids = all_ids - first_row
    is_owned = (local_ids >= 0) & (local_ids < rows_here)
    safe_ids = jnp.clip(local_ids, 0, rows_here - 1)
    owned_count = jnp.sum(is_owned.astype(jnp.int32))

    def few_owned(_):
        flat_owned = is_owned.reshape(-1)
        owned_int = is_owned.astype(jnp.int32)
        row_counts = jnp.cumsum(owned_int, axis=1)
        row_totals = row_counts[:, -1]
        running = (row_counts + (jnp.cumsum(row_totals) - row_totals)[:, None]).reshape(-1)
        rank = jnp.arange(SPARSE_PAIRS, dtype=jnp.int32)
        chosen = flat_owned[None, :] & (running[None, :] == rank[:, None] + 1)
        pair_index = jnp.arange(flat_owned.shape[0], dtype=jnp.int32)
        pair_at = jnp.sum(jnp.where(chosen, pair_index[None, :], 0), axis=1)
        row_of = jnp.sum(jnp.where(chosen, safe_ids.reshape(-1)[None, :], 0), axis=1)
        row_pick = jnp.arange(rows_here, dtype=jnp.int32)[None, :] == row_of[:, None]
        rows = jnp.dot(row_pick.astype(index_rows.dtype), index_rows, preferred_element_type=jnp.float32)
        text_of = pair_at // all_ids.shape[1]
        text_pick = jnp.arange(all_queries.shape[0], dtype=jnp.int32)[None, :] == text_of[:, None]
        queries = jnp.dot(
            text_pick.astype(all_queries.dtype), all_queries, preferred_element_type=jnp.float32
        )
        values = jnp.sum(rows.astype(jnp.float32) * queries.astype(jnp.float32), axis=-1)
        return jnp.sum(
            jnp.where(chosen, values[:, None], jnp.float32(0.0)), axis=0
        ).reshape(all_ids.shape)

    def many_owned(_):
        all_scores = jnp.einsum(
            "td,rd->tr", all_queries, index_rows, preferred_element_type=jnp.float32
        )
        score_rows = jnp.take(all_scores.T, safe_ids.reshape(-1), axis=0).reshape(
            safe_ids.shape[0], safe_ids.shape[1], safe_ids.shape[0]
        )
        picked = jnp.einsum("tct->tc", score_rows)
        return jnp.where(is_owned, picked, jnp.float32(0.0))

    owner_terms = lax.cond(owned_count <= SPARSE_PAIRS, few_owned, many_owned, None)
    owner_terms = (
        owner_terms.reshape(req_count, text_count, tp_count, quarter)
        .transpose(0, 2, 1, 3)
        .reshape(device_count, text_count, quarter)
    )
    scores = jnp.sum(lax.all_to_all(owner_terms, ("req", "tp"), 0, 0, tiled=True), axis=0)
    return (hidden_out, scores)


def solution(mesh):
    placed = (
        P("req", "tp", None),
        P("req"),
        P(None, None, "tp"),
        P(None, "tp"),
        P("tp", None),
        P(),
        P(),
        P(),
        P(None, "tp"),
        P("tp"),
        P("tp", None),
        P(),
        P(),
        P(),
        P(("req", "tp"), None),
        P("req", "tp"),
    )
    return jax.shard_map(
        per_device,
        mesh=mesh,
        in_specs=placed,
        out_specs=(P("req", "tp", None), P("req", "tp")),
        check_vma=False,
    )
```
